32 devices in a mesh: lat: 4 (over y, core), lon: 8 (over z, x).
Axes of the slice: x: 2, y: 2, z: 4, core: 2. Of those that a mesh axis runs over, the one named last changes fastest.
Arguments:
- noisy: float32 [8, 512, 3072], P(None, 'lat', 'lon'), may hold values from -6 to 6
- coarse: float32 [8, 512, 3072], P(None, 'lat', 'lon'), may hold values from -6 to 6
- step_noise: float32 [8, 512, 3072], P(None, 'lat', 'lon'), may hold values from -6 to 6
- timestep: int32 [1], replicated, may hold values from 985 to 999
- w_time: float32 [128, 1408], replicated, may hold values from -0.5 to 0.5
- w_embed: bfloat16 [64, 64], replicated, may hold values from -0.75 to 0.75
- w_enc1: bfloat16 [576, 64], replicated, may hold values from -0.25 to 0.25
- w_down1: bfloat16 [256, 128], replicated, may hold values from -0.375 to 0.375
- w_enc2: bfloat16 [1152, 128], replicated, may hold values from -0.1875 to 0.1875
- w_down2: bfloat16 [512, 256], replicated, may hold values from -0.25 to 0.25
- w_enc3: bfloat16 [2304, 256], replicated, may hold values from -0.125 to 0.125
- w_down3: bfloat16 [1024, 512], replicated, may hold values from -0.1875 to 0.1875
- w_qkv: bfloat16 [512, 1536], replicated, may hold values from -3 to 3
- w_attn_out: bfloat16 [512, 512], replicated, may hold values from -0.25 to 0.25
- w_up3: bfloat16 [512, 1024], replicated, may hold values from -0.25 to 0.25
- w_dec3: bfloat16 [2304, 256], replicated, may hold values from -0.375 to 0.375
- w_up2: bfloat16 [256, 512], replicated, may hold values from -0.375 to 0.375
- w_dec2: bfloat16 [1152, 128], replicated, may hold values from -0.5 to 0.5
- w_up1: bfloat16 [128, 256], replicated, may hold values from -0.5 to 0.5
- w_dec1: bfloat16 [576, 64], replicated, may hold values from -0.75 to 0.75
- w_head: bfloat16 [64, 32], replicated, may hold values from -0.75 to 0.75
Outputs:
- denoised: float32 [8, 512, 3072], P(None, 'lat', 'lon')
The draws below stay inside these ranges and needn't reach their ends.
All inputs are finite; a program needn't handle non-finite values.
Results may differ from the reference program's by a relative error of at most 0.025.
Values may be sent and summed in bfloat16 or wider, within the bound.
No kernel may reach another device: no remote copies, remote signals or barrier semaphores. Data moves between devices by JAX's collectives and lax.ppermute only.
A program may use at most 128 MiB of HBM per device.

```python
import math
import jax
import jax.numpy as jnp
from jax import lax

VARS = 8
C1 = 64
C2 = 128
C3 = 256
C4 = 512
HEAD_DIM = 64
TFREQ = 128
T_STEPS = 1000
NLAT = 512
NLON = 3072
TEMB = 1408


def draw_w_qkv(key, part):
    base_key = jax.random.fold_in(jax.random.fold_in(key, 7331), 0)
    attention_weights = jax.random.truncated_normal(base_key, -4.0, 4.0, (C4, 3 * C4), jnp.float32) * (2.0 * C4 ** (-0.5))
    return attention_weights.astype(jnp.bfloat16)


def level_of(rng, dims, pieces, smallest, largest):
    def one(axis_at, shards_of):
        heights = jax.random.uniform(jax.random.fold_in(jax.random.fold_in(rng, 6), axis_at), (shards_of,), jnp.float32, smallest / len(pieces), largest / len(pieces))
        return jnp.repeat(jnp.exp(heights), dims[axis_at] // shards_of).reshape((-1,) + (1,) * (len(dims) - axis_at - 1))

    loudness = one(*pieces[0])
    for cut in pieces[1:]:
        loudness = loudness * one(*cut)
    return loudness


def gaussian(rng, dims, scale, most, shards=(), held_as=jnp.bfloat16):
    array = jax.random.normal(rng, dims, jnp.float32) * scale
    if len(shards) > 0:
        array = level_of(rng, dims, shards, -0.22, 0.18) * array
    return jnp.clip(array, min=-most, max=most).astype(held_as)


def setup_inputs(seed: int = 0) -> dict:
    arg_keys = jax.random.split(jax.random.key(seed), 22)
    return {
        "noisy": gaussian(arg_keys[0], (VARS, NLAT, NLON), 1.0, 6.0, ((1, 4), (2, 8)), jnp.float32),
        "coarse": gaussian(arg_keys[1], (VARS, NLAT, NLON), 1.0, 6.0, ((1, 4), (2, 8)), jnp.float32),
        "step_noise": gaussian(arg_keys[2], (VARS, NLAT, NLON), 1.0, 6.0, ((1, 4), (2, 8)), jnp.float32),
        "timestep": jax.random.randint(arg_keys[3], (1,), 985, 1000).astype(jnp.int32),
        "w_time": gaussian(arg_keys[4], (TFREQ, TEMB), TFREQ ** -0.5, 0.5, (), jnp.float32),
        "w_embed": gaussian(arg_keys[5], (8 * VARS, C1), (8 * VARS) ** -0.5, 0.75),
        "w_enc1": gaussian(arg_keys[6], (9 * C1, C1), (9 * C1) ** -0.5, 0.25),
        "w_down1": gaussian(arg_keys[7], (4 * C1, C2), (4 * C1) ** -0.5, 0.375),
        "w_enc2": gaussian(arg_keys[8], (9 * C2, C2), (9 * C2) ** -0.5, 0.1875),
        "w_down2": gaussian(arg_keys[9], (4 * C2, C3), (4 * C2) ** -0.5, 0.25),
        "w_enc3": gaussian(arg_keys[10], (9 * C3, C3), (9 * C3) ** -0.5, 0.125),
        "w_down3": gaussian(arg_keys[11], (4 * C3, C4), (4 * C3) ** -0.5, 0.1875),
        "w_qkv": draw_w_qkv(jax.random.fold_in(arg_keys[21], 71), 0),
        "w_attn_out": gaussian(arg_keys[13], (C4, C4), C4 ** -0.5, 0.25),
        "w_up3": gaussian(arg_keys[14], (C4, 4 * C3), C4 ** -0.5, 0.25),
        "w_dec3": gaussian(arg_keys[15], (9 * C3, C3), C3 ** -0.5, 0.375),
        "w_up2": gaussian(arg_keys[16], (C3, 4 * C2), C3 ** -0.5, 0.375),
        "w_dec2": gaussian(arg_keys[17], (9 * C2, C2), C2 ** -0.5, 0.5),
        "w_up1": gaussian(arg_keys[18], (C2, 4 * C1), C2 ** -0.5, 0.5),
        "w_dec1": gaussian(arg_keys[19], (9 * C1, C1), C1 ** -0.5, 0.75),
        "w_head": gaussian(arg_keys[20], (C1, 4 * VARS), C1 ** -0.5, 0.75),
    }


def plan(step):
    frac = (step.astype(jnp.float32) / T_STEPS + 0.008) / 1.008
    return jnp.cos(frac * (math.pi / 2)) ** 2

def time_embed(timestep, w_time):
    half = w_time.shape[0] // 2
    freqs = jnp.exp(-math.log(10000.0) * jnp.arange(half, dtype=jnp.float32) / half)
    angle = timestep.astype(jnp.float32)[0] * freqs
    feats = jnp.concatenate([jnp.sin(angle), jnp.cos(angle)])[None]
    return jax.nn.silu(jnp.dot(feats, w_time, precision=lax.Precision.HIGHEST))[0]

def normed(h, bias):
    hf = h.astype(jnp.float32)
    return hf * lax.rsqrt(lax.optimization_barrier(jnp.mean(hf * hf, axis=-1, keepdims=True)) + 1e-06) + bias

def pad_rims(u):
    rows = jnp.pad(u, ((1, 1), (0, 0), (0, 0)))
    return jnp.concatenate([rows[:, -1:], rows, rows[:, :1]], axis=1)

def block(h, weight, bias, padder):
    rows, cols = (h.shape[0], h.shape[1])
    u = jax.nn.silu(normed(h, bias)).astype(jnp.bfloat16)
    padded = padder(u)
    taps = jnp.concatenate([padded[i:i + rows, j:j + cols] for i in range(3) for j in range(3)], axis=-1)
    conv = jnp.dot(taps, weight, preferred_element_type=jnp.float32)
    return (h.astype(jnp.float32) + conv).astype(jnp.bfloat16)

def down(h, weight):
    rows, cols, chans = h.shape
    merged = h.reshape(rows // 2, 2, cols // 2, 2, chans).transpose(0, 2, 1, 3, 4).reshape(rows // 2, cols // 2, 4 * chans)
    return jnp.dot(merged, weight, preferred_element_type=jnp.float32).astype(jnp.bfloat16)

def upsample(h, weight, skip):
    rows, cols = (h.shape[0], h.shape[1])
    spread = jnp.dot(h, weight, preferred_element_type=jnp.float32)
    chans = spread.shape[-1] // 4
    spread = spread.reshape(rows, cols, 2, 2, chans).transpose(0, 2, 1, 3, 4).reshape(2 * rows, 2 * cols, chans)
    return (spread + skip.astype(jnp.float32)).astype(jnp.bfloat16)

def embed(noisy, coarse, weight):
    stacked = jnp.concatenate([noisy, coarse], axis=0)
    chans, rows, cols = stacked.shape
    patches = stacked.reshape(chans, rows // 2, 2, cols // 2, 2).transpose(1, 3, 0, 2, 4)
    patches = patches.reshape(rows // 2, cols // 2, 4 * chans).astype(jnp.bfloat16)
    return jnp.dot(patches, weight, preferred_element_type=jnp.float32).astype(jnp.bfloat16)

def unpatch(h, weight, nvars):
    rows, cols = (h.shape[0], h.shape[1])
    out = jnp.dot(h, weight, preferred_element_type=jnp.float32)
    return out.reshape(rows, cols, nvars, 2, 2).transpose(2, 0, 3, 1, 4).reshape(nvars, 2 * rows, 2 * cols)

def attend(query_rows, key_rows, value_rows):
    score_scale = query_rows.shape[-1] ** (-0.5)
    attention_scores = jnp.einsum('eon,ecn->eoc', query_rows.astype(jnp.float32), key_rows.astype(jnp.float32)) * score_scale
    attention_weights = jax.nn.softmax(attention_scores, axis=-1).astype(jnp.bfloat16)
    return jnp.einsum('imv,ivf->imf', attention_weights.astype(jnp.float32), value_rows.astype(jnp.float32)).astype(jnp.bfloat16)

def split_heads(qkv, width):
    rows, cols = (qkv.shape[0], qkv.shape[1])
    parts = []
    for index in range(3):
        piece = qkv[:, :, index * width:(index + 1) * width]
        parts.append(piece.reshape(rows, cols, width // HEAD_DIM, HEAD_DIM).transpose(0, 2, 1, 3))
    return parts

def attention_block(h, bias, w_qkv, w_attn_out, mixer):
    rows, cols, width = h.shape
    u = normed(h, bias).astype(jnp.bfloat16)
    qkv = jnp.dot(u, w_qkv, preferred_element_type=jnp.float32).astype(jnp.bfloat16)
    query_rows, key_rows, value_rows = split_heads(qkv, width)
    mixed = mixer(query_rows, key_rows, value_rows)
    mixed = mixed.transpose(0, 2, 1, 3).reshape(rows, cols, width)
    out = jnp.dot(mixed, w_attn_out, preferred_element_type=jnp.float32)
    return (h.astype(jnp.float32) + out).astype(jnp.bfloat16)

def whole_rows(query_rows, key_rows, value_rows):
    return lax.map(lambda item: attend(item[0], item[1], item[2]), (query_rows, key_rows, value_rows))

def final_update(noisy, eps, step_noise, timestep):
    current_alpha_product = plan(timestep[0])
    abar_prev = plan(timestep[0] - 1)
    beta = jnp.minimum(1.0 - current_alpha_product / abar_prev, 0.999)
    mean = (noisy - beta / jnp.sqrt(1.0 - current_alpha_product) * eps) / jnp.sqrt(1.0 - beta)
    sigma = jnp.sqrt(beta * (1.0 - abar_prev) / (1.0 - current_alpha_product))
    return mean + sigma * step_noise

def network(noisy, coarse, step_noise, timestep, w_time, w_embed, w_enc1, w_down1, w_enc2, w_down2, w_enc3, w_down3, w_qkv, w_attn_out, w_up3, w_dec3, w_up2, w_dec2, w_up1, w_dec1, w_head, padder, mixer):
    temb = time_embed(timestep, w_time)
    c1, c2, c3, c4 = (w_enc1.shape[1], w_enc2.shape[1], w_enc3.shape[1], w_qkv.shape[0])
    bounds = [0, c1, c1 + c2, c1 + c2 + c3, c1 + c2 + c3 + c4, c1 + c2 + 2 * c3 + c4, c1 + 2 * c2 + 2 * c3 + c4, 2 * c1 + 2 * c2 + 2 * c3 + c4]
    biases = [temb[bounds[i]:bounds[i + 1]] for i in range(7)]
    e0 = embed(noisy, coarse, w_embed)
    e1 = block(e0, w_enc1, biases[0], padder)
    e2 = block(down(e1, w_down1), w_enc2, biases[1], padder)
    e3 = block(down(e2, w_down2), w_enc3, biases[2], padder)
    a4 = attention_block(down(e3, w_down3), biases[3], w_qkv, w_attn_out, mixer)
    g3 = block(upsample(a4, w_up3, e3), w_dec3, biases[4], padder)
    g2 = block(upsample(g3, w_up2, e2), w_dec2, biases[5], padder)
    g1 = block(upsample(g2, w_up1, e1), w_dec1, biases[6], padder)
    eps = unpatch(g1, w_head, noisy.shape[0])
    return final_update(noisy, eps, step_noise, timestep)

def reference(noisy, coarse, step_noise, timestep, w_time, w_embed, w_enc1, w_down1, w_enc2, w_down2, w_enc3, w_down3, w_qkv, w_attn_out, w_up3, w_dec3, w_up2, w_dec2, w_up1, w_dec1, w_head):
    return network(noisy, coarse, step_noise, timestep, w_time, w_embed, w_enc1, w_down1, w_enc2, w_down2, w_enc3, w_down3, w_qkv, w_attn_out, w_up3, w_dec3, w_up2, w_dec2, w_up1, w_dec1, w_head, pad_rims, whole_rows)
```

```python
import functools
import math

import jax
import jax.numpy as jnp
from jax import lax
from jax.experimental import pallas as pl
from jax.experimental.pallas import tpu as pltpu
from jax.sharding import PartitionSpec as P

HEAD_DIM = 64
T_STEPS = 1000
BF = jnp.bfloat16
F32 = jnp.float32
EPS = 1e-06


def plan(step):
    frac = (step.astype(jnp.float32) / T_STEPS + 0.008) / 1.008
    return jnp.cos(frac * (math.pi / 2)) ** 2


def time_embed(timestep, w_time):
    half = w_time.shape[0] // 2
    freqs = jnp.exp(-math.log(10000.0) * jnp.arange(half, dtype=jnp.float32) / half)
    angle = timestep.astype(jnp.float32)[0] * freqs
    feats = jnp.concatenate([jnp.sin(angle), jnp.cos(angle)])[None]
    return jax.nn.silu(jnp.dot(feats, w_time, precision=lax.Precision.HIGHEST))[0]


def update_factors(timestep):
    current_alpha_product = plan(timestep[0])
    abar_prev = plan(timestep[0] - 1)
    beta = jnp.minimum(1.0 - current_alpha_product / abar_prev, 0.999)
    keep = 1.0 / jnp.sqrt(1.0 - beta)
    noise = beta / jnp.sqrt(1.0 - current_alpha_product) * keep
    sigma = jnp.sqrt(beta * (1.0 - abar_prev) / (1.0 - current_alpha_product))
    return jnp.stack([keep, noise, sigma])


def iota(shape, dim):
    return lax.broadcasted_iota(jnp.int32, shape, dim)


def dotf(a, b):
    return jnp.dot(a, b, preferred_element_type=F32)


def mean_matrix(chans):
    size = 256
    same = (iota((size, size), 0) & -chans) == (iota((size, size), 1) & -chans)
    return jnp.where(same, 1.0 / chans, 0.0).astype(BF)


def scaled(x, bias, mean):
    squares = (x * x).astype(BF)
    size = mean.shape[0]
    parts = [dotf(squares[:, i : i + size], mean) for i in range(0, x.shape[1], size)]
    return x * lax.rsqrt(jnp.concatenate(parts, axis=1) + EPS) + bias


def activate(x, bias, mean):
    half = 0.5 * scaled(x, bias, mean)
    return half + half * jnp.tanh(half)


def row_factor(index, low, high, flags):
    return jnp.where(index < low, flags[0], jnp.where(index >= high, flags[1], 1.0))


def put_taps1(ref, parity, k, u):
    size = u.shape[0]
    pairs = [u[:, p * 128 : (p + 1) * 128] for p in range(4)]
    first = iota((size, 128), 1) < 64
    after = pairs[1:] + [pltpu.roll(pairs[0], size - 1, 0)]
    before = [pltpu.roll(pairs[3], 1, 0)] + pairs[:3]
    for p in range(4):
        ref[parity, k, :, p * 256 : p * 256 + 128] = pairs[p].astype(BF)
        ref[parity, k, :, p * 256 + 128 : (p + 1) * 256] = jnp.where(first, after[p], before[p]).astype(BF)


def put_taps(ref, k, u, chans):
    size, lanes = u.shape
    ref[k, :, 0:chans] = pltpu.roll(u[:, lanes - chans :], 1, 0).astype(BF)
    ref[k, :, chans : chans + lanes] = u.astype(BF)
    ref[k, :, chans + lanes :] = pltpu.roll(u[:, :chans], size - 1, 0).astype(BF)


def fill_conv1(out_ref, w_ref):
    chans = w_ref.shape[1]
    twice = jnp.where((iota((chans, 128), 1) & 63) == iota((chans, 128), 0), 1.0, 0.0).astype(BF)
    wide = dotf(w_ref[...], twice)
    left = iota((chans, 128), 1) < 64
    zero = jnp.zeros((chans, 128), F32)
    for t in range(4):
        for ro in range(2):
            a = t - ro
            for j, dx in enumerate((0, 1, 2, -1)):
                halves = []
                for co in range(2):
                    b = dx - co + 1
                    good = 0 <= a < 3 and 0 <= b < 3
                    halves.append(wide[(a * 3 + b) * chans : (a * 3 + b + 1) * chans] if good else zero)
                value = jnp.where(left, halves[0], halves[1]).astype(BF)
                row = t * 256 + j * 64
                out_ref[row : row + 64, ro * 128 : (ro + 1) * 128] = value


def fill_conv2(out_ref, w_ref):
    zero = jnp.zeros((128, 128), BF)
    for a in range(3):
        part = w_ref[a * 384 : (a + 1) * 384, :]
        out_ref[a * 512 : a * 512 + 384, 0:128] = part
        out_ref[a * 512 + 384 : (a + 1) * 512, 0:128] = zero
        out_ref[a * 512 : a * 512 + 128, 128:256] = zero
        out_ref[a * 512 + 128 : (a + 1) * 512, 128:256] = part


def conv1(taps_ref, i, count, w_ref):
    size = taps_ref.shape[2]
    rows = [
        taps_ref[1, pl.ds(i, count)],
        taps_ref[0, pl.ds(i + 1, count)],
        taps_ref[1, pl.ds(i + 1, count)],
        taps_ref[0, pl.ds(i + 2, count)],
    ]
    lhs = [
        jnp.concatenate([r[:, :, p * 256 : (p + 1) * 256].reshape(count * size, 256) for r in rows], axis=1)
        for p in range(4)
    ]
    return dotf(jnp.concatenate(lhs, axis=0), w_ref[...])


def conv(taps_ref, o, count, reach, w_ref):
    size = taps_ref.shape[1]
    rows = [taps_ref[pl.ds(o + a, count)] for a in range(3)]
    lhs = [
        jnp.concatenate(
            [r[:, :, q * 256 : q * 256 + reach].reshape(count * size, reach) for r in rows], axis=1
        )
        for q in range(2)
    ]
    return dotf(jnp.concatenate(lhs, axis=0), w_ref[...])


def loop(count, body):
    def step(i, carry):
        body(i)
        return carry

    lax.fori_loop(0, count, step, 0)


def fill_embed(out_ref, w_ref):
    feats, chans = w_ref.shape
    twice = jnp.where((iota((chans, 128), 1) & 63) == iota((chans, 128), 0), 1.0, 0.0).astype(BF)
    wide = dotf(w_ref[...], twice).astype(BF)
    k = iota((512, feats), 0)
    source = ((k >> 3) & 15) * 4 + (k & 1) * 2 + ((k >> 7) & 1)
    pick = jnp.where(source == iota((512, feats), 1), 1.0, 0.0).astype(BF)
    wide = dotf(pick, wide)
    k = iota((512, 128), 0)
    right = iota((512, 128), 1) >= 64
    same_cell = right == ((k >> 8) == 1)
    for i in range(4):
        keep = same_cell & (((k & 7) >> 1) == i)
        out_ref[:, i * 128 : (i + 1) * 128] = jnp.where(keep, wide, 0.0).astype(BF)


def embed_rows(noisy_ref, coarse_ref, w_ref, turn_ref):
    cols = noisy_ref.shape[2]
    n = cols // 16
    out = []
    for o in range(2):
        block = jnp.concatenate(
            [noisy_ref[:, o * 8 : (o + 1) * 8, :].reshape(64, cols), coarse_ref[:, o * 8 : (o + 1) * 8, :].reshape(64, cols)],
            axis=0,
        )
        turn_ref[o] = block.T
        lhs = [
            jnp.concatenate([turn_ref[o, pl.ds(4 * p + s, n, stride=16), :] for s in range(4)], axis=1)
            for p in range(4)
        ]
        res = dotf(jnp.concatenate(lhs, axis=0).astype(BF), w_ref[...])
        for i in range(4):
            out.append(
                jnp.concatenate([res[p * n : (p + 1) * n, i * 128 : (i + 1) * 128] for p in range(4)], axis=1)
            )
    return out


def embed_edge_kernel(w_ref, noisy_ref, coarse_ref, pay_ref, wide_ref, turn_ref, strip_ref):
    @pl.when(pl.program_id(0) == 0)
    def _():
        fill_embed(wide_ref, w_ref)

    rows = embed_rows(noisy_ref, coarse_ref, wide_ref, turn_ref)
    n = rows[0].shape[0]
    pay_ref[0, 0 : 8 * n, :] = jnp.concatenate(rows, axis=0).astype(BF)
    for j in range(8):
        strip_ref[j : j + 1, :] = rows[j][0:1]
        strip_ref[8 + j : 9 + j, :] = rows[j][n - 1 : n]
    pay_ref[0, 8 * n :, :] = strip_ref[...].astype(BF)


def embed_mid_kernel(w_ref, noisy_ref, coarse_ref, mid_ref, left_ref, right_ref, wide_ref, turn_ref, strip_ref):
    @pl.when(pl.program_id(0) == 0)
    def _():
        fill_embed(wide_ref, w_ref)

    rows = embed_rows(noisy_ref, coarse_ref, wide_ref, turn_ref)
    n = rows[0].shape[0]
    mid_ref[...] = jnp.concatenate(rows, axis=0).astype(BF)
    k = pl.program_id(0)
    base = pl.multiple_of(k * 8, 8)
    strip_ref[0, pl.ds(base, 8), :] = jnp.concatenate([r[0:1] for r in rows], axis=0)
    strip_ref[1, pl.ds(base, 8), :] = jnp.concatenate([r[n - 1 : n] for r in rows], axis=0)

    @pl.when(k == pl.num_programs(0) - 1)
    def _():
        left_ref[...] = strip_ref[0].astype(BF)
        right_ref[...] = strip_ref[1].astype(BF)


def whole(shape):
    return pl.BlockSpec(shape, lambda *_: (0,) * len(shape))


def embed_edges(noisy, coarse, w_embed):
    nvars, rows, cols = noisy.shape
    n = cols // 16
    last = rows // 16 - 1
    field = pl.BlockSpec((nvars, 16, cols), lambda k: (0, k * last, 0))
    return pl.pallas_call(
        embed_edge_kernel,
        name="embed_edges",
        grid=(2,),
        in_specs=[whole(w_embed.shape), field, field],
        out_specs=pl.BlockSpec((1, 8 * n + 16, 512), lambda k: (k, 0, 0)),
        out_shape=jax.ShapeDtypeStruct((2, 8 * n + 16, 512), BF),
        scratch_shapes=[pltpu.VMEM((512, 512), BF), pltpu.VMEM((2, cols, 128), F32), pltpu.VMEM((16, 512), F32)],
    )(w_embed, noisy, coarse)


def embed_middle(noisy, coarse, w_embed):
    nvars, rows, cols = noisy.shape
    n = cols // 16
    steps = rows // 16 - 2
    field = pl.BlockSpec((nvars, 16, cols), lambda k: (0, k + 1, 0))
    return pl.pallas_call(
        embed_mid_kernel,
        name="embed_middle",
        grid=(steps,),
        in_specs=[whole(w_embed.shape), field, field],
        out_specs=[pl.BlockSpec((8 * n, 512), lambda k: (k, 0)), whole((8 * steps, 512)), whole((8 * steps, 512))],
        out_shape=[
            jax.ShapeDtypeStruct((8 * steps * n, 512), BF),
            jax.ShapeDtypeStruct((8 * steps, 512), BF),
            jax.ShapeDtypeStruct((8 * steps, 512), BF),
        ],
        scratch_shapes=[
            pltpu.VMEM((512, 512), BF),
            pltpu.VMEM((2, cols, 128), F32),
            pltpu.VMEM((2, 8 * steps, 512), F32),
        ],
    )(w_embed, noisy, coarse)


def encoder_kernel(
    flags, bias_ref, pay_ref, mid_ref, top_ref, bot_ref, lhalo_ref, rhalo_ref,
    w1_ref, wd1_ref, w2_ref, wd2_ref, w3_ref, wd3_ref,
    e1_ref, e2_ref, e3_ref, d3_ref,
    conv1_ref, conv2_ref, lf_ref, rf_ref, h1_ref, taps1_ref, d1_ref, taps2_ref, d2_ref, taps3_ref,
    *, n, size, rows1,
):
    fill_conv1(conv1_ref, w1_ref)
    fill_conv2(conv2_ref, w2_ref)
    lf_ref[...] = lhalo_ref[...].astype(F32)
    rf_ref[...] = rhalo_ref[...].astype(F32)
    mean1, mean2, mean3 = mean_matrix(64), mean_matrix(128), mean_matrix(256)
    tail = size - n
    place = iota((tail, 512), 0)
    rows2, rows3 = rows1 // 2, rows1 // 4

    def first(x, index):
        full = []
        for j in range(4):
            right = rf_ref[pl.ds(index + j, 1), :]
            left = lf_ref[pl.ds(index + j, 1), :]
            rim = jnp.where(place == 0, right, jnp.where(place == tail - 1, left, 0.0))
            full += [x[j * n : (j + 1) * n], rim]
        h = jnp.concatenate(full, axis=0)
        u = activate(h, bias_ref[0:1, :], mean1)
        k = index // 2
        for j in range(4):
            part = u[j * size : (j + 1) * size] * row_factor(index + j, 8, rows1 + 8, flags)
            h1_ref[j % 2, k + j // 2] = h[j * size : (j + 1) * size].astype(BF)
            put_taps1(taps1_ref, j % 2, k + j // 2, part)

    for j in range(2):
        part = slice(j * 4 * n, (j + 1) * 4 * n)
        first(top_ref[part, :].astype(F32), j * 4)
        first(pay_ref[0, part, :].astype(F32), 8 + j * 4)
        first(pay_ref[1, part, :].astype(F32), rows1 + j * 4)
        first(bot_ref[part, :].astype(F32), rows1 + 8 + j * 4)
    loop((rows1 - 16) // 4, lambda i: first(mid_ref[pl.ds(pl.multiple_of(i * 4 * n, 4 * n), 4 * n), :].astype(F32), 16 + i * 4))

    count = 2

    def second(c):
        i = c * count
        acc = conv1(taps1_ref, i, count, conv1_ref)
        flat = count * size
        merged = []
        for p in range(4):
            halves = []
            for ro in range(2):
                lanes = slice(p * 128, (p + 1) * 128)
                prior = h1_ref[ro, pl.ds(i + 1, count), :, lanes].reshape(flat, 128).astype(F32)
                e = (prior + acc[p * flat : (p + 1) * flat, ro * 128 : (ro + 1) * 128]).astype(BF)
                e1_ref[ro, pl.ds(i, count), :, lanes] = e.reshape(count, size, 128)
                halves.append(e)
            merged.append(jnp.concatenate(halves, axis=1))
        d = dotf(jnp.concatenate(merged, axis=0), wd1_ref[...]).astype(BF)
        d = jnp.concatenate([d[p * flat : (p + 1) * flat] for p in range(4)], axis=1)
        d1_ref[pl.ds(i, count)] = d.reshape(count, size, 512)
        u = activate(d.astype(F32), bias_ref[1:2, :], mean2)
        for j in range(count):
            put_taps(taps2_ref, i + j, u[j * size : (j + 1) * size] * row_factor(i + j, 3, rows2 + 3, flags), 128)

    loop((rows2 + 6) // count, second)

    count2 = 2

    def third(c):
        i = c * count2
        o = 2 * i
        acc = conv(taps2_ref, o, 2 * count2, 512, conv2_ref)
        flat = 2 * count2 * size
        merged = []
        for q in range(2):
            lanes = slice(q * 256, (q + 1) * 256)
            prior = d1_ref[pl.ds(o + 1, 2 * count2), :, lanes].reshape(flat, 256).astype(F32)
            e = (prior + acc[q * flat : (q + 1) * flat]).astype(BF).reshape(2 * count2, size, 256)
            e2_ref[pl.ds(o, 2 * count2), :, lanes] = e
            for j in range(count2):
                merged.append(jnp.concatenate([e[2 * j], e[2 * j + 1]], axis=1))
        d = dotf(jnp.concatenate(merged, axis=0), wd2_ref[...]).astype(BF)
        d = jnp.concatenate([d[: flat // 2], d[flat // 2 :]], axis=1)
        d2_ref[pl.ds(i, count2)] = d.reshape(count2, size, 512)
        u = activate(d.astype(F32), bias_ref[2:3, :], mean3)
        for j in range(count2):
            put_taps(taps3_ref, i + j, u[j * size : (j + 1) * size] * row_factor(i + j, 1, rows3 + 1, flags), 256)

    loop((rows3 + 2) // count2, third)

    def fourth(i):
        o = 4 * i
        acc = conv(taps3_ref, o, 4, 768, w3_ref)
        flat = 4 * size
        acc = jnp.concatenate([acc[:flat], acc[flat:]], axis=1)
        e = (d2_ref[pl.ds(o + 1, 4)].reshape(flat, 512).astype(F32) + acc).astype(BF).reshape(4, size, 512)
        e3_ref[pl.ds(o, 4)] = e
        merged = [jnp.concatenate([e[2 * j], e[2 * j + 1]], axis=1) for j in range(2)]
        d = dotf(jnp.concatenate(merged, axis=0), wd3_ref[...])
        for j in range(2):
            d3_ref[2 * i + j] = d[j * size : j * size + n].astype(BF)

    loop(rows3 // 4, fourth)


def encoder(flags, biases, pay, mid, top, bot, lhalo, rhalo, weights, n, size):
    rows1 = lhalo.shape[0] - 16
    k1, rows2, rows3 = rows1 // 2 + 8, rows1 // 2, rows1 // 4
    vmem = pltpu.VMEM
    return pl.pallas_call(
        functools.partial(encoder_kernel, n=n, size=size, rows1=rows1),
        name="encoder",
        in_specs=[pl.BlockSpec(memory_space=pltpu.SMEM)] + [pl.BlockSpec(memory_space=pltpu.VMEM)] * 13,
        out_specs=[pl.BlockSpec(memory_space=pltpu.VMEM)] * 4,
        out_shape=[
            jax.ShapeDtypeStruct((2, rows2 + 6, size, 512), BF),
            jax.ShapeDtypeStruct((rows2 + 4, size, 512), BF),
            jax.ShapeDtypeStruct((rows3, size, 512), BF),
            jax.ShapeDtypeStruct((rows3 // 2, n, 512), BF),
        ],
        scratch_shapes=[
            vmem((1024, 256), BF),
            vmem((1536, 256), BF),
            vmem((rows1 + 16, 512), F32),
            vmem((rows1 + 16, 512), F32),
            vmem((2, k1, size, 512), BF),
            vmem((2, k1, size, 1024), BF),
            vmem((rows2 + 6, size, 512), BF),
            vmem((rows2 + 6, size, 768), BF),
            vmem((rows3 + 2, size, 512), BF),
            vmem((rows3 + 2, size, 1024), BF),
        ],
    )(flags, biases, pay, mid, top, bot, lhalo, rhalo, *weights)


def attention_kernel(
    x_ref, bias_ref, e3_ref, lhalo_ref, rhalo_ref, wqkv_ref, wout_ref, out_ref, full_ref, mixed_ref, a4_ref, *, n, size
):
    tail = size - n
    place = iota((tail, 512), 0)
    rows, length, width = x_ref.shape
    lf = lhalo_ref[...].astype(F32)
    rf = rhalo_ref[...].astype(F32)
    for r in range(e3_ref.shape[0]):
        rim = jnp.where(place == 0, rf[r : r + 1], jnp.where(place == tail - 1, lf[r : r + 1], 0.0))
        full_ref[r] = jnp.concatenate([e3_ref[r, 0:n, :].astype(F32), rim], axis=0).astype(BF)

    scale = HEAD_DIM**-0.5
    for row in range(rows):
        x = x_ref[row].astype(F32)
        mean = jnp.mean(x * x, axis=1, keepdims=True)
        u = (x * lax.rsqrt(mean + EPS) + bias_ref[3:4, :]).astype(BF)
        qkv = dotf(u, wqkv_ref[...]).astype(BF)
        left = iota((length, 128), 1) < 64
        for h in range(width // 128):
            q = qkv[:, h * 128 : (h + 1) * 128].astype(F32) * scale
            k = qkv[:, width + h * 128 : width + (h + 1) * 128]
            v = qkv[:, 2 * width + h * 128 : 2 * width + (h + 1) * 128]
            outs = []
            for side in range(2):
                mine = left if side == 0 else jnp.logical_not(left)
                qs = jnp.where(mine, q, 0.0).astype(BF)
                s = lax.dot_general(qs, k, (((1,), (1,)), ((), ())), preferred_element_type=F32)
                e = jnp.exp(s - jnp.max(s, axis=1, keepdims=True))
                total = jnp.sum(e, axis=1, keepdims=True)
                outs.append(dotf(e.astype(BF), v) / total)
            mixed_ref[:, h * 128 : (h + 1) * 128] = jnp.where(left, outs[0], outs[1]).astype(BF)
        a4_ref[...] = x + dotf(mixed_ref[...], wout_ref[...])
        for t in range(length // n):
            after = (t * n + n) % length
            before = (t * n - 1) % length
            rim = jnp.where(
                place == 0,
                a4_ref[after : after + 1, :],
                jnp.where(place == tail - 1, a4_ref[before : before + 1, :], 0.0),
            )
            out_ref[t, row] = jnp.concatenate([a4_ref[t * n : (t + 1) * n, :], rim], axis=0).astype(BF)


def attention(x, biases, e3, lhalo, rhalo, w_qkv, w_out, n, size):
    rows, length, width = x.shape
    return pl.pallas_call(
        functools.partial(attention_kernel, n=n, size=size),
        name="attention",
        out_shape=[
            jax.ShapeDtypeStruct((length // n, rows, size, width), BF),
            jax.ShapeDtypeStruct((e3.shape[0], size, width), BF),
        ],
        scratch_shapes=[pltpu.VMEM((length, width), BF), pltpu.VMEM((length, width), F32)],
    )(x, biases, e3, lhalo, rhalo, w_qkv, w_out)


def fill_head(out_ref, w_ref):
    chans, outs = w_ref.shape
    col = iota((outs, 512), 1)
    source = ((col >> 3) & 7) * 4 + (col & 1) * 2 + ((col >> 7) & 1)
    pick = jnp.where(source == iota((outs, 512), 0), 1.0, 0.0).astype(BF)
    wide = dotf(w_ref[...], pick)
    col = iota((chans, 512), 1)
    for o in range(2):
        for i in range(4):
            for c in range(2):
                keep = (((col >> 6) & 1) == o) & (((col & 7) >> 1) == i) & ((col >> 8) == c)
                row = o * 512 + i * 128 + c * 64
                out_ref[row : row + 64, :] = jnp.where(keep, wide, 0.0).astype(BF)


def decoder_kernel(
    flags, factors, bias_ref, a4_ref, e3_ref, top_ref, bot_ref, e2_ref, e1_ref,
    wu3_ref, w3_ref, wu2_ref, w2_ref, wu1_ref, w1_ref, wh_ref, noisy_ref, noise_ref,
    out_ref,
    conv1_ref, conv2_ref, head_ref, h3_ref, taps3_ref, h2_ref, taps2_ref, h1_ref, taps1_ref, turn_ref,
    *, n, size, rows1,
):
    rows2, rows3 = rows1 // 2, rows1 // 4
    rows4 = rows1 // 8
    step = pl.program_id(0)

    def prepare():
        fill_conv1(conv1_ref, w1_ref)
        fill_conv2(conv2_ref, w2_ref)
        fill_head(head_ref, wh_ref)
        mean1, mean2, mean3 = mean_matrix(64), mean_matrix(128), mean_matrix(256)

        def third(a, e, index):
            count = a.shape[0]
            spread = dotf(a.reshape(count * size, 512), wu3_ref[...])
            for j in range(count):
                for ro in range(2):
                    part = spread[j * size : (j + 1) * size, ro * 512 : (ro + 1) * 512]
                    h = (part + e[2 * j + ro].astype(F32)).astype(BF)
                    row = 2 * (index + j) + ro
                    h3_ref[row] = h
                    u = activate(h.astype(F32), bias_ref[4:5, :], mean3)
                    put_taps(taps3_ref, row, u * row_factor(row, 2, rows3 + 2, flags), 256)

        third(top_ref[0:1], top_ref[1:3], 0)
        third(bot_ref[0:1], bot_ref[1:3], rows4 + 1)
        loop(rows4 // 2, lambda i: third(a4_ref[pl.ds(2 * i, 2)], e3_ref[pl.ds(4 * i, 4)], 1 + 2 * i))

        count3 = 2

        def second(c):
            o = c * count3
            acc = conv(taps3_ref, o, count3, 768, w3_ref)
            flat = count3 * size
            g = []
            for q in range(2):
                prior = h3_ref[pl.ds(o + 1, count3), :, q * 256 : (q + 1) * 256].reshape(flat, 256).astype(F32)
                g.append((prior + acc[q * flat : (q + 1) * flat]).astype(BF))
            spread = dotf(jnp.concatenate(g, axis=0), wu2_ref[...])
            for j in range(count3):
                for ro in range(2):
                    part = [
                        spread[q * flat + j * size : q * flat + (j + 1) * size, ro * 256 : (ro + 1) * 256]
                        for q in range(2)
                    ]
                    row = 2 * (o + j) + ro
                    h = (jnp.concatenate(part, axis=1) + e2_ref[row].astype(F32)).astype(BF)
                    h2_ref[row] = h
                    u = activate(h.astype(F32), bias_ref[5:6, :], mean2)
                    put_taps(taps2_ref, row, u * row_factor(row, 2, rows2 + 2, flags), 128)

        loop((rows3 + 2) // count3, second)

        count2 = 2

        def first(c):
            o = c * count2
            acc = conv(taps2_ref, o, count2, 512, conv2_ref)
            flat = count2 * size
            g = []
            for q in range(2):
                prior = h2_ref[pl.ds(o + 1, count2), :, q * 256 : (q + 1) * 256].reshape(flat, 256).astype(F32)
                both = (prior + acc[q * flat : (q + 1) * flat]).astype(BF)
                g += [both[:, :128], both[:, 128:]]
            spread = dotf(jnp.concatenate(g, axis=0), wu1_ref[...])
            for j in range(count2):
                for ro in range(2):
                    part = [
                        spread[p * flat + j * size : p * flat + (j + 1) * size, ro * 128 : (ro + 1) * 128]
                        for p in range(4)
                    ]
                    h = (jnp.concatenate(part, axis=1) + e1_ref[ro, o + j + 2].astype(F32)).astype(BF)
                    h1_ref[ro, o + j] = h
                    u = activate(h.astype(F32), bias_ref[6:7, :], mean1)
                    row = 2 * (o + j) + ro
                    put_taps1(taps1_ref, ro, o + j, u * row_factor(row, 2, rows1 + 2, flags))

        loop((rows2 + 2) // count2, first)

    pl.when(step == 0)(prepare)

    i = step * 4
    acc = conv1(taps1_ref, i, 4, conv1_ref)
    flat = 4 * size
    octets = []
    g = []
    for p in range(4):
        halves = []
        for ro in range(2):
            prior = h1_ref[ro, pl.ds(i + 1, 4), :, p * 128 : (p + 1) * 128].reshape(flat, 128).astype(F32)
            halves.append((prior + acc[p * flat : (p + 1) * flat, ro * 128 : (ro + 1) * 128]).astype(BF))
        both = jnp.concatenate(halves, axis=1)
        g.append(jnp.concatenate([both[j * size : (j + 1) * size] for j in range(4)], axis=1))
    spread = dotf(jnp.concatenate(g, axis=0), head_ref[...])
    for p in range(4):
        for s in range(4):
            turn_ref[pl.ds(4 * p + s, n, stride=16), :] = spread[p * size : p * size + n, s * 128 : (s + 1) * 128]
    eps = turn_ref[...].T
    nvars, _, cols = noisy_ref.shape
    for o in range(2):
        part = eps[o * 64 : (o + 1) * 64].reshape(nvars, 8, cols)
        rows = slice(o * 8, (o + 1) * 8)
        out_ref[:, rows, :] = factors[0] * noisy_ref[:, rows, :] - factors[1] * part + factors[2] * noise_ref[:, rows, :]


def decoder(flags, factors, biases, a4, e3, top, bot, e2, e1, weights, noisy, step_noise, n, size):
    nvars, lat, cols = noisy.shape
    rows1 = lat // 2
    rows2, rows3 = rows1 // 2, rows1 // 4
    field = pl.BlockSpec((nvars, 16, cols), lambda k: (0, k, 0))
    smem = pl.BlockSpec(memory_space=pltpu.SMEM)
    vmem = pltpu.VMEM
    return pl.pallas_call(
        functools.partial(decoder_kernel, n=n, size=size, rows1=rows1),
        name="decoder",
        grid=(rows1 // 8,),
        in_specs=[smem, smem] + [pl.BlockSpec(memory_space=pltpu.VMEM)] * 14 + [field, field],
        out_specs=field,
        out_shape=jax.ShapeDtypeStruct(noisy.shape, F32),
        scratch_shapes=[
            vmem((1024, 256), BF),
            vmem((1536, 256), BF),
            vmem((1024, 512), BF),
            vmem((rows3 + 4, size, 512), BF),
            vmem((rows3 + 4, size, 1024), BF),
            vmem((rows2 + 4, size, 512), BF),
            vmem((rows2 + 4, size, 768), BF),
            vmem((2, rows2 + 2, size, 512), BF),
            vmem((2, rows2 + 2, size, 1024), BF),
            vmem((cols, 128), F32),
        ],
    )(flags, factors, biases, a4, e3, top, bot, e2, e1, *weights, noisy, step_noise)


def shift(array, axis, by, closed):
    count = lax.axis_size(axis)
    if closed:
        pairs = [(i, (i + by) % count) for i in range(count)]
    else:
        pairs = [(i, i + by) for i in range(count) if 0 <= i + by < count]
    return lax.ppermute(array, axis, pairs)


def body(
    noisy, coarse, step_noise, timestep, w_time, w_embed, w_enc1, w_down1, w_enc2, w_down2, w_enc3, w_down3,
    w_qkv, w_attn_out, w_up3, w_dec3, w_up2, w_dec2, w_up1, w_dec1, w_head,
):
    nvars, lat, cols = noisy.shape
    n = cols // 16
    size = -(-(n + 2) // 16) * 16
    rows1 = lat // 2
    rows4 = lat // 16
    groups = lax.axis_size("lon")
    lat_at, lat_count = lax.axis_index("lat"), lax.axis_size("lat")
    flags = jnp.stack([lat_at > 0, lat_at < lat_count - 1]).astype(F32)

    pay = embed_edges(noisy, coarse, w_embed)
    from_top = shift(pay[1], "lat", 1, False)
    from_bot = shift(pay[0], "lat", -1, False)
    mid, mid_left, mid_right = embed_middle(noisy, coarse, w_embed)

    temb = time_embed(timestep, w_time)
    factors = update_factors(timestep)
    widths = [w_enc1.shape[1], w_enc2.shape[1], w_enc3.shape[1], w_qkv.shape[0], w_dec3.shape[1], w_dec2.shape[1], w_dec1.shape[1]]
    starts = [sum(widths[:i]) for i in range(7)]
    biases = jnp.stack([jnp.tile(temb[s : s + w], 512 // w) for s, w in zip(starts, widths)])

    cut = 8 * n
    left = jnp.concatenate([from_top[cut : cut + 8], pay[0, cut : cut + 8], mid_left, pay[1, cut : cut + 8], from_bot[cut : cut + 8]])
    right = jnp.concatenate([from_top[cut + 8 :], pay[0, cut + 8 :], mid_right, pay[1, cut + 8 :], from_bot[cut + 8 :]])
    rhalo = shift(left, "lon", -1, True)
    lhalo = shift(right, "lon", 1, True)

    e1, e2, e3, d3 = encoder(
        flags, biases, pay, mid, from_top, from_bot, lhalo, rhalo,
        (w_enc1, w_down1, w_enc2, w_down2, w_enc3, w_down3), n, size,
    )

    rhalo3 = shift(e3[:, 0], "lon", -1, True)
    lhalo3 = shift(e3[:, n - 1], "lon", 1, True)

    copies = max(1, groups // rows4)
    each = max(1, rows4 // groups)
    sent = jnp.repeat(d3, copies, axis=0) if copies > 1 else d3
    got = lax.all_to_all(sent.reshape(groups, each * n, 512), "lon", split_axis=0, concat_axis=0, tiled=True)
    got = got.reshape(groups, each, n, 512)
    got = got.transpose(1, 0, 2, 3).reshape(each, groups * n, 512) if each > 1 else got.reshape(1, groups * n, 512)
    out, e3 = attention(got, biases, e3, lhalo3, rhalo3, w_qkv, w_attn_out, n, size)
    a4 = lax.all_to_all(out.reshape(groups, each * size, 512), "lon", split_axis=0, concat_axis=0, tiled=True)
    a4 = a4.reshape(groups * each, size, 512)
    if copies > 1:
        a4 = a4.reshape(rows4, copies, size, 512)[:, 0]

    top = shift(jnp.concatenate([a4[-1:], e3[-2:]]), "lat", 1, False)
    bot = shift(jnp.concatenate([a4[:1], e3[:2]]), "lat", -1, False)
    return decoder(
        flags, factors, biases, a4, e3, top, bot, e2, e1,
        (w_up3, w_dec3, w_up2, w_dec2, w_up1, w_dec1, w_head), noisy, step_noise, n, size,
    )


def solution(mesh):
    field = P(None, "lat", "lon")
    return jax.shard_map(
        body, mesh=mesh, in_specs=(field, field, field) + (P(),) * 18, out_specs=field, check_vma=False
    )
```

```python
import functools
import math

import jax
import jax.numpy as jnp
from jax import lax
from jax.experimental import pallas as pl
from jax.experimental.pallas import tpu as pltpu
from jax.sharding import PartitionSpec as P

HEAD_DIM = 64
T_STEPS = 1000
BF = jnp.bfloat16
F32 = jnp.float32
EPS = 1e-06


def plan(step):
    frac = (step.astype(jnp.float32) / T_STEPS + 0.008) / 1.008
    return jnp.cos(frac * (math.pi / 2)) ** 2


def time_embed(timestep, w_time):
    half = w_time.shape[0] // 2
    freqs = jnp.exp(-math.log(10000.0) * jnp.arange(half, dtype=jnp.float32) / half)
    angle = timestep.astype(jnp.float32)[0] * freqs
    feats = jnp.concatenate([jnp.sin(angle), jnp.cos(angle)])[None]
    return jax.nn.silu(jnp.dot(feats, w_time, precision=lax.Precision.HIGHEST))[0]


def update_factors(timestep):
    current_alpha_product = plan(timestep[0])
    abar_prev = plan(timestep[0] - 1)
    beta = jnp.minimum(1.0 - current_alpha_product / abar_prev, 0.999)
    keep = 1.0 / jnp.sqrt(1.0 - beta)
    noise = beta / jnp.sqrt(1.0 - current_alpha_product) * keep
    sigma = jnp.sqrt(beta * (1.0 - abar_prev) / (1.0 - current_alpha_product))
    return jnp.stack([keep, noise, sigma])


def iota(shape, dim):
    return lax.broadcasted_iota(jnp.int32, shape, dim)


def dotf(a, b):
    return jnp.dot(a, b, preferred_element_type=F32)


def mean_matrix(chans):
    size = 256
    same = (iota((size, size), 0) & -chans) == (iota((size, size), 1) & -chans)
    return jnp.where(same, 1.0 / chans, 0.0).astype(BF)


def scaled(x, bias, mean):
    squares = (x * x).astype(BF)
    size = mean.shape[0]
    parts = [dotf(squares[:, i : i + size], mean) for i in range(0, x.shape[1], size)]
    return x * lax.rsqrt(jnp.concatenate(parts, axis=1) + EPS) + bias


def activate(x, bias, mean):
    half = 0.5 * scaled(x, bias, mean)
    return half + half * jnp.tanh(half)


def row_factor(index, low, high, flags):
    return jnp.where(index < low, flags[0], jnp.where(index >= high, flags[1], 1.0))


def put_taps1(ref, parity, k, u):
    size = u.shape[0]
    pairs = [u[:, p * 128 : (p + 1) * 128] for p in range(4)]
    first = iota((size, 128), 1) < 64
    after = pairs[1:] + [pltpu.roll(pairs[0], size - 1, 0)]
    before = [pltpu.roll(pairs[3], 1, 0)] + pairs[:3]
    for p in range(4):
        ref[parity, k, :, p * 256 : p * 256 + 128] = pairs[p].astype(BF)
        ref[parity, k, :, p * 256 + 128 : (p + 1) * 256] = jnp.where(first, after[p], before[p]).astype(BF)


def put_taps(ref, k, u, chans):
    size, lanes = u.shape
    ref[k, :, 0:chans] = pltpu.roll(u[:, lanes - chans :], 1, 0).astype(BF)
    ref[k, :, chans : chans + lanes] = u.astype(BF)
    ref[k, :, chans + lanes :] = pltpu.roll(u[:, :chans], size - 1, 0).astype(BF)


def fill_conv1(out_ref, w_ref):
    chans = w_ref.shape[1]
    twice = jnp.where((iota((chans, 128), 1) & 63) == iota((chans, 128), 0), 1.0, 0.0).astype(BF)
    wide = dotf(w_ref[...], twice)
    left = iota((chans, 128), 1) < 64
    zero = jnp.zeros((chans, 128), F32)
    for t in range(4):
        for ro in range(2):
            a = t - ro
            for j, dx in enumerate((0, 1, 2, -1)):
                halves = []
                for co in range(2):
                    b = dx - co + 1
                    good = 0 <= a < 3 and 0 <= b < 3
                    halves.append(wide[(a * 3 + b) * chans : (a * 3 + b + 1) * chans] if good else zero)
                value = jnp.where(left, halves[0], halves[1]).astype(BF)
                row = t * 256 + j * 64
                out_ref[row : row + 64, ro * 128 : (ro + 1) * 128] = value


def fill_conv2(out_ref, w_ref):
    zero = jnp.zeros((128, 128), BF)
    for a in range(3):
        part = w_ref[a * 384 : (a + 1) * 384, :]
        out_ref[a * 512 : a * 512 + 384, 0:128] = part
        out_ref[a * 512 + 384 : (a + 1) * 512, 0:128] = zero
        out_ref[a * 512 : a * 512 + 128, 128:256] = zero
        out_ref[a * 512 + 128 : (a + 1) * 512, 128:256] = part


def conv1(taps_ref, i, count, w_ref):
    size = taps_ref.shape[2]
    rows = [
        taps_ref[1, pl.ds(i, count)],
        taps_ref[0, pl.ds(i + 1, count)],
        taps_ref[1, pl.ds(i + 1, count)],
        taps_ref[0, pl.ds(i + 2, count)],
    ]
    lhs = [
        jnp.concatenate([r[:, :, p * 256 : (p + 1) * 256].reshape(count * size, 256) for r in rows], axis=1)
        for p in range(4)
    ]
    return dotf(jnp.concatenate(lhs, axis=0), w_ref[...])


def conv(taps_ref, o, count, reach, w_ref):
    size = taps_ref.shape[1]
    rows = [taps_ref[pl.ds(o + a, count)] for a in range(3)]
    lhs = [
        jnp.concatenate(
            [r[:, :, q * 256 : q * 256 + reach].reshape(count * size, reach) for r in rows], axis=1
        )
        for q in range(2)
    ]
    return dotf(jnp.concatenate(lhs, axis=0), w_ref[...])


def loop(count, body):
    def step(i, carry):
        body(i)
        return carry

    lax.fori_loop(0, count, step, 0)


def divisor(total, most):
    return max(d for d in range(1, most + 1) if total % d == 0)


def loop_chunks(total, chunk, body):
    chunk = min(chunk, total)
    steps = -(-total // chunk)
    loop(steps, lambda c: body(jnp.minimum(c * chunk, total - chunk), chunk))


def fill_embed(out_ref, w_ref):
    feats, chans = w_ref.shape
    twice = jnp.where((iota((chans, 128), 1) & 63) == iota((chans, 128), 0), 1.0, 0.0).astype(BF)
    wide = dotf(w_ref[...], twice).astype(BF)
    k = iota((512, feats), 0)
    source = ((k >> 3) & 15) * 4 + (k & 1) * 2 + ((k >> 7) & 1)
    pick = jnp.where(source == iota((512, feats), 1), 1.0, 0.0).astype(BF)
    wide = dotf(pick, wide)
    k = iota((512, 128), 0)
    right = iota((512, 128), 1) >= 64
    same_cell = right == ((k >> 8) == 1)
    for i in range(4):
        keep = same_cell & (((k & 7) >> 1) == i)
        out_ref[:, i * 128 : (i + 1) * 128] = jnp.where(keep, wide, 0.0).astype(BF)


def embed_rows(noisy_ref, coarse_ref, w_ref, turn_ref):
    cols = noisy_ref.shape[2]
    n = cols // 16
    out = []
    for o in range(2):
        block = jnp.concatenate(
            [noisy_ref[:, o * 8 : (o + 1) * 8, :].reshape(64, cols), coarse_ref[:, o * 8 : (o + 1) * 8, :].reshape(64, cols)],
            axis=0,
        )
        turn_ref[o] = block.T
        lhs = [
            jnp.concatenate([turn_ref[o, pl.ds(4 * p + s, n, stride=16), :] for s in range(4)], axis=1)
            for p in range(4)
        ]
        res = dotf(jnp.concatenate(lhs, axis=0).astype(BF), w_ref[...])
        for i in range(4):
            out.append(
                jnp.concatenate([res[p * n : (p + 1) * n, i * 128 : (i + 1) * 128] for p in range(4)], axis=1)
            )
    return out


def strips_kernel(w_ref, nl_ref, cl_ref, nr_ref, cr_ref, wide_ref, left_ref, right_ref, turn_ref, strip_ref):
    fill_embed(wide_ref, w_ref)
    octets = nl_ref.shape[1] // 8
    first = iota((64, 128), 1) < 64
    for o in range(octets):
        rows = slice(o * 8, (o + 1) * 8)
        block = jnp.concatenate(
            [
                jnp.where(first, a[:, rows, :].reshape(64, 128), b[:, rows, :].reshape(64, 128))
                for a, b in ((nl_ref, nr_ref), (cl_ref, cr_ref))
            ],
            axis=0,
        ).T
        turn_ref[0, o * 16 : (o + 1) * 16, :] = block[:16]
        turn_ref[1, o * 16 : (o + 1) * 16, :] = block[112:]
    lhs = [
        jnp.concatenate([turn_ref[side, pl.ds(4 * p + s, octets, stride=16), :] for s in range(4)], axis=1)
        for side in range(2)
        for p in range(4)
    ]
    res = dotf(jnp.concatenate(lhs, axis=0).astype(BF), wide_ref[...])
    for side, out_ref in ((0, left_ref), (1, right_ref)):
        for p in range(4):
            at = (side * 4 + p) * octets
            for i in range(4):
                strip_ref[p, pl.ds(i, octets, stride=4), :] = res[at : at + octets, i * 128 : (i + 1) * 128]
        for p in range(4):
            out_ref[:, p * 128 : (p + 1) * 128] = strip_ref[p].astype(BF)


def embed_mid_kernel(wide_ref, noisy_ref, coarse_ref, mid_ref, turn_ref):
    mid_ref[...] = jnp.concatenate(embed_rows(noisy_ref, coarse_ref, wide_ref, turn_ref), axis=0).astype(BF)


def embed_edge_kernel(wide_ref, left_ref, right_ref, noisy_ref, coarse_ref, top_ref, bot_ref, turn_ref):
    rows = embed_rows(noisy_ref, coarse_ref, wide_ref, turn_ref)
    n = rows[0].shape[0]
    count = left_ref.shape[0]
    for k, ref in ((0, top_ref), (1, bot_ref)):

        @pl.when(pl.program_id(0) == k)
        def _(k=k, ref=ref):
            ref[0 : 8 * n, :] = jnp.concatenate(rows, axis=0).astype(BF)
            at = slice(0, 16) if k == 0 else slice(count - 16, count)
            pick = slice(0, 8) if k == 0 else slice(8, 16)
            rims = [r[at, :].astype(F32)[pick] for r in (left_ref, right_ref)]
            ref[8 * n :, :] = jnp.concatenate(rims, axis=0).astype(BF)


def near(array):
    return pltpu.with_memory_space_constraint(array, pltpu.VMEM)


ANYWHERE = pl.BlockSpec(memory_space=pl.ANY)


class Fetch:
    def __init__(self, sems, **pairs):
        self.copies = {name: pltpu.make_async_copy(src, dst, sems.at[i]) for i, (name, (src, dst)) in enumerate(pairs.items())}
        for copy in self.copies.values():
            copy.start()

    def wait(self, *names):
        for name in names:
            self.copies[name].wait()


def whole(shape):
    return pl.BlockSpec(shape, lambda *_: (0,) * len(shape))


def embed_strips(noisy, coarse, w_embed):
    nvars, rows, cols = noisy.shape
    sides = [pl.BlockSpec((nvars, rows, 128), lambda k: (0, 0, 0)), pl.BlockSpec((nvars, rows, 128), lambda k: (0, 0, cols // 128 - 1))]
    strip = jax.ShapeDtypeStruct((rows // 2, 512), BF)
    return pl.pallas_call(
        strips_kernel,
        name="embed_strips",
        grid=(1,),
        in_specs=[whole(w_embed.shape), sides[0], sides[0], sides[1], sides[1]],
        out_specs=[whole((512, 512)), whole(strip.shape), whole(strip.shape)],
        out_shape=[jax.ShapeDtypeStruct((512, 512), BF), strip, strip],
        scratch_shapes=[pltpu.VMEM((2, rows * 2, 128), F32), pltpu.VMEM((4, rows // 2, 128), F32)],
    )(w_embed, noisy, coarse, noisy, coarse)


def embed_edges(noisy, coarse, wide, left, right):
    nvars, rows, cols = noisy.shape
    n = cols // 16
    last = rows // 16 - 1
    field = pl.BlockSpec((nvars, 16, cols), lambda k: (0, k * last, 0))
    pay = jax.ShapeDtypeStruct((8 * n + 16, 512), BF)
    return pl.pallas_call(
        embed_edge_kernel,
        name="embed_edges",
        grid=(2,),
        in_specs=[whole(wide.shape), whole(left.shape), whole(right.shape), field, field],
        out_specs=[whole(pay.shape)] * 2,
        out_shape=[pay, pay],
        scratch_shapes=[pltpu.VMEM((2, cols, 128), F32)],
    )(wide, near(left), near(right), noisy, coarse)


def embed_middle(noisy, coarse, wide):
    nvars, rows, cols = noisy.shape
    n = cols // 16
    steps = rows // 16 - 2
    field = pl.BlockSpec((nvars, 16, cols), lambda k: (0, k + 1, 0))
    return pl.pallas_call(
        embed_mid_kernel,
        name="embed_middle",
        grid=(steps,),
        in_specs=[whole(wide.shape), field, field],
        out_specs=pl.BlockSpec((8 * n, 512), lambda k: (k, 0)),
        out_shape=jax.ShapeDtypeStruct((8 * steps * n, 512), BF),
        scratch_shapes=[pltpu.VMEM((2, cols, 128), F32)],
    )(wide, noisy, coarse)


def full_rows(x, left, right, n, size):
    tail = size - n
    place = iota((tail, 512), 0)
    full = []
    for j in range(x.shape[0] // n):
        rim = jnp.where(place == 0, right[j], jnp.where(place == tail - 1, left[j], 0.0))
        full += [x[j * n : (j + 1) * n], rim]
    return jnp.concatenate(full, axis=0)


def level1(h_ref, taps_ref, k, h, bias, mean, factor=None):
    size = h_ref.shape[2]
    u = activate(h, bias, mean)
    for j in range(h.shape[0] // size):
        part = u[j * size : (j + 1) * size]
        h_ref[j % 2, k + j // 2] = h[j * size : (j + 1) * size].astype(BF)
        put_taps1(taps_ref, j % 2, k + j // 2, part if factor is None else part * factor)


def enc_conv1(taps_ref, h_ref, i, count, conv_ref, wd_ref, store):
    size = taps_ref.shape[2]
    acc = conv1(taps_ref, i, count, conv_ref)
    flat = count * size
    merged = []
    for p in range(4):
        halves = []
        for ro in range(2):
            lanes = slice(p * 128, (p + 1) * 128)
            prior = h_ref[ro, pl.ds(i + 1, count), :, lanes].reshape(flat, 128).astype(F32)
            e = (prior + acc[p * flat : (p + 1) * flat, ro * 128 : (ro + 1) * 128]).astype(BF)
            store(ro, lanes, e.reshape(count, size, 128))
            halves.append(e)
        merged.append(jnp.concatenate(halves, axis=1))
    d = dotf(jnp.concatenate(merged, axis=0), wd_ref[...]).astype(BF)
    return jnp.concatenate([d[p * flat : (p + 1) * flat] for p in range(4)], axis=1)


def encoder_own_kernel(
    bias_ref, mid_ref, top_ref, bot_ref, lhalo_ref, rhalo_ref, w1_ref, wd1_ref, w2_ref,
    e1_out, d1_out, taps2_out, edge_h_out, edge_taps_out, conv1_out, conv2_out,
    lf_ref, rf_ref, h1_ref, taps1_ref, e1_ref, d1_ref, taps2_ref, conv1_ref, conv2_ref, sem, sems,
    *, n, size,
):
    fill_conv1(conv1_ref, w1_ref)
    fill_conv2(conv2_ref, w2_ref)
    weights_out = Fetch(sems, conv1=(conv1_ref, conv1_out), conv2=(conv2_ref, conv2_out))
    lf_ref[...] = lhalo_ref[...].astype(F32)
    rf_ref[...] = rhalo_ref[...].astype(F32)
    mean1, mean2 = mean_matrix(64), mean_matrix(128)
    rows1 = lhalo_ref.shape[0]

    def first(x, row):
        left = [lf_ref[pl.ds(row + j, 1), :] for j in range(4)]
        right = [rf_ref[pl.ds(row + j, 1), :] for j in range(4)]
        k = row // 2
        level1(h1_ref, taps1_ref, k, full_rows(x.astype(F32), left, right, n, size), bias_ref[0:1, :], mean1)

    for j in range(2):
        part = slice(j * 4 * n, (j + 1) * 4 * n)
        first(top_ref[part, :], j * 4)
        first(bot_ref[part, :], rows1 - 8 + j * 4)
    loop((rows1 - 16) // 4, lambda i: first(mid_ref[pl.ds(pl.multiple_of(i * 4 * n, 4 * n), 4 * n), :], 8 + i * 4))

    edges = []
    for side, k in ((0, 0), (1, rows1 // 2 - 2)):
        for t, (source, out) in enumerate(((h1_ref, edge_h_out), (taps1_ref, edge_taps_out))):
            for ro in range(2):
                copy = pltpu.make_async_copy(
                    source.at[ro, pl.ds(k, 2)], out.at[ro, pl.ds(2 * side, 2)], sems.at[2 + 4 * side + 2 * t + ro]
                )
                copy.start()
                edges.append(copy)

    def second(i, count):
        def store(ro, lanes, e):
            e1_ref[ro, pl.ds(i, count), :, lanes] = e

        d = enc_conv1(taps1_ref, h1_ref, i, count, conv1_ref, wd1_ref, store)
        d1_ref[pl.ds(i, count)] = d.reshape(count, size, 512)
        u = activate(d.astype(F32), bias_ref[1:2, :], mean2)
        for j in range(count):
            put_taps(taps2_ref, i + j, u[j * size : (j + 1) * size], 128)
        for copy in leave(i):
            copy.start()

    chunk = divisor(rows1 // 2 - 2, 6)
    steps = (rows1 // 2 - 2) // chunk

    def leave(i):
        part = pl.ds(i, chunk)
        slot = i // chunk
        return [
            pltpu.make_async_copy(e1_ref.at[0, part], e1_out.at[0, part], sem.at[slot, 0]),
            pltpu.make_async_copy(e1_ref.at[1, part], e1_out.at[1, part], sem.at[slot, 1]),
            pltpu.make_async_copy(d1_ref.at[part], d1_out.at[part], sem.at[slot, 2]),
            pltpu.make_async_copy(taps2_ref.at[part], taps2_out.at[part], sem.at[slot, 3]),
        ]

    loop(steps, lambda c: second(c * chunk, chunk))
    weights_out.wait("conv1", "conv2")
    for copy in edges:
        copy.wait()
    for c in range(steps):
        for copy in leave(c * chunk):
            copy.wait()


def encoder_own(biases, mid, top, bot, lhalo, rhalo, w1, wd1, w2, n, size):
    rows1 = lhalo.shape[0]
    inner = rows1 // 2 - 2
    vmem = pltpu.VMEM
    inside = pl.BlockSpec(memory_space=pltpu.VMEM)
    return pl.pallas_call(
        functools.partial(encoder_own_kernel, n=n, size=size),
        name="encoder_own",
        in_specs=[inside] * 9,
        out_specs=[ANYWHERE] * 7,
        out_shape=[
            jax.ShapeDtypeStruct((2, inner, size, 512), BF),
            jax.ShapeDtypeStruct((inner, size, 512), BF),
            jax.ShapeDtypeStruct((inner, size, 768), BF),
            jax.ShapeDtypeStruct((2, 4, size, 512), BF),
            jax.ShapeDtypeStruct((2, 4, size, 1024), BF),
            jax.ShapeDtypeStruct((1024, 256), BF),
            jax.ShapeDtypeStruct((1536, 256), BF),
        ],
        scratch_shapes=[
            vmem((rows1, 512), F32),
            vmem((rows1, 512), F32),
            vmem((2, rows1 // 2, size, 512), BF),
            vmem((2, rows1 // 2, size, 1024), BF),
            vmem((2, inner, size, 512), BF),
            vmem((inner, size, 512), BF),
            vmem((inner, size, 768), BF),
            vmem((1024, 256), BF),
            vmem((1536, 256), BF),
            pltpu.SemaphoreType.DMA((inner // divisor(inner, 6), 4)),
            pltpu.SemaphoreType.DMA((10,)),
        ],
    )(biases, mid, top, bot, near(lhalo), near(rhalo), w1, wd1, w2)


def encoder_kernel(
    flags, before, bias_ref, top_ref, bot_ref, wd1_ref,
    edge_h_ref, edge_taps_ref, conv1_in, conv2_in, d1_own_ref, taps2_own_ref, wd2_in, w3_in, wd3_in,
    e1_ref, e2_out, e3_out, send_ref,
    h1_ref, taps1_ref, d1_ref, taps2_ref, d2_ref, taps3_ref, d3_ref, edge_ref,
    conv1_ref, conv2_ref, wd2_ref, w3_ref, wd3_ref, e2_ref, e3_ref, sems, sems2, sems3,
    *, n, size, rows1, sent,
):
    rows2, rows3 = rows1 // 2, rows1 // 4
    inner = rows2 - 2
    fetch = Fetch(
        sems,
        **{
            f"{name}{side}{ro}": (
                source.at[ro, pl.ds(2 * side, 2)],
                target.at[ro, pl.ds(4 if side == 0 else 6, 2)],
            )
            for name, source, target in (("h", edge_h_ref, h1_ref), ("t", edge_taps_ref, taps1_ref))
            for side in range(2)
            for ro in range(2)
        },
        conv1=(conv1_in, conv1_ref),
        conv2=(conv2_in, conv2_ref),
        d1=(d1_own_ref, d1_ref.at[pl.ds(4, inner)]),
        taps2=(taps2_own_ref, taps2_ref.at[pl.ds(4, inner)]),
        wd2=(wd2_in, wd2_ref),
        w3=(w3_in, w3_ref),
        wd3=(wd3_in, wd3_ref),
    )
    mean1, mean2, mean3 = mean_matrix(64), mean_matrix(128), mean_matrix(256)

    for side, ref in ((0, top_ref), (1, bot_ref)):
        base = 6 * side
        rims = ref[8 * n :, :].astype(F32)
        x = ref[0 : 8 * n, :].astype(F32)
        left = [rims[j : j + 1] for j in range(8)]
        right = [rims[8 + j : 9 + j] for j in range(8)]
        at = base if side == 0 else base + 2
        level1(h1_ref, taps1_ref, at, full_rows(x, left, right, n, size), bias_ref[0:1, :], mean1, flags[side])

    fetch.wait("conv1", *(f"{name}{side}{ro}" for name in "ht" for side in range(2) for ro in range(2)))
    for side in range(2):

        def store(ro, lanes, e, side=side):
            keep = slice(2, 4) if side == 0 else slice(0, 2)
            e1_ref[ro, 2 * side : 2 * side + 2, :, lanes] = e[keep]

        d = enc_conv1(taps1_ref, h1_ref, 6 * side, 4, conv1_ref, wd1_ref, store)
        at = 0 if side == 0 else rows2 + 2
        d1_ref[at : at + 4] = d.reshape(4, size, 512)
        u = activate(d.astype(F32), bias_ref[1:2, :], mean2)
        for j in range(4):
            inside = j == 3 if side == 0 else j == 0
            part = u[j * size : (j + 1) * size]
            put_taps(taps2_ref, at + j, part if inside else part * flags[side], 128)

    fetch.wait("conv2", "d1", "taps2", "wd2")
    chunk2, chunk3 = divisor(rows3 + 2, 6), divisor(rows3 // 2, 4)

    def leave2(i):
        part = pl.ds(2 * i, 2 * chunk2)
        return pltpu.make_async_copy(e2_ref.at[part], e2_out.at[part], sems2.at[i // chunk2])

    def leave3(i):
        part = pl.ds(2 * i, 2 * chunk3)
        return pltpu.make_async_copy(e3_ref.at[part], e3_out.at[part], sems3.at[i // chunk3])

    def third(i, count2):
        o = 2 * i
        acc = conv(taps2_ref, o, 2 * count2, 512, conv2_ref)
        flat = 2 * count2 * size
        merged = []
        for q in range(2):
            lanes = slice(q * 256, (q + 1) * 256)
            prior = d1_ref[pl.ds(o + 1, 2 * count2), :, lanes].reshape(flat, 256).astype(F32)
            e = (prior + acc[q * flat : (q + 1) * flat]).astype(BF).reshape(2 * count2, size, 256)
            e2_ref[pl.ds(o, 2 * count2), :, lanes] = e
            for j in range(count2):
                merged.append(jnp.concatenate([e[2 * j], e[2 * j + 1]], axis=1))
        d = dotf(jnp.concatenate(merged, axis=0), wd2_ref[...]).astype(BF)
        d = jnp.concatenate([d[: flat // 2], d[flat // 2 :]], axis=1)
        d2_ref[pl.ds(i, count2)] = d.reshape(count2, size, 512)
        u = activate(d.astype(F32), bias_ref[2:3, :], mean3)
        for j in range(count2):
            put_taps(taps3_ref, i + j, u[j * size : (j + 1) * size] * row_factor(i + j, 1, rows3 + 1, flags), 256)
        leave2(i).start()

    loop((rows3 + 2) // chunk2, lambda c: third(c * chunk2, chunk2))
    fetch.wait("w3", "wd3")

    def fourth(i, count3):
        o = 2 * i
        acc = conv(taps3_ref, o, 2 * count3, 768, w3_ref)
        flat = 2 * count3 * size
        acc = jnp.concatenate([acc[:flat], acc[flat:]], axis=1)
        e = (d2_ref[pl.ds(o + 1, 2 * count3)].reshape(flat, 512).astype(F32) + acc).astype(BF)
        wide = e.astype(F32)
        for j in range(2 * count3):
            edge_ref[0, pl.ds(o + j, 1), :] = wide[j * size : j * size + 1]
            edge_ref[1, pl.ds(o + j, 1), :] = wide[j * size + n - 1 : j * size + n]
        e = e.reshape(2 * count3, size, 512)
        e3_ref[pl.ds(o, 2 * count3)] = e
        merged = [jnp.concatenate([e[2 * j], e[2 * j + 1]], axis=1) for j in range(count3)]
        d = dotf(jnp.concatenate(merged, axis=0), wd3_ref[...])
        for j in range(count3):
            d3_ref[i + j] = d[j * size : j * size + n].astype(BF)
        leave3(i).start()

    loop(rows3 // 2 // chunk3, lambda c: fourth(c * chunk3, chunk3))

    left = edge_ref[0].astype(BF)
    right = edge_ref[1].astype(BF)
    groups, each, copies = sent
    for d in range(groups):
        send_ref[d, 0:rows3, :] = jnp.where(before[0] == d, left, right)
        for e in range(each):
            row = d * each + e if copies == 1 else d // copies
            send_ref[d, rows3 + e * n : rows3 + (e + 1) * n, :] = d3_ref[row]
    for c in range((rows3 + 2) // chunk2):
        leave2(c * chunk2).wait()
    for c in range(rows3 // 2 // chunk3):
        leave3(c * chunk3).wait()


def encoder(flags, before, biases, top, bot, edge_h, edge_taps, weights, d1, taps2, n, size, rows1, sent):
    rows2, rows3 = rows1 // 2, rows1 // 4
    vmem = pltpu.VMEM
    smem = pl.BlockSpec(memory_space=pltpu.SMEM)
    inside = pl.BlockSpec(memory_space=pltpu.VMEM)
    conv1_w, wd1, conv2_w, wd2, w3, wd3 = weights
    return pl.pallas_call(
        functools.partial(encoder_kernel, n=n, size=size, rows1=rows1, sent=sent),
        name="encoder",
        in_specs=[smem] * 2 + [inside] * 4 + [ANYWHERE] * 9,
        out_specs=[inside, ANYWHERE, ANYWHERE, inside],
        out_shape=[
            jax.ShapeDtypeStruct((2, 4, size, 512), BF),
            jax.ShapeDtypeStruct((rows2 + 4, size, 512), BF),
            jax.ShapeDtypeStruct((rows3, size, 512), BF),
            jax.ShapeDtypeStruct((sent[0], rows3 + sent[1] * n, 512), BF),
        ],
        scratch_shapes=[
            vmem((2, 12, size, 512), BF),
            vmem((2, 12, size, 1024), BF),
            vmem((rows2 + 6, size, 512), BF),
            vmem((rows2 + 6, size, 768), BF),
            vmem((rows3 + 2, size, 512), BF),
            vmem((rows3 + 2, size, 1024), BF),
            vmem((rows3 // 2, n, 512), BF),
            vmem((2, rows3, 512), F32),
            vmem(conv1_w.shape, BF),
            vmem(conv2_w.shape, BF),
            vmem(wd2.shape, BF),
            vmem(w3.shape, BF),
            vmem(wd3.shape, BF),
            vmem((rows2 + 4, size, 512), BF),
            vmem((rows3, size, 512), BF),
            pltpu.SemaphoreType.DMA((15,)),
            pltpu.SemaphoreType.DMA(((rows3 + 2) // divisor(rows3 + 2, 6),)),
            pltpu.SemaphoreType.DMA((rows3 // 2 // divisor(rows3 // 2, 4),)),
        ],
    )(
        flags, before, biases, near(top), near(bot), wd1,
        edge_h, edge_taps, conv1_w, conv2_w, d1, taps2, wd2, w3, wd3,
    )


def attention_kernel(
    sides, x_ref, bias_ref, wqkv_ref, e3_in, wout_in, out_ref, full_ref, mixed_ref, a4_ref, e3_ref, wout_ref, sems,
    *, n, size, each,
):
    fetch = Fetch(sems, e3=(e3_in, e3_ref), wout=(wout_in, wout_ref))
    tail = size - n
    place = iota((tail, 512), 0)
    groups, _, width = x_ref.shape
    length = groups * n
    edge = e3_ref.shape[0]
    scale = HEAD_DIM**-0.5
    for row in range(each):
        at = edge + row * n
        x = jnp.concatenate([x_ref[g, at : at + n, :].astype(F32) for g in range(groups)], axis=0)
        mean = jnp.mean(x * x, axis=1, keepdims=True)
        u = (x * lax.rsqrt(mean + EPS) + bias_ref[3:4, :]).astype(BF)
        qkv = dotf(u, wqkv_ref[...]).astype(BF)
        left = iota((length, 128), 1) < 64
        for h in range(width // 128):
            q = qkv[:, h * 128 : (h + 1) * 128].astype(F32) * scale
            k = qkv[:, width + h * 128 : width + (h + 1) * 128]
            v = qkv[:, 2 * width + h * 128 : 2 * width + (h + 1) * 128]
            outs = []
            for side in range(2):
                mine = left if side == 0 else jnp.logical_not(left)
                qs = jnp.where(mine, q, 0.0).astype(BF)
                s = lax.dot_general(qs, k, (((1,), (1,)), ((), ())), preferred_element_type=F32)
                e = jnp.exp(s - jnp.max(s, axis=1, keepdims=True))
                total = jnp.sum(e, axis=1, keepdims=True)
                outs.append(dotf(e.astype(BF), v) / total)
            mixed_ref[:, h * 128 : (h + 1) * 128] = jnp.where(left, outs[0], outs[1]).astype(BF)
        if row == 0:
            fetch.wait("e3", "wout")
        a4_ref[...] = x + dotf(mixed_ref[...], wout_ref[...])
        for t in range(length // n):
            after = (t * n + n) % length
            before = (t * n - 1) % length
            rim = jnp.where(
                place == 0,
                a4_ref[after : after + 1, :],
                jnp.where(place == tail - 1, a4_ref[before : before + 1, :], 0.0),
            )
            out_ref[t, row] = jnp.concatenate([a4_ref[t * n : (t + 1) * n, :], rim], axis=0).astype(BF)

    lf = x_ref[sides[0], 0:edge, :].astype(F32)
    rf = x_ref[sides[1], 0:edge, :].astype(F32)
    for r in range(edge):
        rim = jnp.where(place == 0, rf[r : r + 1], jnp.where(place == tail - 1, lf[r : r + 1], 0.0))
        full_ref[r] = jnp.concatenate([e3_ref[r, 0:n, :].astype(F32), rim], axis=0).astype(BF)


def attention(sides, x, biases, e3, w_qkv, w_out, n, size, each):
    groups, _, width = x.shape
    length = groups * n
    return pl.pallas_call(
        functools.partial(attention_kernel, n=n, size=size, each=each),
        name="attention",
        in_specs=[pl.BlockSpec(memory_space=pltpu.SMEM)] + [pl.BlockSpec(memory_space=pltpu.VMEM)] * 3 + [ANYWHERE] * 2,
        out_shape=[
            jax.ShapeDtypeStruct((groups, each, size, width), BF),
            jax.ShapeDtypeStruct((e3.shape[0], size, width), BF),
        ],
        scratch_shapes=[
            pltpu.VMEM((length, width), BF),
            pltpu.VMEM((length, width), F32),
            pltpu.VMEM(e3.shape, BF),
            pltpu.VMEM(w_out.shape, BF),
            pltpu.SemaphoreType.DMA((2,)),
        ],
    )(sides, near(x), biases, w_qkv, e3, w_out)


def fill_head(out_ref, w_ref):
    chans, outs = w_ref.shape
    col = iota((outs, 512), 1)
    source = ((col >> 3) & 7) * 4 + (col & 1) * 2 + ((col >> 7) & 1)
    pick = jnp.where(source == iota((outs, 512), 0), 1.0, 0.0).astype(BF)
    wide = dotf(w_ref[...], pick)
    col = iota((chans, 512), 1)
    for o in range(2):
        for i in range(4):
            for c in range(2):
                keep = (((col >> 6) & 1) == o) & (((col & 7) >> 1) == i) & ((col >> 8) == c)
                row = o * 512 + i * 128 + c * 64
                out_ref[row : row + 64, :] = jnp.where(keep, wide, 0.0).astype(BF)


def prepare_kernel(w1_ref, w2_ref, wh_ref, conv1_ref, conv2_ref, head_ref):
    fill_conv1(conv1_ref, w1_ref)
    fill_conv2(conv2_ref, w2_ref)
    fill_head(head_ref, wh_ref)


def prepare(w1, w2, wh):
    shapes = [(1024, 256), (1536, 256), (1024, 512)]
    return pl.pallas_call(
        prepare_kernel, name="prepare", out_shape=[jax.ShapeDtypeStruct(x, BF) for x in shapes]
    )(w1, w2, wh)


def up3(a, e, put, wu_ref, bias, mean, size, factor=None):
    spread = dotf(a.reshape(-1, 512), wu_ref[...])
    for j in range(a.shape[0]):
        for ro in range(2):
            part = spread[j * size : (j + 1) * size, ro * 512 : (ro + 1) * 512]
            h = (part + e[2 * j + ro].astype(F32)).astype(BF)
            u = activate(h.astype(F32), bias, mean)
            put(2 * j + ro, h, u if factor is None else u * factor)


def conv_rows(rows, reach, w_ref):
    count, size, _ = rows[0].shape
    lhs = [
        jnp.concatenate(
            [r[:, :, q * 256 : q * 256 + reach].reshape(count * size, reach) for r in rows], axis=1
        )
        for q in range(2)
    ]
    return dotf(jnp.concatenate(lhs, axis=0), w_ref[...])


def up2(prior, acc, e, put, wu_ref, bias, mean, size):
    count = prior.shape[0]
    flat = count * size
    g = []
    for q in range(2):
        mine = prior[:, :, q * 256 : (q + 1) * 256].reshape(flat, 256).astype(F32)
        g.append((mine + acc[q * flat : (q + 1) * flat]).astype(BF))
    spread = dotf(jnp.concatenate(g, axis=0), wu_ref[...])
    for j in range(count):
        for ro in range(2):
            part = [
                spread[q * flat + j * size : q * flat + (j + 1) * size, ro * 256 : (ro + 1) * 256] for q in range(2)
            ]
            h = (jnp.concatenate(part, axis=1) + e(2 * j + ro).astype(F32)).astype(BF)
            put(2 * j + ro, h, activate(h.astype(F32), bias, mean))


def up1(prior, acc, e, put, wu_ref, bias, mean, size):
    count = prior.shape[0]
    flat = count * size
    g = []
    for q in range(2):
        mine = prior[:, :, q * 256 : (q + 1) * 256].reshape(flat, 256).astype(F32)
        both = (mine + acc[q * flat : (q + 1) * flat]).astype(BF)
        g += [both[:, :128], both[:, 128:]]
    spread = dotf(jnp.concatenate(g, axis=0), wu_ref[...])
    for j in range(count):
        for ro in range(2):
            part = [
                spread[p * flat + j * size : p * flat + (j + 1) * size, ro * 128 : (ro + 1) * 128] for p in range(4)
            ]
            h = (jnp.concatenate(part, axis=1) + e(j, ro).astype(F32)).astype(BF)
            put(j, ro, h, activate(h.astype(F32), bias, mean))


def decoder_own_kernel(
    bias_ref, a4_ref, e3_ref, wu3_ref, w3_in, wu2_in, e2_in,
    h2_out, taps2_out, edge_h_out, edge_taps_out,
    h3_ref, taps3_ref, w3_ref, wu2_ref, e2_ref, h2_ref, taps2_ref, sems, sems2,
    *, size,
):
    rows4, rows3 = a4_ref.shape[0], e3_ref.shape[0]
    fetch = Fetch(
        sems, w3=(w3_in, w3_ref), wu2=(wu2_in, wu2_ref), e2=(e2_in.at[pl.ds(4, 2 * rows3 - 4)], e2_ref)
    )
    mean2, mean3 = mean_matrix(128), mean_matrix(256)

    def third(i, count):
        def put(j, h, u):
            h3_ref[2 * i + j] = h
            put_taps(taps3_ref, 2 * i + j, u, 256)

        up3(a4_ref[pl.ds(i, count)], e3_ref[pl.ds(2 * i, 2 * count)], put, wu3_ref, bias_ref[4:5, :], mean3, size)

    loop_chunks(rows4, 4, third)

    edges = []
    for side, at in ((0, 0), (1, rows3 - 2)):
        edges.append(
            pltpu.make_async_copy(taps3_ref.at[pl.ds(at, 2)], edge_taps_out.at[pl.ds(2 * side, 2)], sems.at[3 + side])
        )
        edges.append(
            pltpu.make_async_copy(h3_ref.at[pl.ds(at + side, 1)], edge_h_out.at[pl.ds(side, 1)], sems.at[5 + side])
        )
    for copy in edges:
        copy.start()
    chunk = divisor(rows3 - 2, 7)

    def leave(o):
        part = pl.ds(2 * o, 2 * chunk)
        return [
            pltpu.make_async_copy(h2_ref.at[part], h2_out.at[part], sems2.at[o // chunk, 0]),
            pltpu.make_async_copy(taps2_ref.at[part], taps2_out.at[part], sems2.at[o // chunk, 1]),
        ]

    def second(o, count):
        def put(j, h, u):
            h2_ref[2 * o + j] = h
            put_taps(taps2_ref, 2 * o + j, u, 128)

        acc = conv(taps3_ref, o, count, 768, w3_ref)
        up2(h3_ref[pl.ds(o + 1, count)], acc, lambda j: e2_ref[2 * o + j], put, wu2_ref, bias_ref[5:6, :], mean2, size)

        for copy in leave(o):
            copy.start()

    fetch.wait("w3", "wu2", "e2")
    loop((rows3 - 2) // chunk, lambda c: second(c * chunk, chunk))
    for copy in edges:
        copy.wait()
    for c in range((rows3 - 2) // chunk):
        for copy in leave(c * chunk):
            copy.wait()


def decoder_own(biases, a4, e3, e2, wu3, w3, wu2, size):
    rows3 = e3.shape[0]
    inner = 2 * (rows3 - 2)
    out = pltpu.VMEM
    inside = pl.BlockSpec(memory_space=pltpu.VMEM)
    return pl.pallas_call(
        functools.partial(decoder_own_kernel, size=size),
        name="decoder_own",
        in_specs=[inside] * 4 + [ANYWHERE] * 3,
        out_specs=[ANYWHERE] * 4,
        out_shape=[
            jax.ShapeDtypeStruct((inner, size, 512), BF),
            jax.ShapeDtypeStruct((inner, size, 768), BF),
            jax.ShapeDtypeStruct((2, size, 512), BF),
            jax.ShapeDtypeStruct((4, size, 1024), BF),
        ],
        scratch_shapes=[
            out((rows3, size, 512), BF),
            out((rows3, size, 1024), BF),
            out(w3.shape, BF),
            out(wu2.shape, BF),
            out((2 * rows3 - 4, size, 512), BF),
            out((inner, size, 512), BF),
            out((inner, size, 768), BF),
            pltpu.SemaphoreType.DMA((7,)),
            pltpu.SemaphoreType.DMA(((rows3 - 2) // divisor(rows3 - 2, 7), 2)),
        ],
    )(biases, near(a4), e3, wu3, w3, wu2, e2)


def decoder_kernel(
    flags, factors, bias_ref, top_ref, bot_ref, edge_h_ref, edge_taps_ref, wu1_ref, wu3_ref,
    h2_own_ref, taps2_own_ref, e2_in, w3_in, wu2_in, e1_edge_in, conv2_in, e1_own_in, conv1_in, head_in, noisy_ref, noise_ref,
    out_ref,
    h3_ref, taps3_ref, h2_ref, taps2_ref, h1_ref, taps1_ref, turn_ref,
    e2_ref, w3_ref, wu2_ref, e1_edge_ref, conv2_ref, e1_own_ref, conv1_ref, head_ref, sems,
    *, n, size, rows1,
):
    rows2 = rows1 // 2
    inner = rows2 - 4
    step = pl.program_id(0)

    def prepare():
        fetch = Fetch(
            sems,
            w3=(w3_in, w3_ref),
            e2a=(e2_in.at[pl.ds(0, 4)], e2_ref.at[pl.ds(0, 4)]),
            e2b=(e2_in.at[pl.ds(rows2, 4)], e2_ref.at[pl.ds(4, 4)]),
            wu2=(wu2_in, wu2_ref),
            h2=(h2_own_ref, h2_ref.at[pl.ds(4, inner)]),
            taps2=(taps2_own_ref, taps2_ref.at[pl.ds(4, inner)]),
            conv2=(conv2_in, conv2_ref),
            e1_edge=(e1_edge_in, e1_edge_ref),
            e1_own=(e1_own_in, e1_own_ref),
            conv1=(conv1_in, conv1_ref),
            head=(head_in, head_ref),
        )
        mean1, mean2, mean3 = mean_matrix(64), mean_matrix(128), mean_matrix(256)
        bias3, bias2, bias1 = bias_ref[4:5, :], bias_ref[5:6, :], bias_ref[6:7, :]

        for side, ref in ((0, top_ref), (1, bot_ref)):
            at = 0 if side == 0 else 6

            def put3(j, h, u, at=at, side=side):
                if j == 1 - side:
                    h3_ref[3 * side] = h
                put_taps(taps3_ref, at + j, u, 256)

            up3(ref[0:1], ref[1:3], put3, wu3_ref, bias3, mean3, size, flags[side])
            own = 2 if side == 0 else 4
            taps3_ref[own : own + 2] = edge_taps_ref[2 * side : 2 * side + 2]
            h3_ref[1 + side] = edge_h_ref[side]

        rows = [jnp.concatenate([taps3_ref[a : a + 2], taps3_ref[4 + a : 6 + a]], axis=0) for a in range(3)]

        def place2(j):
            return j if j < 4 else rows2 + j - 4

        def put2(j, h, u):
            if j < 2:
                u = u * flags[0]
            if j >= 6:
                u = u * flags[1]
            h2_ref[place2(j)] = h
            put_taps(taps2_ref, place2(j), u, 128)

        fetch.wait("w3", "wu2", "e2a", "e2b")
        up2(h3_ref[...], conv_rows(rows, 768, w3_ref), lambda j: e2_ref[j], put2, wu2_ref, bias2, mean2, size)
        fetch.wait("h2", "taps2", "conv2", "e1_edge")

        rows = [jnp.concatenate([taps2_ref[a : a + 2], taps2_ref[rows2 + a : rows2 + a + 2]], axis=0) for a in range(3)]
        prior = jnp.concatenate([h2_ref[1:3], h2_ref[rows2 + 1 : rows2 + 3]], axis=0)

        def put1(j, ro, h, u):
            k = j if j < 2 else rows2 + j - 2
            if j == 0:
                u = u * flags[0]
            if j == 3:
                u = u * flags[1]
            h1_ref[ro, k] = h
            put_taps1(taps1_ref, ro, k, u)

        acc = conv_rows(rows, 512, conv2_ref)
        up1(prior, acc, lambda j, ro: e1_edge_ref[ro, j], put1, wu1_ref, bias1, mean1, size)

        def first(i, count):
            o = i + 2

            def put(j, ro, h, u):
                h1_ref[ro, o + j] = h
                put_taps1(taps1_ref, ro, o + j, u)

            acc = conv(taps2_ref, o, count, 512, conv2_ref)
            up1(h2_ref[pl.ds(o + 1, count)], acc, lambda j, ro: e1_own_ref[ro, i + j], put, wu1_ref, bias1, mean1, size)

        fetch.wait("e1_own")
        loop_chunks(rows2 - 2, 6, first)
        fetch.wait("conv1", "head")

    pl.when(step == 0)(prepare)

    i = step * 4
    acc = conv1(taps1_ref, i, 4, conv1_ref)
    flat = 4 * size
    g = []
    for p in range(4):
        halves = []
        for ro in range(2):
            prior = h1_ref[ro, pl.ds(i + 1, 4), :, p * 128 : (p + 1) * 128].reshape(flat, 128).astype(F32)
            halves.append((prior + acc[p * flat : (p + 1) * flat, ro * 128 : (ro + 1) * 128]).astype(BF))
        both = jnp.concatenate(halves, axis=1)
        g.append(jnp.concatenate([both[j * size : (j + 1) * size] for j in range(4)], axis=1))
    spread = dotf(jnp.concatenate(g, axis=0), head_ref[...])
    for p in range(4):
        for s in range(4):
            turn_ref[pl.ds(4 * p + s, n, stride=16), :] = spread[p * size : p * size + n, s * 128 : (s + 1) * 128]
    eps = turn_ref[...].T
    nvars, _, cols = noisy_ref.shape
    for o in range(2):
        part = eps[o * 64 : (o + 1) * 64].reshape(nvars, 8, cols)
        rows = slice(o * 8, (o + 1) * 8)
        out_ref[:, rows, :] = factors[0] * noisy_ref[:, rows, :] - factors[1] * part + factors[2] * noise_ref[:, rows, :]


def decoder(flags, factors, biases, top, bot, edge_h, edge_taps, e2, e1_own, e1_edge, weights, h2, taps2, noisy, step_noise, n, size):
    nvars, lat, cols = noisy.shape
    rows1 = lat // 2
    rows2 = rows1 // 2
    field = pl.BlockSpec((nvars, 16, cols), lambda k: (0, k, 0))
    smem = pl.BlockSpec(memory_space=pltpu.SMEM)
    inside = pl.BlockSpec(memory_space=pltpu.VMEM)
    vmem = pltpu.VMEM
    wu3, w3, wu2, conv2_w, wu1, conv1_w, head_w = weights
    late = [w3, wu2, e1_edge, conv2_w, e1_own, conv1_w, head_w]
    return pl.pallas_call(
        functools.partial(decoder_kernel, n=n, size=size, rows1=rows1),
        name="decoder",
        grid=(rows1 // 8,),
        in_specs=[smem, smem] + [inside] * 7 + [ANYWHERE] * 10 + [field, field],
        out_specs=field,
        out_shape=jax.ShapeDtypeStruct(noisy.shape, F32),
        scratch_shapes=[
            vmem((4, size, 512), BF),
            vmem((8, size, 1024), BF),
            vmem((rows2 + 4, size, 512), BF),
            vmem((rows2 + 4, size, 768), BF),
            vmem((2, rows2 + 2, size, 512), BF),
            vmem((2, rows2 + 2, size, 1024), BF),
            vmem((cols, 128), F32),
            vmem((8, size, 512), BF),
        ]
        + [vmem(x.shape, BF) for x in late]
        + [pltpu.SemaphoreType.DMA((11,))],
    )(
        flags, factors, biases, near(top), near(bot), edge_h, edge_taps, wu1, wu3,
        h2, taps2, e2, *late, noisy, step_noise,
    )


def shift(array, axis, by, closed):
    count = lax.axis_size(axis)
    if closed:
        pairs = [(i, (i + by) % count) for i in range(count)]
    else:
        pairs = [(i, i + by) for i in range(count) if 0 <= i + by < count]
    return lax.ppermute(array, axis, pairs)


def body(
    noisy, coarse, step_noise, timestep, w_time, w_embed, w_enc1, w_down1, w_enc2, w_down2, w_enc3, w_down3,
    w_qkv, w_attn_out, w_up3, w_dec3, w_up2, w_dec2, w_up1, w_dec1, w_head,
):
    nvars, lat, cols = noisy.shape
    n = cols // 16
    size = -(-(n + 2) // 16) * 16
    rows1 = lat // 2
    rows4 = lat // 16
    groups = lax.axis_size("lon")
    lat_at, lat_count = lax.axis_index("lat"), lax.axis_size("lat")
    flags = jnp.stack([lat_at > 0, lat_at < lat_count - 1]).astype(F32)

    wide, left, right = embed_strips(noisy, coarse, w_embed)
    rhalo = shift(left, "lon", -1, True)
    lhalo = shift(right, "lon", 1, True)
    mid = embed_middle(noisy, coarse, wide)

    temb = time_embed(timestep, w_time)
    factors = update_factors(timestep)
    widths = [w_enc1.shape[1], w_enc2.shape[1], w_enc3.shape[1], w_qkv.shape[0], w_dec3.shape[1], w_dec2.shape[1], w_dec1.shape[1]]
    starts = [sum(widths[:i]) for i in range(7)]
    biases = jnp.stack([jnp.tile(temb[s : s + w], 512 // w) for s, w in zip(starts, widths)])

    top, bot = embed_edges(noisy, coarse, wide, lhalo, rhalo)
    from_top = shift(bot, "lat", 1, False)
    from_bot = shift(top, "lat", -1, False)
    e1_own, d1, taps2, edge_h, edge_taps, conv1_w, conv2_w = encoder_own(
        biases, mid, top, bot, lhalo, rhalo, w_enc1, w_down1, w_enc2, n, size
    )

    copies = max(1, groups // rows4)
    each = max(1, rows4 // groups)
    lon_at = lax.axis_index("lon")
    sides = jnp.stack([(lon_at - 1) % groups, (lon_at + 1) % groups]).astype(jnp.int32)
    e1_edge, e2, e3, sent = encoder(
        flags, sides, biases, from_top, from_bot, edge_h, edge_taps,
        (conv1_w, w_down1, conv2_w, w_down2, w_enc3, w_down3), d1, taps2, n, size, rows1, (groups, each, copies),
    )
    got = lax.all_to_all(sent, "lon", split_axis=0, concat_axis=0, tiled=True)
    out, e3 = attention(sides, got, biases, e3, w_qkv, w_attn_out, n, size, each)
    a4 = lax.all_to_all(out.reshape(groups, each * size, 512), "lon", split_axis=0, concat_axis=0, tiled=True)
    a4 = a4.reshape(groups * each, size, 512)
    if copies > 1:
        a4 = a4.reshape(rows4, copies, size, 512)[:, 0]

    top = shift(jnp.concatenate([a4[-1:], e3[-2:]]), "lat", 1, False)
    bot = shift(jnp.concatenate([a4[:1], e3[:2]]), "lat", -1, False)
    h2, taps2, edge_h, edge_taps = decoder_own(biases, a4, e3, e2, w_up3, w_dec3, w_up2, size)
    conv1_w, conv2_w, head_w = prepare(w_dec1, w_dec2, w_head)
    return decoder(
        flags, factors, biases, top, bot, edge_h, edge_taps, e2, e1_own, e1_edge,
        (w_up3, w_dec3, w_up2, conv2_w, w_up1, conv1_w, head_w), h2, taps2, noisy, step_noise, n, size,
    )


def solution(mesh):
    field = P(None, "lat", "lon")
    return jax.shard_map(
        body, mesh=mesh, in_specs=(field, field, field) + (P(),) * 18, out_specs=field, check_vma=False
    )
```

```python
import functools
import math

import jax
import jax.numpy as jnp
from jax import lax
from jax.experimental import pallas as pl
from jax.experimental.pallas import tpu as pltpu
from jax.sharding import PartitionSpec as P

HEAD_DIM = 64
T_STEPS = 1000
BF = jnp.bfloat16
F32 = jnp.float32
EPS = 1e-06


def plan(step):
    frac = (step.astype(jnp.float32) / T_STEPS + 0.008) / 1.008
    return jnp.cos(frac * (math.pi / 2)) ** 2


def time_embed(timestep, w_time):
    half = w_time.shape[0] // 2
    freqs = jnp.exp(-math.log(10000.0) * jnp.arange(half, dtype=jnp.float32) / half)
    angle = timestep.astype(jnp.float32)[0] * freqs
    feats = jnp.concatenate([jnp.sin(angle), jnp.cos(angle)])[None]
    return jax.nn.silu(jnp.dot(feats, w_time, precision=lax.Precision.HIGHEST))[0]


def update_factors(timestep):
    current_alpha_product = plan(timestep[0])
    abar_prev = plan(timestep[0] - 1)
    beta = jnp.minimum(1.0 - current_alpha_product / abar_prev, 0.999)
    keep = 1.0 / jnp.sqrt(1.0 - beta)
    noise = beta / jnp.sqrt(1.0 - current_alpha_product) * keep
    sigma = jnp.sqrt(beta * (1.0 - abar_prev) / (1.0 - current_alpha_product))
    return jnp.stack([keep, noise, sigma])


def iota(shape, dim):
    return lax.broadcasted_iota(jnp.int32, shape, dim)


def dotf(a, b):
    return jnp.dot(a, b, preferred_element_type=F32)


def dot_tn(a, b):
    return lax.dot_general(a, b, (((0,), (0,)), ((), ())), preferred_element_type=F32)


def ends(count_of_lat):
    at = lax.axis_index("lat")
    return [jnp.where(at > 0, 1.0, 0.0), jnp.where(at < count_of_lat - 1, 1.0, 0.0)]


def mean_matrix(chans):
    size = 256
    same = (iota((size, size), 0) & -chans) == (iota((size, size), 1) & -chans)
    return jnp.where(same, 4.0 / chans, 0.0).astype(BF)


def activate(x, bias, mean):
    squares = (x * x).astype(BF)
    size = mean.shape[0]
    parts = [dotf(squares[:, i : i + size], mean) for i in range(0, x.shape[1], size)]
    half = x * lax.rsqrt(jnp.concatenate(parts, axis=1) + 4 * EPS) + bias
    return half + half * jnp.tanh(half)


def row_factor(index, low, high, flags):
    return jnp.where(index < low, flags[0], jnp.where(index >= high, flags[1], 1.0))


def put_taps1(ref, parity, k, u):
    size = u.shape[0]
    pairs = [u[:, p * 128 : (p + 1) * 128] for p in range(4)]
    first = iota((size, 128), 1) < 64
    after = pairs[1:] + [pltpu.roll(pairs[0], size - 1, 0)]
    before = [pltpu.roll(pairs[3], 1, 0)] + pairs[:3]
    for p in range(4):
        ref[parity, k, 2 * p] = pairs[p].astype(BF)
        ref[parity, k, 2 * p + 1] = jnp.where(first, after[p], before[p]).astype(BF)


def put_taps(ref, k, u, chans):
    size, lanes = u.shape
    parts = [u[:, i : i + 128] for i in range(0, lanes, 128)]
    edge = chans // 128
    around = (
        [pltpu.roll(x, 1, 0) for x in parts[-edge:]] + parts + [pltpu.roll(x, size - 1, 0) for x in parts[:edge]]
    )
    for i, part in enumerate(around):
        ref[k, i] = part.astype(BF)


def lanes_of(rows, first, last):
    count, _, size, _ = rows.shape
    return [rows[:, b].reshape(count * size, 128) for b in range(first, last)]


def fill_conv1(out_ref, w_ref):
    chans = w_ref.shape[0]
    twice = jnp.where((iota((chans, 128), 1) & 63) == iota((chans, 128), 0), 1.0, 0.0).astype(BF)
    wide = dot_tn(w_ref[...], twice)
    left = iota((chans, 128), 1) < 64
    zero = jnp.zeros((chans, 128), F32)
    for t in range(4):
        for ro in range(2):
            a = t - ro
            for j, dx in enumerate((0, 1, 2, -1)):
                halves = []
                for co in range(2):
                    b = dx - co + 1
                    good = 0 <= a < 3 and 0 <= b < 3
                    halves.append(wide[(a * 3 + b) * chans : (a * 3 + b + 1) * chans] if good else zero)
                value = jnp.where(left, halves[0], halves[1]).astype(BF)
                row = t * 256 + j * 64
                out_ref[row : row + 64, ro * 128 : (ro + 1) * 128] = value


def fill_conv2(out_ref, w_ref):
    zero = jnp.zeros((128, 128), BF)
    for a in range(3):
        part = w_ref[a * 384 : (a + 1) * 384, :]
        out_ref[a * 512 : a * 512 + 384, 0:128] = part
        out_ref[a * 512 + 384 : (a + 1) * 512, 0:128] = zero
        out_ref[a * 512 : a * 512 + 128, 128:256] = zero
        out_ref[a * 512 + 128 : (a + 1) * 512, 128:256] = part


def conv1(taps_ref, i, count, w_ref):
    rows = [
        taps_ref[1, pl.ds(i, count)],
        taps_ref[0, pl.ds(i + 1, count)],
        taps_ref[1, pl.ds(i + 1, count)],
        taps_ref[0, pl.ds(i + 2, count)],
    ]
    lhs = [jnp.concatenate([x for r in rows for x in lanes_of(r, 2 * p, 2 * p + 2)], axis=1) for p in range(4)]
    return dotf(jnp.concatenate(lhs, axis=0), w_ref[...])


def conv_rows(rows, reach, w_ref):
    lhs = [
        jnp.concatenate([x for r in rows for x in lanes_of(r, 2 * q, 2 * q + reach // 128)], axis=1) for q in range(2)
    ]
    return dotf(jnp.concatenate(lhs, axis=0), w_ref[...])


def conv(taps_ref, o, count, reach, w_ref):
    return conv_rows([taps_ref[pl.ds(o + a, count)] for a in range(3)], reach, w_ref)


def loop(count, body):
    def step(i, carry):
        body(i)
        return carry

    lax.fori_loop(0, count, step, 0)


def divisor(total, most):
    return max(d for d in range(1, most + 1) if total % d == 0)


def loop_chunks(total, chunk, body):
    chunk = min(chunk, total)
    steps = -(-total // chunk)
    loop(steps, lambda c: body(jnp.minimum(c * chunk, total - chunk), chunk))


def fill_embed(out_ref, w_ref):
    feats, chans = w_ref.shape
    twice = jnp.where((iota((chans, 128), 1) & 63) == iota((chans, 128), 0), 1.0, 0.0).astype(BF)
    wide = dotf(w_ref[...], twice).astype(BF)
    k = iota((512, feats), 0)
    source = ((k >> 3) & 15) * 4 + (k & 1) * 2 + ((k >> 7) & 1)
    pick = jnp.where(source == iota((512, feats), 1), 1.0, 0.0).astype(BF)
    wide = dotf(pick, wide)
    k = iota((512, 128), 0)
    right = iota((512, 128), 1) >= 64
    same_cell = right == ((k >> 8) == 1)
    for i in range(4):
        keep = same_cell & (((k & 7) >> 1) == i)
        out_ref[:, i * 128 : (i + 1) * 128] = jnp.where(keep, wide, 0.0).astype(BF)


def embed_rows(noisy_ref, coarse_ref, w_ref, turn_ref):
    cols = noisy_ref.shape[2]
    n = cols // 16
    out = []
    for o in range(2):
        block = jnp.concatenate(
            [noisy_ref[:, o * 8 : (o + 1) * 8, :].reshape(64, cols), coarse_ref[:, o * 8 : (o + 1) * 8, :].reshape(64, cols)],
            axis=0,
        )
        turn_ref[o] = block.T
        lhs = [
            jnp.concatenate([turn_ref[o, pl.ds(4 * p + s, n, stride=16), :] for s in range(4)], axis=1)
            for p in range(4)
        ]
        res = dotf(jnp.concatenate(lhs, axis=0).astype(BF), w_ref[...])
        for i in range(4):
            out.append(
                jnp.concatenate([res[p * n : (p + 1) * n, i * 128 : (i + 1) * 128] for p in range(4)], axis=1)
            )
    return out


def strips_kernel(w_ref, nl_ref, cl_ref, nr_ref, cr_ref, wide_ref, left_ref, right_ref, turn_ref, strip_ref):
    fill_embed(wide_ref, w_ref)
    octets = nl_ref.shape[1] // 8
    first = iota((64, 128), 1) < 64
    for o in range(octets):
        rows = slice(o * 8, (o + 1) * 8)
        block = jnp.concatenate(
            [
                jnp.where(first, a[:, rows, :].reshape(64, 128), b[:, rows, :].reshape(64, 128))
                for a, b in ((nl_ref, nr_ref), (cl_ref, cr_ref))
            ],
            axis=0,
        ).T
        turn_ref[0, o * 16 : (o + 1) * 16, :] = block[:16]
        turn_ref[1, o * 16 : (o + 1) * 16, :] = block[112:]
    lhs = [
        jnp.concatenate([turn_ref[side, pl.ds(4 * p + s, octets, stride=16), :] for s in range(4)], axis=1)
        for side in range(2)
        for p in range(4)
    ]
    res = dotf(jnp.concatenate(lhs, axis=0).astype(BF), wide_ref[...])
    for side, out_ref in ((0, left_ref), (1, right_ref)):
        for p in range(4):
            at = (side * 4 + p) * octets
            for i in range(4):
                strip_ref[p, pl.ds(i, octets, stride=4), :] = res[at : at + octets, i * 128 : (i + 1) * 128]
        for p in range(4):
            out_ref[:, p * 128 : (p + 1) * 128] = strip_ref[p].astype(BF)


def embed_mid_kernel(wide_ref, noisy_ref, coarse_ref, mid_ref, turn_ref):
    mid_ref[...] = jnp.concatenate(embed_rows(noisy_ref, coarse_ref, wide_ref, turn_ref), axis=0).astype(BF)


def embed_edge_kernel(wide_ref, left_ref, right_ref, noisy_ref, coarse_ref, top_ref, bot_ref, turn_ref):
    rows = embed_rows(noisy_ref, coarse_ref, wide_ref, turn_ref)
    n = rows[0].shape[0]
    count = left_ref.shape[0]
    for k, ref in ((0, top_ref), (1, bot_ref)):

        @pl.when(pl.program_id(0) == k)
        def _(k=k, ref=ref):
            ref[0 : 8 * n, :] = jnp.concatenate(rows, axis=0).astype(BF)
            at = slice(0, 16) if k == 0 else slice(count - 16, count)
            pick = slice(0, 8) if k == 0 else slice(8, 16)
            rims = [r[at, :].astype(F32)[pick] for r in (left_ref, right_ref)]
            ref[8 * n :, :] = jnp.concatenate(rims, axis=0).astype(BF)


def near(array):
    return pltpu.with_memory_space_constraint(array, pltpu.VMEM)


ANYWHERE = pl.BlockSpec(memory_space=pl.ANY)


class Fetch:
    def __init__(self, sems, **pairs):
        self.copies = {name: pltpu.make_async_copy(src, dst, sems.at[i]) for i, (name, (src, dst)) in enumerate(pairs.items())}
        for copy in self.copies.values():
            copy.start()

    def wait(self, *names):
        for name in names:
            self.copies[name].wait()


def whole(shape):
    return pl.BlockSpec(shape, lambda *_: (0,) * len(shape))


def embed_strips(noisy, coarse, w_embed):
    nvars, rows, cols = noisy.shape
    sides = [pl.BlockSpec((nvars, rows, 128), lambda k: (0, 0, 0)), pl.BlockSpec((nvars, rows, 128), lambda k: (0, 0, cols // 128 - 1))]
    strip = jax.ShapeDtypeStruct((rows // 2, 512), BF)
    return pl.pallas_call(
        strips_kernel,
        name="embed_strips",
        grid=(1,),
        in_specs=[whole(w_embed.shape), sides[0], sides[0], sides[1], sides[1]],
        out_specs=[whole((512, 512)), whole(strip.shape), whole(strip.shape)],
        out_shape=[jax.ShapeDtypeStruct((512, 512), BF), strip, strip],
        scratch_shapes=[pltpu.VMEM((2, rows * 2, 128), F32), pltpu.VMEM((4, rows // 2, 128), F32)],
    )(w_embed, noisy, coarse, noisy, coarse)


def embed_edges(noisy, coarse, wide, left, right):
    nvars, rows, cols = noisy.shape
    n = cols // 16
    last = rows // 16 - 1
    field = pl.BlockSpec((nvars, 16, cols), lambda k: (0, k * last, 0))
    pay = jax.ShapeDtypeStruct((8 * n + 16, 512), BF)
    return pl.pallas_call(
        embed_edge_kernel,
        name="embed_edges",
        grid=(2,),
        in_specs=[whole(wide.shape), whole(left.shape), whole(right.shape), field, field],
        out_specs=[whole(pay.shape)] * 2,
        out_shape=[pay, pay],
        scratch_shapes=[pltpu.VMEM((2, cols, 128), F32)],
    )(wide, near(left), near(right), noisy, coarse)


def embed_middle(noisy, coarse, wide):
    nvars, rows, cols = noisy.shape
    n = cols // 16
    steps = rows // 16 - 2
    field = pl.BlockSpec((nvars, 16, cols), lambda k: (0, k + 1, 0))
    return pl.pallas_call(
        embed_mid_kernel,
        name="embed_middle",
        grid=(steps,),
        in_specs=[whole(wide.shape), field, field],
        out_specs=pl.BlockSpec((8 * n, 512), lambda k: (k, 0)),
        out_shape=jax.ShapeDtypeStruct((8 * steps * n, 512), BF),
        scratch_shapes=[pltpu.VMEM((2, cols, 128), F32)],
    )(wide, noisy, coarse)


def full_rows(x, left, right, n, size):
    tail = size - n
    place = iota((tail, 512), 0)
    full = []
    for j in range(x.shape[0] // n):
        rim = jnp.where(place == 0, right[j], jnp.where(place == tail - 1, left[j], 0.0))
        full += [x[j * n : (j + 1) * n], rim]
    return jnp.concatenate(full, axis=0)


def level1(h_ref, taps_ref, k, h, bias, mean, factor=None):
    size = h_ref.shape[2]
    u = activate(h, bias, mean)
    for j in range(h.shape[0] // size):
        part = u[j * size : (j + 1) * size]
        h_ref[j % 2, k + j // 2] = h[j * size : (j + 1) * size].astype(BF)
        put_taps1(taps_ref, j % 2, k + j // 2, part if factor is None else part * factor)


def enc_conv1(taps_ref, h_ref, i, count, conv_ref, wd_ref, store):
    size = taps_ref.shape[3]
    acc = conv1(taps_ref, i, count, conv_ref)
    flat = count * size
    merged = []
    for p in range(4):
        halves = []
        for ro in range(2):
            lanes = slice(p * 128, (p + 1) * 128)
            prior = h_ref[ro, pl.ds(i + 1, count), :, lanes].reshape(flat, 128).astype(F32)
            e = (prior + acc[p * flat : (p + 1) * flat, ro * 128 : (ro + 1) * 128]).astype(BF)
            store(ro, lanes, e.reshape(count, size, 128))
            halves.append(e)
        merged.append(jnp.concatenate(halves, axis=1))
    d = dotf(jnp.concatenate(merged, axis=0), wd_ref[...]).astype(BF)
    return jnp.concatenate([d[p * flat : (p + 1) * flat] for p in range(4)], axis=1)


def encoder_own_kernel(
    bias_ref, mid_ref, top_ref, bot_ref, lhalo_ref, rhalo_ref, w1_ref, wd1_ref, w2_ref,
    e1_out, d1_out, taps2_out, edge_h_out, edge_taps_out, conv1_out, conv2_out,
    lf_ref, rf_ref, h1_ref, taps1_ref, e1_ref, d1_ref, taps2_ref, conv1_ref, conv2_ref, sem, sems,
    *, n, size,
):
    fill_conv1(conv1_ref, w1_ref)
    fill_conv2(conv2_ref, w2_ref)
    weights_out = Fetch(sems, conv1=(conv1_ref, conv1_out), conv2=(conv2_ref, conv2_out))
    lf_ref[...] = lhalo_ref[...].astype(F32)
    rf_ref[...] = rhalo_ref[...].astype(F32)
    mean1, mean2 = mean_matrix(64), mean_matrix(128)
    rows1 = lhalo_ref.shape[0]

    def first(x, row):
        left = [lf_ref[pl.ds(row + j, 1), :] for j in range(4)]
        right = [rf_ref[pl.ds(row + j, 1), :] for j in range(4)]
        k = row // 2
        level1(h1_ref, taps1_ref, k, full_rows(x.astype(F32), left, right, n, size), bias_ref[0:1, :], mean1)

    def first_at(row):
        if row < 8:
            first(top_ref[row * n : (row + 4) * n, :], row)
        elif row < rows1 - 8:
            first(mid_ref[(row - 8) * n : (row - 4) * n, :], row)
        else:
            at = row - rows1 + 8
            first(bot_ref[at * n : (at + 4) * n, :], row)

    def second(i, count):
        def store(ro, lanes, e):
            e1_ref[ro, pl.ds(i, count), :, lanes] = e

        d = enc_conv1(taps1_ref, h1_ref, i, count, conv1_ref, wd1_ref, store)
        d1_ref[pl.ds(i, count)] = d.reshape(count, size, 512)
        u = activate(d.astype(F32), bias_ref[1:2, :], mean2)
        for j in range(count):
            put_taps(taps2_ref, i + j, u[j * size : (j + 1) * size], 128)
        for copy in leave(i):
            copy.start()

    chunk = divisor(rows1 // 2 - 2, 6)
    steps = (rows1 // 2 - 2) // chunk

    def leave(i):
        part = pl.ds(i, chunk)
        slot = i // chunk
        return [
            pltpu.make_async_copy(e1_ref.at[0, part], e1_out.at[0, part], sem.at[slot, 0]),
            pltpu.make_async_copy(e1_ref.at[1, part], e1_out.at[1, part], sem.at[slot, 1]),
            pltpu.make_async_copy(d1_ref.at[part], d1_out.at[part], sem.at[slot, 2]),
            pltpu.make_async_copy(taps2_ref.at[part], taps2_out.at[part], sem.at[slot, 3]),
        ]

    done = 0
    for c in range(steps + 1):
        need = rows1 if c == steps else min(rows1, -(-(2 * chunk * (c + 1) + 3) // 4) * 4)
        while done < need:
            first_at(done)
            done += 4
        if c:
            second((c - 1) * chunk, chunk)
    edges = []
    for side, k in ((0, 0), (1, rows1 // 2 - 2)):
        for t, (source, out) in enumerate(((h1_ref, edge_h_out), (taps1_ref, edge_taps_out))):
            for ro in range(2):
                copy = pltpu.make_async_copy(
                    source.at[ro, pl.ds(k, 2)], out.at[ro, pl.ds(2 * side, 2)], sems.at[2 + 4 * side + 2 * t + ro]
                )
                copy.start()
                edges.append(copy)
    weights_out.wait("conv1", "conv2")
    for copy in edges:
        copy.wait()
    for c in range(steps):
        for copy in leave(c * chunk):
            copy.wait()


def encoder_own(biases, mid, top, bot, lhalo, rhalo, w1, wd1, w2, n, size):
    rows1 = lhalo.shape[0]
    inner = rows1 // 2 - 2
    vmem = pltpu.VMEM
    inside = pl.BlockSpec(memory_space=pltpu.VMEM)
    return pl.pallas_call(
        functools.partial(encoder_own_kernel, n=n, size=size),
        name="encoder_own",
        in_specs=[inside] * 9,
        out_specs=[ANYWHERE] * 7,
        out_shape=[
            jax.ShapeDtypeStruct((2, inner, size, 512), BF),
            jax.ShapeDtypeStruct((inner, size, 512), BF),
            jax.ShapeDtypeStruct((inner, 6, size, 128), BF),
            jax.ShapeDtypeStruct((2, 4, size, 512), BF),
            jax.ShapeDtypeStruct((2, 4, 8, size, 128), BF),
            jax.ShapeDtypeStruct((1024, 256), BF),
            jax.ShapeDtypeStruct((1536, 256), BF),
        ],
        scratch_shapes=[
            vmem((rows1, 512), F32),
            vmem((rows1, 512), F32),
            vmem((2, rows1 // 2, size, 512), BF),
            vmem((2, rows1 // 2, 8, size, 128), BF),
            vmem((2, inner, size, 512), BF),
            vmem((inner, size, 512), BF),
            vmem((inner, 6, size, 128), BF),
            vmem((1024, 256), BF),
            vmem((1536, 256), BF),
            pltpu.SemaphoreType.DMA((inner // divisor(inner, 6), 4)),
            pltpu.SemaphoreType.DMA((10,)),
        ],
    )(biases, mid, top, bot, near(lhalo), near(rhalo), w1.T, wd1, w2)


def encoder_kernel(
    bias_ref, top_ref, bot_ref, wd1_ref,
    edge_h_ref, edge_taps_ref, conv1_in, conv2_in, d1_own_ref, taps2_own_ref, wd2_in, w3_in, wd3_in,
    e1_ref, e2_out, e3_out, send_ref,
    h1_ref, taps1_ref, d1_ref, taps2_ref, d2_ref, taps3_ref, d3_ref, edge_ref,
    conv1_ref, conv2_ref, wd2_ref, w3_ref, wd3_ref, e2_ref, e3_ref, sems, sems2, sems3,
    *, n, size, rows1, sent, lat,
):
    flags = ends(lat)
    rows2, rows3 = rows1 // 2, rows1 // 4
    inner = rows2 - 2
    fetch = Fetch(
        sems,
        **{
            f"{name}{side}{ro}": (
                source.at[ro, pl.ds(2 * side, 2)],
                target.at[ro, pl.ds(4 if side == 0 else 6, 2)],
            )
            for name, source, target in (("h", edge_h_ref, h1_ref), ("t", edge_taps_ref, taps1_ref))
            for side in range(2)
            for ro in range(2)
        },
        conv1=(conv1_in, conv1_ref),
        conv2=(conv2_in, conv2_ref),
        d1=(d1_own_ref, d1_ref.at[pl.ds(4, inner)]),
        taps2=(taps2_own_ref, taps2_ref.at[pl.ds(4, inner)]),
        wd2=(wd2_in, wd2_ref),
        w3=(w3_in, w3_ref),
        wd3=(wd3_in, wd3_ref),
    )
    mean1, mean2, mean3 = mean_matrix(64), mean_matrix(128), mean_matrix(256)

    for side, ref in ((0, top_ref), (1, bot_ref)):
        base = 6 * side
        rims = ref[8 * n :, :].astype(F32)
        x = ref[0 : 8 * n, :].astype(F32)
        left = [rims[j : j + 1] for j in range(8)]
        right = [rims[8 + j : 9 + j] for j in range(8)]
        at = base if side == 0 else base + 2
        level1(h1_ref, taps1_ref, at, full_rows(x, left, right, n, size), bias_ref[0:1, :], mean1, flags[side])

    fetch.wait("conv1", *(f"{name}{side}{ro}" for name in "ht" for side in range(2) for ro in range(2)))
    for side in range(2):

        def store(ro, lanes, e, side=side):
            keep = slice(2, 4) if side == 0 else slice(0, 2)
            e1_ref[ro, 2 * side : 2 * side + 2, :, lanes] = e[keep]

        d = enc_conv1(taps1_ref, h1_ref, 6 * side, 4, conv1_ref, wd1_ref, store)
        at = 0 if side == 0 else rows2 + 2
        d1_ref[at : at + 4] = d.reshape(4, size, 512)
        u = activate(d.astype(F32), bias_ref[1:2, :], mean2)
        for j in range(4):
            inside = j == 3 if side == 0 else j == 0
            part = u[j * size : (j + 1) * size]
            put_taps(taps2_ref, at + j, part if inside else part * flags[side], 128)

    fetch.wait("conv2", "d1", "taps2", "wd2")
    chunk2, chunk3 = divisor(rows3 + 2, 6), divisor(rows3 // 2, 4)

    def leave2(i):
        part = pl.ds(2 * i, 2 * chunk2)
        return pltpu.make_async_copy(e2_ref.at[part], e2_out.at[part], sems2.at[i // chunk2])

    def leave3(i):
        part = pl.ds(2 * i, 2 * chunk3)
        return pltpu.make_async_copy(e3_ref.at[part], e3_out.at[part], sems3.at[i // chunk3])

    def third(i, count2):
        o = 2 * i
        acc = conv(taps2_ref, o, 2 * count2, 512, conv2_ref)
        flat = 2 * count2 * size
        merged = []
        for q in range(2):
            lanes = slice(q * 256, (q + 1) * 256)
            prior = d1_ref[pl.ds(o + 1, 2 * count2), :, lanes].reshape(flat, 256).astype(F32)
            e = (prior + acc[q * flat : (q + 1) * flat]).astype(BF).reshape(2 * count2, size, 256)
            e2_ref[pl.ds(o, 2 * count2), :, lanes] = e
            for j in range(count2):
                merged.append(jnp.concatenate([e[2 * j], e[2 * j + 1]], axis=1))
        d = dotf(jnp.concatenate(merged, axis=0), wd2_ref[...]).astype(BF)
        d = jnp.concatenate([d[: flat // 2], d[flat // 2 :]], axis=1)
        d2_ref[pl.ds(i, count2)] = d.reshape(count2, size, 512)
        u = activate(d.astype(F32), bias_ref[2:3, :], mean3)
        for j in range(count2):
            put_taps(taps3_ref, i + j, u[j * size : (j + 1) * size] * row_factor(i + j, 1, rows3 + 1, flags), 256)
        leave2(i).start()

    loop((rows3 + 2) // chunk2, lambda c: third(c * chunk2, chunk2))
    fetch.wait("w3", "wd3")

    def fourth(i, count3):
        o = 2 * i
        acc = conv(taps3_ref, o, 2 * count3, 768, w3_ref)
        flat = 2 * count3 * size
        acc = jnp.concatenate([acc[:flat], acc[flat:]], axis=1)
        e = (d2_ref[pl.ds(o + 1, 2 * count3)].reshape(flat, 512).astype(F32) + acc).astype(BF)
        wide = e.astype(F32)
        for j in range(2 * count3):
            edge_ref[0, pl.ds(o + j, 1), :] = wide[j * size : j * size + 1]
            edge_ref[1, pl.ds(o + j, 1), :] = wide[j * size + n - 1 : j * size + n]
        e = e.reshape(2 * count3, size, 512)
        e3_ref[pl.ds(o, 2 * count3)] = e
        merged = [jnp.concatenate([e[2 * j], e[2 * j + 1]], axis=1) for j in range(count3)]
        d = dotf(jnp.concatenate(merged, axis=0), wd3_ref[...])
        for j in range(count3):
            d3_ref[i + j] = d[j * size : j * size + n].astype(BF)
        leave3(i).start()

    loop(rows3 // 2 // chunk3, lambda c: fourth(c * chunk3, chunk3))

    left = edge_ref[0].astype(BF)
    right = edge_ref[1].astype(BF)
    groups, each, copies = sent
    before = lax.rem(lax.axis_index("lon") + groups - 1, groups)
    for d in range(groups):
        send_ref[d, 0:rows3, :] = jnp.where(before == d, left, right)
        for e in range(each):
            row = d * each + e if copies == 1 else d // copies
            send_ref[d, rows3 + e * n : rows3 + (e + 1) * n, :] = d3_ref[row]
    for c in range((rows3 + 2) // chunk2):
        leave2(c * chunk2).wait()
    for c in range(rows3 // 2 // chunk3):
        leave3(c * chunk3).wait()


def encoder(lat_count, biases, top, bot, edge_h, edge_taps, weights, d1, taps2, n, size, rows1, sent):
    rows2, rows3 = rows1 // 2, rows1 // 4
    vmem = pltpu.VMEM
    inside = pl.BlockSpec(memory_space=pltpu.VMEM)
    conv1_w, wd1, conv2_w, wd2, w3, wd3 = weights
    return pl.pallas_call(
        functools.partial(encoder_kernel, n=n, size=size, rows1=rows1, sent=sent, lat=lat_count),
        name="encoder",
        in_specs=[inside] * 4 + [ANYWHERE] * 9,
        out_specs=[inside, ANYWHERE, ANYWHERE, inside],
        out_shape=[
            jax.ShapeDtypeStruct((2, 4, size, 512), BF),
            jax.ShapeDtypeStruct((rows2 + 4, size, 512), BF),
            jax.ShapeDtypeStruct((rows3, size, 512), BF),
            jax.ShapeDtypeStruct((sent[0], rows3 + sent[1] * n, 512), BF),
        ],
        scratch_shapes=[
            vmem((2, 12, size, 512), BF),
            vmem((2, 12, 8, size, 128), BF),
            vmem((rows2 + 6, size, 512), BF),
            vmem((rows2 + 6, 6, size, 128), BF),
            vmem((rows3 + 2, size, 512), BF),
            vmem((rows3 + 2, 8, size, 128), BF),
            vmem((rows3 // 2, n, 512), BF),
            vmem((2, rows3, 512), F32),
            vmem(conv1_w.shape, BF),
            vmem(conv2_w.shape, BF),
            vmem(wd2.shape, BF),
            vmem(w3.shape, BF),
            vmem(wd3.shape, BF),
            vmem((rows2 + 4, size, 512), BF),
            vmem((rows3, size, 512), BF),
            pltpu.SemaphoreType.DMA((15,)),
            pltpu.SemaphoreType.DMA(((rows3 + 2) // divisor(rows3 + 2, 6),)),
            pltpu.SemaphoreType.DMA((rows3 // 2 // divisor(rows3 // 2, 4),)),
        ],
    )(
        biases, near(top), near(bot), wd1,
        edge_h, edge_taps, conv1_w, conv2_w, d1, taps2, wd2, w3, wd3,
    )


def attention_kernel(
    x_ref, bias_ref, wqkv_ref, e3_in, wout_in, out_ref, full_ref, mixed_ref, a4_ref, e3_ref, wout_ref, sems,
    *, n, size, each,
):
    fetch = Fetch(sems, e3=(e3_in, e3_ref), wout=(wout_in, wout_ref))
    tail = size - n
    place = iota((tail, 512), 0)
    groups, _, width = x_ref.shape
    length = groups * n
    edge = e3_ref.shape[0]
    scale = HEAD_DIM**-0.5
    for row in range(each):
        at = edge + row * n
        x = jnp.concatenate([x_ref[g, at : at + n, :].astype(F32) for g in range(groups)], axis=0)
        mean = jnp.mean(x * x, axis=1, keepdims=True)
        u = (x * lax.rsqrt(mean + EPS) + bias_ref[3:4, :]).astype(BF)
        qkv = dotf(u, wqkv_ref[...]).astype(BF)
        left = iota((length, 128), 1) < 64
        for h in range(width // 128):
            q = qkv[:, h * 128 : (h + 1) * 128].astype(F32) * scale
            k = qkv[:, width + h * 128 : width + (h + 1) * 128]
            v = qkv[:, 2 * width + h * 128 : 2 * width + (h + 1) * 128]
            outs = []
            for side in range(2):
                mine = left if side == 0 else jnp.logical_not(left)
                qs = jnp.where(mine, q, 0.0).astype(BF)
                s = lax.dot_general(qs, k, (((1,), (1,)), ((), ())), preferred_element_type=F32)
                e = jnp.exp(s - jnp.max(s, axis=1, keepdims=True))
                total = jnp.sum(e, axis=1, keepdims=True)
                outs.append(dotf(e.astype(BF), v) / total)
            mixed_ref[:, h * 128 : (h + 1) * 128] = jnp.where(left, outs[0], outs[1]).astype(BF)
        if row == 0:
            fetch.wait("e3", "wout")
        a4_ref[...] = x + dotf(mixed_ref[...], wout_ref[...])
        for t in range(length // n):
            after = (t * n + n) % length
            before = (t * n - 1) % length
            rim = jnp.where(
                place == 0,
                a4_ref[after : after + 1, :],
                jnp.where(place == tail - 1, a4_ref[before : before + 1, :], 0.0),
            )
            out_ref[t, row] = jnp.concatenate([a4_ref[t * n : (t + 1) * n, :], rim], axis=0).astype(BF)

    here = lax.axis_index("lon")
    lf = x_ref[lax.rem(here + groups - 1, groups), 0:edge, :].astype(F32)
    rf = x_ref[lax.rem(here + 1, groups), 0:edge, :].astype(F32)
    for r in range(edge):
        rim = jnp.where(place == 0, rf[r : r + 1], jnp.where(place == tail - 1, lf[r : r + 1], 0.0))
        full_ref[r] = jnp.concatenate([e3_ref[r, 0:n, :].astype(F32), rim], axis=0).astype(BF)


def attention(x, biases, e3, w_qkv, w_out, n, size, each):
    groups, _, width = x.shape
    length = groups * n
    return pl.pallas_call(
        functools.partial(attention_kernel, n=n, size=size, each=each),
        name="attention",
        in_specs=[pl.BlockSpec(memory_space=pltpu.VMEM)] * 3 + [ANYWHERE] * 2,
        out_shape=[
            jax.ShapeDtypeStruct((groups, each, size, width), BF),
            jax.ShapeDtypeStruct((e3.shape[0], size, width), BF),
        ],
        scratch_shapes=[
            pltpu.VMEM((length, width), BF),
            pltpu.VMEM((length, width), F32),
            pltpu.VMEM(e3.shape, BF),
            pltpu.VMEM(w_out.shape, BF),
            pltpu.SemaphoreType.DMA((2,)),
        ],
    )(near(x), biases, w_qkv, e3, w_out)


def fill_head(out_ref, w_ref):
    outs, chans = w_ref.shape
    col = iota((outs, 512), 1)
    source = ((col >> 3) & 7) * 4 + (col & 1) * 2 + ((col >> 7) & 1)
    pick = jnp.where(source == iota((outs, 512), 0), 1.0, 0.0).astype(BF)
    wide = dot_tn(w_ref[...], pick)
    col = iota((chans, 512), 1)
    for o in range(2):
        for i in range(4):
            for c in range(2):
                keep = (((col >> 6) & 1) == o) & (((col & 7) >> 1) == i) & ((col >> 8) == c)
                row = o * 512 + i * 128 + c * 64
                out_ref[row : row + 64, :] = jnp.where(keep, wide, 0.0).astype(BF)


def up3(a, e, put, wu_ref, bias, mean, size, factor=None):
    spread = dotf(a.reshape(-1, 512), wu_ref[...])
    for j in range(a.shape[0]):
        for ro in range(2):
            part = spread[j * size : (j + 1) * size, ro * 512 : (ro + 1) * 512]
            h = (part + e[2 * j + ro].astype(F32)).astype(BF)
            u = activate(h.astype(F32), bias, mean)
            put(2 * j + ro, h, u if factor is None else u * factor)


def up2(prior, acc, e, put, wu_ref, bias, mean, size):
    count = prior.shape[0]
    flat = count * size
    g = []
    for q in range(2):
        mine = prior[:, :, q * 256 : (q + 1) * 256].reshape(flat, 256).astype(F32)
        g.append((mine + acc[q * flat : (q + 1) * flat]).astype(BF))
    spread = dotf(jnp.concatenate(g, axis=0), wu_ref[...])
    for j in range(count):
        for ro in range(2):
            part = [
                spread[q * flat + j * size : q * flat + (j + 1) * size, ro * 256 : (ro + 1) * 256] for q in range(2)
            ]
            h = (jnp.concatenate(part, axis=1) + e(2 * j + ro).astype(F32)).astype(BF)
            put(2 * j + ro, h, activate(h.astype(F32), bias, mean))


def up1(prior, acc, e, put, wu_ref, size):
    count = prior.shape[0]
    flat = count * size
    g = []
    for q in range(2):
        mine = prior[:, :, q * 256 : (q + 1) * 256].reshape(flat, 256).astype(F32)
        both = (mine + acc[q * flat : (q + 1) * flat]).astype(BF)
        g += [both[:, :128], both[:, 128:]]
    spread = dotf(jnp.concatenate(g, axis=0), wu_ref[...])
    for j in range(count):
        for ro in range(2):
            part = [
                spread[p * flat + j * size : p * flat + (j + 1) * size, ro * 128 : (ro + 1) * 128] for p in range(4)
            ]
            h = (jnp.concatenate(part, axis=1) + e(j, ro).astype(F32)).astype(BF)
            put(j, ro, h)


def decoder_own_kernel(
    bias_ref, a4_ref, e3_ref, wu3_ref, w3_in, wu2_in, e2_in,
    h2_out, taps2_out, edge_h_out, edge_taps_out,
    h3_ref, taps3_ref, w3_ref, wu2_ref, e2_ref, h2_ref, taps2_ref, sems, sems2,
    *, size,
):
    rows4, rows3 = a4_ref.shape[0], e3_ref.shape[0]
    fetch = Fetch(
        sems, w3=(w3_in, w3_ref), wu2=(wu2_in, wu2_ref), e2=(e2_in.at[pl.ds(4, 2 * rows3 - 4)], e2_ref)
    )
    mean2, mean3 = mean_matrix(128), mean_matrix(256)

    def third(i, count):
        def put(j, h, u):
            h3_ref[2 * i + j] = h
            put_taps(taps3_ref, 2 * i + j, u, 256)

        up3(a4_ref[pl.ds(i, count)], e3_ref[pl.ds(2 * i, 2 * count)], put, wu3_ref, bias_ref[4:5, :], mean3, size)

    loop_chunks(rows4, 4, third)

    edges = []
    for side, at in ((0, 0), (1, rows3 - 2)):
        edges.append(
            pltpu.make_async_copy(taps3_ref.at[pl.ds(at, 2)], edge_taps_out.at[pl.ds(2 * side, 2)], sems.at[3 + side])
        )
        edges.append(
            pltpu.make_async_copy(h3_ref.at[pl.ds(at + side, 1)], edge_h_out.at[pl.ds(side, 1)], sems.at[5 + side])
        )
    for copy in edges:
        copy.start()
    chunk = divisor(rows3 - 2, 7)

    def leave(o):
        part = pl.ds(2 * o, 2 * chunk)
        return [
            pltpu.make_async_copy(h2_ref.at[part], h2_out.at[part], sems2.at[o // chunk, 0]),
            pltpu.make_async_copy(taps2_ref.at[part], taps2_out.at[part], sems2.at[o // chunk, 1]),
        ]

    def second(o, count):
        def put(j, h, u):
            h2_ref[2 * o + j] = h
            put_taps(taps2_ref, 2 * o + j, u, 128)

        acc = conv(taps3_ref, o, count, 768, w3_ref)
        up2(h3_ref[pl.ds(o + 1, count)], acc, lambda j: e2_ref[2 * o + j], put, wu2_ref, bias_ref[5:6, :], mean2, size)

        for copy in leave(o):
            copy.start()

    fetch.wait("w3", "wu2", "e2")
    loop((rows3 - 2) // chunk, lambda c: second(c * chunk, chunk))
    for copy in edges:
        copy.wait()
    for c in range((rows3 - 2) // chunk):
        for copy in leave(c * chunk):
            copy.wait()


def decoder_own(biases, a4, e3, e2, wu3, w3, wu2, size):
    rows3 = e3.shape[0]
    inner = 2 * (rows3 - 2)
    out = pltpu.VMEM
    inside = pl.BlockSpec(memory_space=pltpu.VMEM)
    return pl.pallas_call(
        functools.partial(decoder_own_kernel, size=size),
        name="decoder_own",
        in_specs=[inside] * 4 + [ANYWHERE] * 3,
        out_specs=[ANYWHERE] * 4,
        out_shape=[
            jax.ShapeDtypeStruct((inner, size, 512), BF),
            jax.ShapeDtypeStruct((inner, 6, size, 128), BF),
            jax.ShapeDtypeStruct((2, size, 512), BF),
            jax.ShapeDtypeStruct((4, 8, size, 128), BF),
        ],
        scratch_shapes=[
            out((rows3, size, 512), BF),
            out((rows3, 8, size, 128), BF),
            out(w3.shape, BF),
            out(wu2.shape, BF),
            out((2 * rows3 - 4, size, 512), BF),
            out((inner, size, 512), BF),
            out((inner, 6, size, 128), BF),
            pltpu.SemaphoreType.DMA((7,)),
            pltpu.SemaphoreType.DMA(((rows3 - 2) // divisor(rows3 - 2, 7), 2)),
        ],
    )(biases, near(a4), e3, wu3, w3, wu2, e2)


def decoder_kernel(
    factors, bias_ref, top_ref, bot_ref, edge_h_ref, edge_taps_ref, wu1_ref, wu3_ref, w2_ref, w1_ref, wh_ref,
    h2_own_ref, taps2_own_ref, e2_in, w3_in, wu2_in, e1_edge_in, e1_own_in, noisy_ref, noise_ref,
    out_ref,
    h3_ref, taps3_ref, h2_ref, taps2_ref, h1_ref, taps1_ref, turn_ref,
    e2_ref, w3_ref, wu2_ref, e1_edge_ref, e1_own_ref, conv2_ref, conv1_ref, head_ref, g_ref, sems,
    *, n, size, rows1, lat,
):
    rows2 = rows1 // 2
    inner = rows2 - 4
    step = pl.program_id(0)
    last = pl.num_programs(0) - 2

    def prepare():
        fetch = Fetch(
            sems,
            w3=(w3_in, w3_ref),
            e2a=(e2_in.at[pl.ds(0, 4)], e2_ref.at[pl.ds(0, 4)]),
            e2b=(e2_in.at[pl.ds(rows2, 4)], e2_ref.at[pl.ds(4, 4)]),
            wu2=(wu2_in, wu2_ref),
            h2=(h2_own_ref, h2_ref.at[pl.ds(4, inner)]),
            taps2=(taps2_own_ref, taps2_ref.at[pl.ds(4, inner)]),
            e1_edge=(e1_edge_in, e1_edge_ref),
            e1_own=(e1_own_in, e1_own_ref),
        )
        flags = ends(lat)
        fill_conv1(conv1_ref, w1_ref)
        fill_conv2(conv2_ref, w2_ref)
        fill_head(head_ref, wh_ref)
        mean1, mean2, mean3 = mean_matrix(64), mean_matrix(128), mean_matrix(256)
        bias3, bias2, bias1 = bias_ref[4:5, :], bias_ref[5:6, :], bias_ref[6:7, :]

        for side, ref in ((0, top_ref), (1, bot_ref)):
            at = 0 if side == 0 else 6

            def put3(j, h, u, at=at, side=side):
                if j == 1 - side:
                    h3_ref[3 * side] = h
                put_taps(taps3_ref, at + j, u, 256)

            up3(ref[0:1], ref[1:3], put3, wu3_ref, bias3, mean3, size, flags[side])
            own = 2 if side == 0 else 4
            taps3_ref[own : own + 2] = edge_taps_ref[2 * side : 2 * side + 2]
            h3_ref[1 + side] = edge_h_ref[side]

        rows = [jnp.concatenate([taps3_ref[a : a + 2], taps3_ref[4 + a : 6 + a]], axis=0) for a in range(3)]

        def place2(j):
            return j if j < 4 else rows2 + j - 4

        def put2(j, h, u):
            if j < 2:
                u = u * flags[0]
            if j >= 6:
                u = u * flags[1]
            h2_ref[place2(j)] = h
            put_taps(taps2_ref, place2(j), u, 128)

        fetch.wait("w3", "wu2", "e2a", "e2b")
        up2(h3_ref[...], conv_rows(rows, 768, w3_ref), lambda j: e2_ref[j], put2, wu2_ref, bias2, mean2, size)
        fetch.wait("h2", "taps2", "e1_edge")

        rows = [jnp.concatenate([taps2_ref[a : a + 2], taps2_ref[rows2 + a : rows2 + a + 2]], axis=0) for a in range(3)]
        prior = jnp.concatenate([h2_ref[1:3], h2_ref[rows2 + 1 : rows2 + 3]], axis=0)

        def lay(ro, k, factor=None):
            u = activate(h1_ref[ro, k].astype(F32), bias1, mean1)
            put_taps1(taps1_ref, ro, k, u if factor is None else u * factor)

        def put1(j, ro, h):
            h1_ref[ro, j if j < 2 else rows2 + j - 2] = h

        acc = conv_rows(rows, 512, conv2_ref)
        up1(prior, acc, lambda j, ro: e1_edge_ref[ro, j], put1, wu1_ref, size)

        def first(i, count):
            def put(j, ro, h):
                h1_ref[ro, i + 2 + j] = h

            acc = conv(taps2_ref, i + 2, count, 512, conv2_ref)
            up1(h2_ref[pl.ds(i + 3, count)], acc, lambda j, ro: e1_own_ref[ro, i + j], put, wu1_ref, size)

        def behind(i, count):
            for j in range(count):
                for ro in range(2):
                    lay(ro, i + 2 + j)

        chunk = divisor(rows2 - 2, 6)
        steps = (rows2 - 2) // chunk
        fetch.wait("e1_own")
        for ro in range(2):
            lay(ro, 0, flags[0])
            lay(ro, 1)
            lay(ro, rows2)
            lay(ro, rows2 + 1, flags[1])
        first(0, chunk)

        def both(c):
            behind((c - 1) * chunk, chunk)
            first(c * chunk, chunk)

        loop(steps - 1, lambda c: both(c + 1))
        behind((steps - 1) * chunk, chunk)

    pl.when(step == 0)(prepare)

    spread = dotf(g_ref[...], head_ref[...])
    for p in range(4):
        for s in range(4):
            turn_ref[pl.ds(4 * p + s, n, stride=16), :] = spread[p * size : p * size + n, s * 128 : (s + 1) * 128]
    eps = turn_ref[...].T
    nvars, _, cols = noisy_ref.shape
    for o in range(2):
        part = eps[o * 64 : (o + 1) * 64].reshape(nvars, 8, cols)
        rows = slice(o * 8, (o + 1) * 8)
        out_ref[:, rows, :] = factors[0] * noisy_ref[:, rows, :] - factors[1] * part + factors[2] * noise_ref[:, rows, :]

    i = jnp.minimum(step, last) * 4
    acc = conv1(taps1_ref, i, 4, conv1_ref)
    flat = 4 * size
    for p in range(4):
        halves = []
        for ro in range(2):
            prior = h1_ref[ro, pl.ds(i + 1, 4), :, p * 128 : (p + 1) * 128].reshape(flat, 128).astype(F32)
            halves.append((prior + acc[p * flat : (p + 1) * flat, ro * 128 : (ro + 1) * 128]).astype(BF))
        both = jnp.concatenate(halves, axis=1)
        for j in range(4):
            g_ref[p * size : (p + 1) * size, j * 256 : (j + 1) * 256] = both[j * size : (j + 1) * size]


def decoder(lat_count, factors, biases, top, bot, edge_h, edge_taps, e2, e1_own, e1_edge, weights, h2, taps2, noisy, step_noise, n, size):
    nvars, lat, cols = noisy.shape
    rows1 = lat // 2
    rows2 = rows1 // 2
    field = pl.BlockSpec((nvars, 16, cols), lambda k: (0, jnp.maximum(k - 1, 0), 0))
    smem = pl.BlockSpec(memory_space=pltpu.SMEM)
    inside = pl.BlockSpec(memory_space=pltpu.VMEM)
    vmem = pltpu.VMEM
    wu3, w3, wu2, w2, wu1, w1, wh = weights
    late = [w3, wu2, e1_edge, e1_own]
    return pl.pallas_call(
        functools.partial(decoder_kernel, n=n, size=size, rows1=rows1, lat=lat_count),
        name="decoder",
        grid=(rows1 // 8 + 1,),
        in_specs=[smem] + [inside] * 10 + [ANYWHERE] * 7 + [field, field],
        out_specs=field,
        out_shape=jax.ShapeDtypeStruct(noisy.shape, F32),
        scratch_shapes=[
            vmem((4, size, 512), BF),
            vmem((8, 8, size, 128), BF),
            vmem((rows2 + 4, size, 512), BF),
            vmem((rows2 + 4, 6, size, 128), BF),
            vmem((2, rows2 + 2, size, 512), BF),
            vmem((2, rows2 + 2, 8, size, 128), BF),
            vmem((cols, 128), F32),
            vmem((8, size, 512), BF),
        ]
        + [vmem(x.shape, BF) for x in late]
        + [vmem((1536, 256), BF), vmem((1024, 256), BF), vmem((1024, 512), BF), vmem((4 * size, 1024), BF)]
        + [pltpu.SemaphoreType.DMA((8,))],
    )(
        factors, biases, near(top), near(bot), edge_h, edge_taps, wu1, wu3, w2, w1.T, wh.T,
        h2, taps2, e2, *late, noisy, step_noise,
    )


def shift(array, axis, by, closed):
    count = lax.axis_size(axis)
    if closed:
        pairs = [(i, (i + by) % count) for i in range(count)]
    else:
        pairs = [(i, i + by) for i in range(count) if 0 <= i + by < count]
    return lax.ppermute(array, axis, pairs)


def body(
    noisy, coarse, step_noise, timestep, w_time, w_embed, w_enc1, w_down1, w_enc2, w_down2, w_enc3, w_down3,
    w_qkv, w_attn_out, w_up3, w_dec3, w_up2, w_dec2, w_up1, w_dec1, w_head,
):
    nvars, lat, cols = noisy.shape
    n = cols // 16
    size = -(-(n + 2) // 16) * 16
    rows1 = lat // 2
    rows4 = lat // 16
    groups = lax.axis_size("lon")
    lat_count = lax.axis_size("lat")

    wide, left, right = embed_strips(noisy, coarse, w_embed)
    rhalo = shift(left, "lon", -1, True)
    lhalo = shift(right, "lon", 1, True)
    mid = embed_middle(noisy, coarse, wide)

    temb = time_embed(timestep, w_time)
    factors = update_factors(timestep)
    widths = [w_enc1.shape[1], w_enc2.shape[1], w_enc3.shape[1], w_qkv.shape[0], w_dec3.shape[1], w_dec2.shape[1], w_dec1.shape[1]]
    starts = [sum(widths[:i]) for i in range(7)]
    biases = jnp.stack(
        [jnp.tile(temb[s : s + w], 512 // w) * (1.0 if i == 3 else 0.5) for i, (s, w) in enumerate(zip(starts, widths))]
    )

    top, bot = embed_edges(noisy, coarse, wide, lhalo, rhalo)
    from_top = shift(bot, "lat", 1, False)
    from_bot = shift(top, "lat", -1, False)
    e1_own, d1, taps2, edge_h, edge_taps, conv1_w, conv2_w = encoder_own(
        biases, mid, top, bot, lhalo, rhalo, w_enc1, w_down1, w_enc2, n, size
    )

    copies = max(1, groups // rows4)
    each = max(1, rows4 // groups)
    e1_edge, e2, e3, sent = encoder(
        lat_count, biases, from_top, from_bot, edge_h, edge_taps,
        (conv1_w, w_down1, conv2_w, w_down2, w_enc3, w_down3), d1, taps2, n, size, rows1, (groups, each, copies),
    )
    got = lax.all_to_all(sent, "lon", split_axis=0, concat_axis=0, tiled=True)
    out, e3 = attention(got, biases, e3, w_qkv, w_attn_out, n, size, each)
    a4 = lax.all_to_all(out.reshape(groups, each * size, 512), "lon", split_axis=0, concat_axis=0, tiled=True)
    a4 = a4.reshape(groups * each, size, 512)
    if copies > 1:
        a4 = a4.reshape(rows4, copies, size, 512)[:, 0]

    top = shift(jnp.concatenate([a4[-1:], e3[-2:]]), "lat", 1, False)
    bot = shift(jnp.concatenate([a4[:1], e3[:2]]), "lat", -1, False)
    h2, taps2, edge_h, edge_taps = decoder_own(biases, a4, e3, e2, w_up3, w_dec3, w_up2, size)
    return decoder(
        lat_count, factors, biases, top, bot, edge_h, edge_taps, e2, e1_own, e1_edge,
        (w_up3, w_dec3, w_up2, w_dec2, w_up1, w_dec1, w_head), h2, taps2, noisy, step_noise, n, size,
    )


def solution(mesh):
    field = P(None, "lat", "lon")
    return jax.shard_map(
        body, mesh=mesh, in_specs=(field, field, field) + (P(),) * 18, out_specs=field, check_vma=False
    )
```

```python
import functools
import math

import jax
import jax.numpy as jnp
from jax import lax
from jax.experimental import pallas as pl
from jax.experimental.pallas import tpu as pltpu
from jax.sharding import PartitionSpec as P

HEAD_DIM = 64
T_STEPS = 1000
BF = jnp.bfloat16
F32 = jnp.float32
EPS = 1e-06


def plan(step):
    frac = (step.astype(jnp.float32) / T_STEPS + 0.008) / 1.008
    return jnp.cos(frac * (math.pi / 2)) ** 2


def time_embed(timestep, w_time):
    half = w_time.shape[0] // 2
    freqs = jnp.exp(-math.log(10000.0) * jnp.arange(half, dtype=jnp.float32) / half)
    angle = timestep.astype(jnp.float32)[0] * freqs
    feats = jnp.concatenate([jnp.sin(angle), jnp.cos(angle)])[None]
    return jax.nn.silu(jnp.dot(feats, w_time, precision=lax.Precision.HIGHEST))[0]


def update_factors(timestep):
    current_alpha_product = plan(timestep[0])
    abar_prev = plan(timestep[0] - 1)
    beta = jnp.minimum(1.0 - current_alpha_product / abar_prev, 0.999)
    keep = 1.0 / jnp.sqrt(1.0 - beta)
    noise = beta / jnp.sqrt(1.0 - current_alpha_product) * keep
    sigma = jnp.sqrt(beta * (1.0 - abar_prev) / (1.0 - current_alpha_product))
    return jnp.stack([keep, noise, sigma])


def iota(shape, dim):
    return lax.broadcasted_iota(jnp.int32, shape, dim)


def dotf(a, b):
    return jnp.dot(a, b, preferred_element_type=F32)


def dot_tn(a, b):
    return lax.dot_general(a, b, (((0,), (0,)), ((), ())), preferred_element_type=F32)


def ends(count_of_lat):
    at = lax.axis_index("lat")
    return [jnp.where(at > 0, 1.0, 0.0), jnp.where(at < count_of_lat - 1, 1.0, 0.0)]


def mean_matrix(chans):
    size = 256
    same = (iota((size, size), 0) & -chans) == (iota((size, size), 1) & -chans)
    return jnp.where(same, 4.0 / chans, 0.0).astype(BF)


def activate(x, bias, mean):
    squares = (x * x).astype(BF)
    size = mean.shape[0]
    parts = [dotf(squares[:, i : i + size], mean) for i in range(0, x.shape[1], size)]
    half = x * lax.rsqrt(jnp.concatenate(parts, axis=1) + 4 * EPS) + bias
    return half + half * jnp.tanh(half)


def row_factor(index, low, high, flags):
    return jnp.where(index < low, flags[0], jnp.where(index >= high, flags[1], 1.0))


def put_taps1(ref, parity, k, u):
    size = u.shape[0]
    pairs = [u[:, p * 128 : (p + 1) * 128] for p in range(4)]
    first = iota((size, 128), 1) < 64
    after = pairs[1:] + [pltpu.roll(pairs[0], size - 1, 0)]
    before = [pltpu.roll(pairs[3], 1, 0)] + pairs[:3]
    for p in range(4):
        ref[parity, k, 2 * p] = pairs[p].astype(BF)
        ref[parity, k, 2 * p + 1] = jnp.where(first, after[p], before[p]).astype(BF)


def put_taps(ref, k, u, chans):
    size, lanes = u.shape
    parts = [u[:, i : i + 128] for i in range(0, lanes, 128)]
    edge = chans // 128
    around = (
        [pltpu.roll(x, 1, 0) for x in parts[-edge:]] + parts + [pltpu.roll(x, size - 1, 0) for x in parts[:edge]]
    )
    for i, part in enumerate(around):
        ref[k, i] = part.astype(BF)


def lanes_of(rows, first, last):
    count, _, size, _ = rows.shape
    return [rows[:, b].reshape(count * size, 128) for b in range(first, last)]


def fill_conv1(out_ref, w_ref):
    chans = w_ref.shape[0]
    twice = jnp.where((iota((chans, 128), 1) & 63) == iota((chans, 128), 0), 1.0, 0.0).astype(BF)
    wide = dot_tn(w_ref[...], twice)
    left = iota((chans, 128), 1) < 64
    zero = jnp.zeros((chans, 128), F32)
    for t in range(4):
        for ro in range(2):
            a = t - ro
            for j, dx in enumerate((0, 1, 2, -1)):
                halves = []
                for co in range(2):
                    b = dx - co + 1
                    good = 0 <= a < 3 and 0 <= b < 3
                    halves.append(wide[(a * 3 + b) * chans : (a * 3 + b + 1) * chans] if good else zero)
                value = jnp.where(left, halves[0], halves[1]).astype(BF)
                row = t * 256 + j * 64
                out_ref[row : row + 64, ro * 128 : (ro + 1) * 128] = value


def fill_conv2(out_ref, w_ref):
    zero = jnp.zeros((128, 128), BF)
    for a in range(3):
        part = w_ref[a * 384 : (a + 1) * 384, :]
        out_ref[a * 512 : a * 512 + 384, 0:128] = part
        out_ref[a * 512 + 384 : (a + 1) * 512, 0:128] = zero
        out_ref[a * 512 : a * 512 + 128, 128:256] = zero
        out_ref[a * 512 + 128 : (a + 1) * 512, 128:256] = part


def conv1(taps_ref, i, count, w_ref):
    rows = [
        taps_ref[1, pl.ds(i, count)],
        taps_ref[0, pl.ds(i + 1, count)],
        taps_ref[1, pl.ds(i + 1, count)],
        taps_ref[0, pl.ds(i + 2, count)],
    ]
    lhs = [jnp.concatenate([x for r in rows for x in lanes_of(r, 2 * p, 2 * p + 2)], axis=1) for p in range(4)]
    return dotf(jnp.concatenate(lhs, axis=0), w_ref[...])


def conv_rows(rows, reach, w_ref):
    lhs = [
        jnp.concatenate([x for r in rows for x in lanes_of(r, 2 * q, 2 * q + reach // 128)], axis=1) for q in range(2)
    ]
    return dotf(jnp.concatenate(lhs, axis=0), w_ref[...])


def conv(taps_ref, o, count, reach, w_ref):
    return conv_rows([taps_ref[pl.ds(o + a, count)] for a in range(3)], reach, w_ref)


def loop(count, body):
    def step(i, carry):
        body(i)
        return carry

    lax.fori_loop(0, count, step, 0)


def divisor(total, most):
    return max(d for d in range(1, most + 1) if total % d == 0)


def loop_chunks(total, chunk, body):
    chunk = min(chunk, total)
    steps = -(-total // chunk)
    loop(steps, lambda c: body(jnp.minimum(c * chunk, total - chunk), chunk))


def fill_embed(out_ref, w_ref):
    feats, chans = w_ref.shape
    twice = jnp.where((iota((chans, 128), 1) & 63) == iota((chans, 128), 0), 1.0, 0.0).astype(BF)
    wide = dotf(w_ref[...], twice).astype(BF)
    k = iota((512, feats), 0)
    source = ((k >> 3) & 15) * 4 + (k & 1) * 2 + ((k >> 7) & 1)
    pick = jnp.where(source == iota((512, feats), 1), 1.0, 0.0).astype(BF)
    wide = dotf(pick, wide)
    k = iota((512, 128), 0)
    right = iota((512, 128), 1) >= 64
    same_cell = right == ((k >> 8) == 1)
    for i in range(4):
        keep = same_cell & (((k & 7) >> 1) == i)
        out_ref[:, i * 128 : (i + 1) * 128] = jnp.where(keep, wide, 0.0).astype(BF)


def embed_rows(fields, w_ref, turn_ref, slot):
    n = fields[0].shape[1] // 16
    turn_ref[slot] = jnp.concatenate(fields, axis=0).T
    lhs = [
        jnp.concatenate([turn_ref[slot, pl.ds(4 * p + s, n, stride=16), :] for s in range(4)], axis=1)
        for p in range(4)
    ]
    res = dotf(jnp.concatenate(lhs, axis=0).astype(BF), w_ref[...])
    return [
        jnp.concatenate([res[p * n : (p + 1) * n, i * 128 : (i + 1) * 128] for p in range(4)], axis=1)
        for i in range(4)
    ]


def strips_kernel(w_ref, nl_ref, cl_ref, nr_ref, cr_ref, wide_ref, left_ref, right_ref, turn_ref, strip_ref):
    fill_embed(wide_ref, w_ref)
    octets = nl_ref.shape[1] // 8
    first = iota((64, 128), 1) < 64
    for o in range(octets):
        rows = slice(o * 8, (o + 1) * 8)
        block = jnp.concatenate(
            [
                jnp.where(first, a[:, rows, :].reshape(64, 128), b[:, rows, :].reshape(64, 128))
                for a, b in ((nl_ref, nr_ref), (cl_ref, cr_ref))
            ],
            axis=0,
        ).T
        turn_ref[0, o * 16 : (o + 1) * 16, :] = block[:16]
        turn_ref[1, o * 16 : (o + 1) * 16, :] = block[112:]
    lhs = [
        jnp.concatenate([turn_ref[side, pl.ds(4 * p + s, octets, stride=16), :] for s in range(4)], axis=1)
        for side in range(2)
        for p in range(4)
    ]
    res = dotf(jnp.concatenate(lhs, axis=0).astype(BF), wide_ref[...])
    for side, out_ref in ((0, left_ref), (1, right_ref)):
        for p in range(4):
            at = (side * 4 + p) * octets
            for i in range(4):
                strip_ref[p, pl.ds(i, octets, stride=4), :] = res[at : at + octets, i * 128 : (i + 1) * 128]
        for p in range(4):
            out_ref[:, p * 128 : (p + 1) * 128] = strip_ref[p].astype(BF)


def embed_kernel(wide_ref, noisy_in, coarse_in, top_out, mid_out, bot_out, x_ref, turn_ref, e0_ref, sems, out_sems):
    _, nvars, rows, cols = x_ref.shape
    n = cols // 16
    chunks = rows // 16

    def reads(c):
        part = pl.ds(pl.multiple_of(16 * c, 16), 16)
        return [
            pltpu.make_async_copy(source.at[:, part, :], x_ref.at[t, :, part, :], sems.at[c, t])
            for t, source in enumerate((noisy_in, coarse_in))
        ]

    def write(c, out, place):
        part = pl.ds(pl.multiple_of(c * 8 * n, 8 * n), 8 * n)
        to = pl.ds(pl.multiple_of(place * 8 * n, 8 * n), 8 * n)
        return pltpu.make_async_copy(e0_ref.at[part], out.at[to], out_sems.at[c])

    def writes(c):
        return write(c, top_out, 0) if c == 0 else write(c, bot_out, 0) if c == chunks - 1 else write(c, mid_out, c - 1)

    for c in range(chunks):
        for copy in reads(c):
            copy.start()

    def chunk(c):
        for copy in reads(c):
            copy.wait()
        out = []
        for o in range(2):
            at = pl.ds(pl.multiple_of(16 * c + 8 * o, 8), 8)
            fields = [x_ref[t, :, at, :].reshape(8 * nvars, cols) for t in range(2)]
            out += embed_rows(fields, wide_ref, turn_ref, o)
        e0_ref[pl.ds(pl.multiple_of(c * 8 * n, 8 * n), 8 * n), :] = jnp.concatenate(out, axis=0).astype(BF)

        @pl.when((c > 0) & (c < chunks - 1))
        def _():
            write(c, mid_out, c - 1).start()

    loop(chunks, chunk)
    for c in (0, chunks - 1):
        writes(c).start()
    for c in range(chunks):
        writes(c).wait()


def rims_kernel(left_ref, right_ref, top_in, bot_in, top_out, bot_out, rim_ref, sems):
    count = left_ref.shape[0]
    at = top_out.shape[0] - 16
    copies = []
    for k, out in ((0, top_out), (1, bot_out)):
        rows = slice(0, 16) if k == 0 else slice(count - 16, count)
        pick = slice(0, 8) if k == 0 else slice(8, 16)
        rim_ref[k] = jnp.concatenate([r[rows, :].astype(F32)[pick] for r in (left_ref, right_ref)], axis=0).astype(BF)
        copies.append(pltpu.make_async_copy(rim_ref.at[k], out.at[pl.ds(at, 16)], sems.at[k]))
        copies[-1].start()
    for copy in copies:
        copy.wait()


def near(array):
    return pltpu.with_memory_space_constraint(array, pltpu.VMEM)


ANYWHERE = pl.BlockSpec(memory_space=pl.ANY)


class Fetch:
    def __init__(self, sems, **pairs):
        self.copies = {name: pltpu.make_async_copy(src, dst, sems.at[i]) for i, (name, (src, dst)) in enumerate(pairs.items())}
        for copy in self.copies.values():
            copy.start()

    def wait(self, *names):
        for name in names:
            self.copies[name].wait()


def whole(shape):
    return pl.BlockSpec(shape, lambda *_: (0,) * len(shape))


def embed_strips(noisy, coarse, w_embed):
    nvars, rows, cols = noisy.shape
    sides = [pl.BlockSpec((nvars, rows, 128), lambda k: (0, 0, 0)), pl.BlockSpec((nvars, rows, 128), lambda k: (0, 0, cols // 128 - 1))]
    strip = jax.ShapeDtypeStruct((rows // 2, 512), BF)
    return pl.pallas_call(
        strips_kernel,
        name="embed_strips",
        grid=(1,),
        in_specs=[whole(w_embed.shape), sides[0], sides[0], sides[1], sides[1]],
        out_specs=[whole((512, 512)), whole(strip.shape), whole(strip.shape)],
        out_shape=[jax.ShapeDtypeStruct((512, 512), BF), strip, strip],
        scratch_shapes=[pltpu.VMEM((2, rows * 2, 128), F32), pltpu.VMEM((4, rows // 2, 128), F32)],
    )(w_embed, noisy, coarse, noisy, coarse)


def embed(noisy, coarse, wide):
    nvars, rows, cols = noisy.shape
    n = cols // 16
    pay = jax.ShapeDtypeStruct((8 * n + 16, 512), BF)
    return pl.pallas_call(
        embed_kernel,
        name="embed",
        in_specs=[pl.BlockSpec(memory_space=pltpu.VMEM), ANYWHERE, ANYWHERE],
        out_specs=[ANYWHERE] * 3,
        out_shape=[pay, jax.ShapeDtypeStruct(((rows // 2 - 16) * n, 512), BF), pay],
        scratch_shapes=[
            pltpu.VMEM((2, nvars, rows, cols), F32),
            pltpu.VMEM((2, cols, 128), F32),
            pltpu.VMEM((rows // 2 * n, 512), BF),
            pltpu.SemaphoreType.DMA((rows // 16, 2)),
            pltpu.SemaphoreType.DMA((rows // 16,)),
        ],
    )(wide, noisy, coarse)


def add_rims(left, right, top, bot):
    inside = pl.BlockSpec(memory_space=pltpu.VMEM)
    return pl.pallas_call(
        rims_kernel,
        name="rims",
        in_specs=[inside, inside, ANYWHERE, ANYWHERE],
        out_specs=[ANYWHERE] * 2,
        out_shape=[jax.ShapeDtypeStruct(top.shape, BF)] * 2,
        scratch_shapes=[pltpu.VMEM((2, 16, 512), BF), pltpu.SemaphoreType.DMA((2,))],
        input_output_aliases={2: 0, 3: 1},
    )(near(left), near(right), top, bot)


def full_rows(x, left, right, n, size):
    tail = size - n
    place = iota((tail, 512), 0)
    full = []
    for j in range(x.shape[0] // n):
        rim = jnp.where(place == 0, right[j], jnp.where(place == tail - 1, left[j], 0.0))
        full += [x[j * n : (j + 1) * n], rim]
    return jnp.concatenate(full, axis=0)


def level1(h_ref, taps_ref, k, h, bias, mean, factor=None):
    size = h_ref.shape[2]
    u = activate(h, bias, mean)
    for j in range(h.shape[0] // size):
        part = u[j * size : (j + 1) * size]
        h_ref[j % 2, k + j // 2] = h[j * size : (j + 1) * size].astype(BF)
        put_taps1(taps_ref, j % 2, k + j // 2, part if factor is None else part * factor)


def enc_conv1(taps_ref, h_ref, i, count, conv_ref, wd_ref, store):
    size = taps_ref.shape[3]
    acc = conv1(taps_ref, i, count, conv_ref)
    flat = count * size
    merged = []
    for p in range(4):
        halves = []
        for ro in range(2):
            lanes = slice(p * 128, (p + 1) * 128)
            prior = h_ref[ro, pl.ds(i + 1, count), :, lanes].reshape(flat, 128).astype(F32)
            e = (prior + acc[p * flat : (p + 1) * flat, ro * 128 : (ro + 1) * 128]).astype(BF)
            store(ro, lanes, e.reshape(count, size, 128))
            halves.append(e)
        merged.append(jnp.concatenate(halves, axis=1))
    d = dotf(jnp.concatenate(merged, axis=0), wd_ref[...]).astype(BF)
    return jnp.concatenate([d[p * flat : (p + 1) * flat] for p in range(4)], axis=1)


def encoder_own_kernel(
    bias_ref, mid_ref, top_ref, bot_ref, lhalo_ref, rhalo_ref, w1_ref, wd1_ref, w2_ref,
    e1_out, d1_out, taps2_out, edge_h_out, edge_taps_out, conv1_out, conv2_out,
    lf_ref, rf_ref, h1_ref, taps1_ref, e1_ref, d1_ref, taps2_ref, conv1_ref, conv2_ref, sem, sems,
    *, n, size,
):
    fill_conv1(conv1_ref, w1_ref)
    fill_conv2(conv2_ref, w2_ref)
    weights_out = Fetch(sems, conv1=(conv1_ref, conv1_out), conv2=(conv2_ref, conv2_out))
    lf_ref[...] = lhalo_ref[...].astype(F32)
    rf_ref[...] = rhalo_ref[...].astype(F32)
    mean1, mean2 = mean_matrix(64), mean_matrix(128)
    rows1 = lhalo_ref.shape[0]

    def first(x, row):
        left = [lf_ref[pl.ds(row + j, 1), :] for j in range(4)]
        right = [rf_ref[pl.ds(row + j, 1), :] for j in range(4)]
        k = row // 2
        level1(h1_ref, taps1_ref, k, full_rows(x.astype(F32), left, right, n, size), bias_ref[0:1, :], mean1)

    def first_at(row):
        if row < 8:
            first(top_ref[row * n : (row + 4) * n, :], row)
        elif row < rows1 - 8:
            first(mid_ref[(row - 8) * n : (row - 4) * n, :], row)
        else:
            at = row - rows1 + 8
            first(bot_ref[at * n : (at + 4) * n, :], row)

    def second(i, count):
        def store(ro, lanes, e):
            e1_ref[ro, pl.ds(i, count), :, lanes] = e

        d = enc_conv1(taps1_ref, h1_ref, i, count, conv1_ref, wd1_ref, store)
        d1_ref[pl.ds(i, count)] = d.reshape(count, size, 512)
        u = activate(d.astype(F32), bias_ref[1:2, :], mean2)
        for j in range(count):
            put_taps(taps2_ref, i + j, u[j * size : (j + 1) * size], 128)
        for copy in leave(i):
            copy.start()

    chunk = divisor(rows1 // 2 - 2, 6)
    steps = (rows1 // 2 - 2) // chunk

    def leave(i):
        part = pl.ds(i, chunk)
        slot = i // chunk
        return [
            pltpu.make_async_copy(e1_ref.at[0, part], e1_out.at[0, part], sem.at[slot, 0]),
            pltpu.make_async_copy(e1_ref.at[1, part], e1_out.at[1, part], sem.at[slot, 1]),
            pltpu.make_async_copy(d1_ref.at[part], d1_out.at[part], sem.at[slot, 2]),
            pltpu.make_async_copy(taps2_ref.at[part], taps2_out.at[part], sem.at[slot, 3]),
        ]

    done = 0
    for c in range(steps + 1):
        need = rows1 if c == steps else min(rows1, -(-(2 * chunk * (c + 1) + 3) // 4) * 4)
        while done < need:
            first_at(done)
            done += 4
        if c:
            second((c - 1) * chunk, chunk)
    edges = []
    for side, k in ((0, 0), (1, rows1 // 2 - 2)):
        for t, (source, out) in enumerate(((h1_ref, edge_h_out), (taps1_ref, edge_taps_out))):
            for ro in range(2):
                copy = pltpu.make_async_copy(
                    source.at[ro, pl.ds(k, 2)], out.at[ro, pl.ds(2 * side, 2)], sems.at[2 + 4 * side + 2 * t + ro]
                )
                copy.start()
                edges.append(copy)
    weights_out.wait("conv1", "conv2")
    for copy in edges:
        copy.wait()
    for c in range(steps):
        for copy in leave(c * chunk):
            copy.wait()


def encoder_own(biases, mid, top, bot, lhalo, rhalo, w1, wd1, w2, n, size):
    rows1 = lhalo.shape[0]
    inner = rows1 // 2 - 2
    vmem = pltpu.VMEM
    inside = pl.BlockSpec(memory_space=pltpu.VMEM)
    return pl.pallas_call(
        functools.partial(encoder_own_kernel, n=n, size=size),
        name="encoder_own",
        in_specs=[inside] * 9,
        out_specs=[ANYWHERE] * 7,
        out_shape=[
            jax.ShapeDtypeStruct((2, inner, size, 512), BF),
            jax.ShapeDtypeStruct((inner, size, 512), BF),
            jax.ShapeDtypeStruct((inner, 6, size, 128), BF),
            jax.ShapeDtypeStruct((2, 4, size, 512), BF),
            jax.ShapeDtypeStruct((2, 4, 8, size, 128), BF),
            jax.ShapeDtypeStruct((1024, 256), BF),
            jax.ShapeDtypeStruct((1536, 256), BF),
        ],
        scratch_shapes=[
            vmem((rows1, 512), F32),
            vmem((rows1, 512), F32),
            vmem((2, rows1 // 2, size, 512), BF),
            vmem((2, rows1 // 2, 8, size, 128), BF),
            vmem((2, inner, size, 512), BF),
            vmem((inner, size, 512), BF),
            vmem((inner, 6, size, 128), BF),
            vmem((1024, 256), BF),
            vmem((1536, 256), BF),
            pltpu.SemaphoreType.DMA((inner // divisor(inner, 6), 4)),
            pltpu.SemaphoreType.DMA((10,)),
        ],
    )(biases, mid, top, bot, near(lhalo), near(rhalo), w1.T, wd1, w2)


def encoder_kernel(
    bias_ref, top_ref, bot_ref, wd1_ref,
    edge_h_ref, edge_taps_ref, conv1_in, conv2_in, d1_own_ref, taps2_own_ref, wd2_in, w3_in, wd3_in,
    e1_ref, e2_out, e3_out, send_ref,
    h1_ref, taps1_ref, d1_ref, taps2_ref, d2_ref, taps3_ref, d3_ref, edge_ref,
    conv1_ref, conv2_ref, wd2_ref, w3_ref, wd3_ref, e2_ref, e3_ref, sems, sems2, sems3,
    *, n, size, rows1, sent, lat,
):
    flags = ends(lat)
    rows2, rows3 = rows1 // 2, rows1 // 4
    inner = rows2 - 2
    fetch = Fetch(
        sems,
        **{
            f"{name}{side}{ro}": (
                source.at[ro, pl.ds(2 * side, 2)],
                target.at[ro, pl.ds(4 if side == 0 else 6, 2)],
            )
            for name, source, target in (("h", edge_h_ref, h1_ref), ("t", edge_taps_ref, taps1_ref))
            for side in range(2)
            for ro in range(2)
        },
        conv1=(conv1_in, conv1_ref),
        conv2=(conv2_in, conv2_ref),
        d1=(d1_own_ref, d1_ref.at[pl.ds(4, inner)]),
        taps2=(taps2_own_ref, taps2_ref.at[pl.ds(4, inner)]),
        wd2=(wd2_in, wd2_ref),
        w3=(w3_in, w3_ref),
        wd3=(wd3_in, wd3_ref),
    )
    mean1, mean2, mean3 = mean_matrix(64), mean_matrix(128), mean_matrix(256)

    for side, ref in ((0, top_ref), (1, bot_ref)):
        base = 6 * side
        rims = ref[8 * n :, :].astype(F32)
        x = ref[0 : 8 * n, :].astype(F32)
        left = [rims[j : j + 1] for j in range(8)]
        right = [rims[8 + j : 9 + j] for j in range(8)]
        at = base if side == 0 else base + 2
        level1(h1_ref, taps1_ref, at, full_rows(x, left, right, n, size), bias_ref[0:1, :], mean1, flags[side])

    fetch.wait("conv1", *(f"{name}{side}{ro}" for name in "ht" for side in range(2) for ro in range(2)))
    for side in range(2):

        def store(ro, lanes, e, side=side):
            keep = slice(2, 4) if side == 0 else slice(0, 2)
            e1_ref[ro, 2 * side : 2 * side + 2, :, lanes] = e[keep]

        d = enc_conv1(taps1_ref, h1_ref, 6 * side, 4, conv1_ref, wd1_ref, store)
        at = 0 if side == 0 else rows2 + 2
        d1_ref[at : at + 4] = d.reshape(4, size, 512)
        u = activate(d.astype(F32), bias_ref[1:2, :], mean2)
        for j in range(4):
            inside = j == 3 if side == 0 else j == 0
            part = u[j * size : (j + 1) * size]
            put_taps(taps2_ref, at + j, part if inside else part * flags[side], 128)

    fetch.wait("conv2", "d1", "taps2", "wd2")
    chunk2, chunk3 = divisor(rows3 + 2, 6), divisor(rows3 // 2, 4)

    def leave2(i):
        part = pl.ds(2 * i, 2 * chunk2)
        return pltpu.make_async_copy(e2_ref.at[part], e2_out.at[part], sems2.at[i // chunk2])

    def leave3(i):
        part = pl.ds(2 * i, 2 * chunk3)
        return pltpu.make_async_copy(e3_ref.at[part], e3_out.at[part], sems3.at[i // chunk3])

    def third(i, count2):
        o = 2 * i
        acc = conv(taps2_ref, o, 2 * count2, 512, conv2_ref)
        flat = 2 * count2 * size
        merged = []
        for q in range(2):
            lanes = slice(q * 256, (q + 1) * 256)
            prior = d1_ref[pl.ds(o + 1, 2 * count2), :, lanes].reshape(flat, 256).astype(F32)
            e = (prior + acc[q * flat : (q + 1) * flat]).astype(BF).reshape(2 * count2, size, 256)
            e2_ref[pl.ds(o, 2 * count2), :, lanes] = e
            for j in range(count2):
                merged.append(jnp.concatenate([e[2 * j], e[2 * j + 1]], axis=1))
        d = dotf(jnp.concatenate(merged, axis=0), wd2_ref[...]).astype(BF)
        d = jnp.concatenate([d[: flat // 2], d[flat // 2 :]], axis=1)
        d2_ref[pl.ds(i, count2)] = d.reshape(count2, size, 512)
        u = activate(d.astype(F32), bias_ref[2:3, :], mean3)
        for j in range(count2):
            put_taps(taps3_ref, i + j, u[j * size : (j + 1) * size] * row_factor(i + j, 1, rows3 + 1, flags), 256)
        leave2(i).start()

    loop((rows3 + 2) // chunk2, lambda c: third(c * chunk2, chunk2))
    fetch.wait("w3", "wd3")

    def fourth(i, count3):
        o = 2 * i
        acc = conv(taps3_ref, o, 2 * count3, 768, w3_ref)
        flat = 2 * count3 * size
        acc = jnp.concatenate([acc[:flat], acc[flat:]], axis=1)
        e = (d2_ref[pl.ds(o + 1, 2 * count3)].reshape(flat, 512).astype(F32) + acc).astype(BF)
        wide = e.astype(F32)
        for j in range(2 * count3):
            edge_ref[0, pl.ds(o + j, 1), :] = wide[j * size : j * size + 1]
            edge_ref[1, pl.ds(o + j, 1), :] = wide[j * size + n - 1 : j * size + n]
        e = e.reshape(2 * count3, size, 512)
        e3_ref[pl.ds(o, 2 * count3)] = e
        merged = [jnp.concatenate([e[2 * j], e[2 * j + 1]], axis=1) for j in range(count3)]
        d = dotf(jnp.concatenate(merged, axis=0), wd3_ref[...])
        for j in range(count3):
            d3_ref[i + j] = d[j * size : j * size + n].astype(BF)
        leave3(i).start()

    loop(rows3 // 2 // chunk3, lambda c: fourth(c * chunk3, chunk3))

    left = edge_ref[0].astype(BF)
    right = edge_ref[1].astype(BF)
    groups, each, copies = sent
    before = lax.rem(lax.axis_index("lon") + groups - 1, groups)
    for d in range(groups):
        send_ref[d, 0:rows3, :] = jnp.where(before == d, left, right)
        for e in range(each):
            row = d * each + e if copies == 1 else d // copies
            send_ref[d, rows3 + e * n : rows3 + (e + 1) * n, :] = d3_ref[row]
    for c in range((rows3 + 2) // chunk2):
        leave2(c * chunk2).wait()
    for c in range(rows3 // 2 // chunk3):
        leave3(c * chunk3).wait()


def encoder(lat_count, biases, top, bot, edge_h, edge_taps, weights, d1, taps2, n, size, rows1, sent):
    rows2, rows3 = rows1 // 2, rows1 // 4
    vmem = pltpu.VMEM
    inside = pl.BlockSpec(memory_space=pltpu.VMEM)
    conv1_w, wd1, conv2_w, wd2, w3, wd3 = weights
    return pl.pallas_call(
        functools.partial(encoder_kernel, n=n, size=size, rows1=rows1, sent=sent, lat=lat_count),
        name="encoder",
        in_specs=[inside] * 4 + [ANYWHERE] * 9,
        out_specs=[inside, ANYWHERE, ANYWHERE, inside],
        out_shape=[
            jax.ShapeDtypeStruct((2, 4, size, 512), BF),
            jax.ShapeDtypeStruct((rows2 + 4, size, 512), BF),
            jax.ShapeDtypeStruct((rows3, size, 512), BF),
            jax.ShapeDtypeStruct((sent[0], rows3 + sent[1] * n, 512), BF),
        ],
        scratch_shapes=[
            vmem((2, 12, size, 512), BF),
            vmem((2, 12, 8, size, 128), BF),
            vmem((rows2 + 6, size, 512), BF),
            vmem((rows2 + 6, 6, size, 128), BF),
            vmem((rows3 + 2, size, 512), BF),
            vmem((rows3 + 2, 8, size, 128), BF),
            vmem((rows3 // 2, n, 512), BF),
            vmem((2, rows3, 512), F32),
            vmem(conv1_w.shape, BF),
            vmem(conv2_w.shape, BF),
            vmem(wd2.shape, BF),
            vmem(w3.shape, BF),
            vmem(wd3.shape, BF),
            vmem((rows2 + 4, size, 512), BF),
            vmem((rows3, size, 512), BF),
            pltpu.SemaphoreType.DMA((15,)),
            pltpu.SemaphoreType.DMA(((rows3 + 2) // divisor(rows3 + 2, 6),)),
            pltpu.SemaphoreType.DMA((rows3 // 2 // divisor(rows3 // 2, 4),)),
        ],
    )(
        biases, near(top), near(bot), wd1,
        edge_h, edge_taps, conv1_w, conv2_w, d1, taps2, wd2, w3, wd3,
    )


def attention_kernel(
    x_ref, bias_ref, wqkv_ref, e3_in, wout_in, out_ref, full_ref, mixed_ref, a4_ref, e3_ref, wout_ref, sems,
    *, n, size, each,
):
    fetch = Fetch(sems, e3=(e3_in, e3_ref), wout=(wout_in, wout_ref))
    tail = size - n
    place = iota((tail, 512), 0)
    groups, _, width = x_ref.shape
    length = groups * n
    edge = e3_ref.shape[0]
    scale = HEAD_DIM**-0.5
    for row in range(each):
        at = edge + row * n
        x = jnp.concatenate([x_ref[g, at : at + n, :].astype(F32) for g in range(groups)], axis=0)
        mean = jnp.mean(x * x, axis=1, keepdims=True)
        u = (x * lax.rsqrt(mean + EPS) + bias_ref[3:4, :]).astype(BF)
        qkv = dotf(u, wqkv_ref[...]).astype(BF)
        left = iota((length, 128), 1) < 64
        for h in range(width // 128):
            q = qkv[:, h * 128 : (h + 1) * 128].astype(F32) * scale
            k = qkv[:, width + h * 128 : width + (h + 1) * 128]
            v = qkv[:, 2 * width + h * 128 : 2 * width + (h + 1) * 128]
            outs = []
            for side in range(2):
                mine = left if side == 0 else jnp.logical_not(left)
                qs = jnp.where(mine, q, 0.0).astype(BF)
                s = lax.dot_general(qs, k, (((1,), (1,)), ((), ())), preferred_element_type=F32)
                e = jnp.exp(s - jnp.max(s, axis=1, keepdims=True))
                total = jnp.sum(e, axis=1, keepdims=True)
                outs.append(dotf(e.astype(BF), v) / total)
            mixed_ref[:, h * 128 : (h + 1) * 128] = jnp.where(left, outs[0], outs[1]).astype(BF)
        if row == 0:
            fetch.wait("e3", "wout")
        a4_ref[...] = x + dotf(mixed_ref[...], wout_ref[...])
        for t in range(length // n):
            after = (t * n + n) % length
            before = (t * n - 1) % length
            rim = jnp.where(
                place == 0,
                a4_ref[after : after + 1, :],
                jnp.where(place == tail - 1, a4_ref[before : before + 1, :], 0.0),
            )
            out_ref[t, row] = jnp.concatenate([a4_ref[t * n : (t + 1) * n, :], rim], axis=0).astype(BF)

    here = lax.axis_index("lon")
    lf = x_ref[lax.rem(here + groups - 1, groups), 0:edge, :].astype(F32)
    rf = x_ref[lax.rem(here + 1, groups), 0:edge, :].astype(F32)
    for r in range(edge):
        rim = jnp.where(place == 0, rf[r : r + 1], jnp.where(place == tail - 1, lf[r : r + 1], 0.0))
        full_ref[r] = jnp.concatenate([e3_ref[r, 0:n, :].astype(F32), rim], axis=0).astype(BF)


def attention(x, biases, e3, w_qkv, w_out, n, size, each):
    groups, _, width = x.shape
    length = groups * n
    return pl.pallas_call(
        functools.partial(attention_kernel, n=n, size=size, each=each),
        name="attention",
        in_specs=[pl.BlockSpec(memory_space=pltpu.VMEM)] * 3 + [ANYWHERE] * 2,
        out_shape=[
            jax.ShapeDtypeStruct((groups, each, size, width), BF),
            jax.ShapeDtypeStruct((e3.shape[0], size, width), BF),
        ],
        scratch_shapes=[
            pltpu.VMEM((length, width), BF),
            pltpu.VMEM((length, width), F32),
            pltpu.VMEM(e3.shape, BF),
            pltpu.VMEM(w_out.shape, BF),
            pltpu.SemaphoreType.DMA((2,)),
        ],
    )(near(x), biases, w_qkv, e3, w_out)


def fill_head(out_ref, w_ref):
    outs, chans = w_ref.shape
    col = iota((outs, 512), 1)
    source = ((col >> 3) & 7) * 4 + (col & 1) * 2 + ((col >> 7) & 1)
    pick = jnp.where(source == iota((outs, 512), 0), 1.0, 0.0).astype(BF)
    wide = dot_tn(w_ref[...], pick)
    col = iota((chans, 512), 1)
    for o in range(2):
        for i in range(4):
            for c in range(2):
                keep = (((col >> 6) & 1) == o) & (((col & 7) >> 1) == i) & ((col >> 8) == c)
                row = o * 512 + i * 128 + c * 64
                out_ref[row : row + 64, :] = jnp.where(keep, wide, 0.0).astype(BF)


def up3(a, e, put, wu_ref, bias, mean, size, factor=None):
    spread = dotf(a.reshape(-1, 512), wu_ref[...])
    for j in range(a.shape[0]):
        for ro in range(2):
            part = spread[j * size : (j + 1) * size, ro * 512 : (ro + 1) * 512]
            h = (part + e[2 * j + ro].astype(F32)).astype(BF)
            u = activate(h.astype(F32), bias, mean)
            put(2 * j + ro, h, u if factor is None else u * factor)


def up2(prior, acc, e, put, wu_ref, bias, mean, size):
    count = prior.shape[0]
    flat = count * size
    g = []
    for q in range(2):
        mine = prior[:, :, q * 256 : (q + 1) * 256].reshape(flat, 256).astype(F32)
        g.append((mine + acc[q * flat : (q + 1) * flat]).astype(BF))
    spread = dotf(jnp.concatenate(g, axis=0), wu_ref[...])
    for j in range(count):
        for ro in range(2):
            part = [
                spread[q * flat + j * size : q * flat + (j + 1) * size, ro * 256 : (ro + 1) * 256] for q in range(2)
            ]
            h = (jnp.concatenate(part, axis=1) + e(2 * j + ro).astype(F32)).astype(BF)
            put(2 * j + ro, h, activate(h.astype(F32), bias, mean))


def up1(prior, acc, e, put, wu_ref, size):
    count = prior.shape[0]
    flat = count * size
    g = []
    for q in range(2):
        mine = prior[:, :, q * 256 : (q + 1) * 256].reshape(flat, 256).astype(F32)
        both = (mine + acc[q * flat : (q + 1) * flat]).astype(BF)
        g += [both[:, :128], both[:, 128:]]
    spread = dotf(jnp.concatenate(g, axis=0), wu_ref[...])
    for j in range(count):
        for ro in range(2):
            part = [
                spread[p * flat + j * size : p * flat + (j + 1) * size, ro * 128 : (ro + 1) * 128] for p in range(4)
            ]
            h = (jnp.concatenate(part, axis=1) + e(j, ro).astype(F32)).astype(BF)
            put(j, ro, h)


def decoder_own_kernel(
    bias_ref, a4_ref, e3_ref, wu3_ref, w3_in, wu2_in, e2_in,
    h2_out, taps2_out, edge_h_out, edge_taps_out,
    h3_ref, taps3_ref, w3_ref, wu2_ref, e2_ref, h2_ref, taps2_ref, sems, sems2,
    *, size,
):
    rows4, rows3 = a4_ref.shape[0], e3_ref.shape[0]
    fetch = Fetch(
        sems, w3=(w3_in, w3_ref), wu2=(wu2_in, wu2_ref), e2=(e2_in.at[pl.ds(4, 2 * rows3 - 4)], e2_ref)
    )
    mean2, mean3 = mean_matrix(128), mean_matrix(256)

    def third(i, count):
        def put(j, h, u):
            h3_ref[2 * i + j] = h
            put_taps(taps3_ref, 2 * i + j, u, 256)

        up3(a4_ref[pl.ds(i, count)], e3_ref[pl.ds(2 * i, 2 * count)], put, wu3_ref, bias_ref[4:5, :], mean3, size)

    loop_chunks(rows4, 4, third)

    edges = []
    for side, at in ((0, 0), (1, rows3 - 2)):
        edges.append(
            pltpu.make_async_copy(taps3_ref.at[pl.ds(at, 2)], edge_taps_out.at[pl.ds(2 * side, 2)], sems.at[3 + side])
        )
        edges.append(
            pltpu.make_async_copy(h3_ref.at[pl.ds(at + side, 1)], edge_h_out.at[pl.ds(side, 1)], sems.at[5 + side])
        )
    for copy in edges:
        copy.start()
    chunk = divisor(rows3 - 2, 7)

    def leave(o):
        part = pl.ds(2 * o, 2 * chunk)
        return [
            pltpu.make_async_copy(h2_ref.at[part], h2_out.at[part], sems2.at[o // chunk, 0]),
            pltpu.make_async_copy(taps2_ref.at[part], taps2_out.at[part], sems2.at[o // chunk, 1]),
        ]

    def second(o, count):
        def put(j, h, u):
            h2_ref[2 * o + j] = h
            put_taps(taps2_ref, 2 * o + j, u, 128)

        acc = conv(taps3_ref, o, count, 768, w3_ref)
        up2(h3_ref[pl.ds(o + 1, count)], acc, lambda j: e2_ref[2 * o + j], put, wu2_ref, bias_ref[5:6, :], mean2, size)

        for copy in leave(o):
            copy.start()

    fetch.wait("w3", "wu2", "e2")
    loop((rows3 - 2) // chunk, lambda c: second(c * chunk, chunk))
    for copy in edges:
        copy.wait()
    for c in range((rows3 - 2) // chunk):
        for copy in leave(c * chunk):
            copy.wait()


def decoder_own(biases, a4, e3, e2, wu3, w3, wu2, size):
    rows3 = e3.shape[0]
    inner = 2 * (rows3 - 2)
    out = pltpu.VMEM
    inside = pl.BlockSpec(memory_space=pltpu.VMEM)
    return pl.pallas_call(
        functools.partial(decoder_own_kernel, size=size),
        name="decoder_own",
        in_specs=[inside] * 4 + [ANYWHERE] * 3,
        out_specs=[ANYWHERE] * 4,
        out_shape=[
            jax.ShapeDtypeStruct((inner, size, 512), BF),
            jax.ShapeDtypeStruct((inner, 6, size, 128), BF),
            jax.ShapeDtypeStruct((2, size, 512), BF),
            jax.ShapeDtypeStruct((4, 8, size, 128), BF),
        ],
        scratch_shapes=[
            out((rows3, size, 512), BF),
            out((rows3, 8, size, 128), BF),
            out(w3.shape, BF),
            out(wu2.shape, BF),
            out((2 * rows3 - 4, size, 512), BF),
            out((inner, size, 512), BF),
            out((inner, 6, size, 128), BF),
            pltpu.SemaphoreType.DMA((7,)),
            pltpu.SemaphoreType.DMA(((rows3 - 2) // divisor(rows3 - 2, 7), 2)),
        ],
    )(biases, near(a4), e3, wu3, w3, wu2, e2)


def decoder_kernel(
    factors, bias_ref, top_ref, bot_ref, edge_h_ref, edge_taps_ref, wu1_ref, wu3_ref, w2_ref, w1_ref, wh_ref,
    h2_own_ref, taps2_own_ref, e2_in, w3_in, wu2_in, e1_edge_in, e1_own_in, noisy_in, noise_in,
    out_ref,
    h3_ref, taps3_ref, h2_ref, taps2_ref, h1_ref, taps1_ref, turn_ref,
    e2_ref, w3_ref, wu2_ref, e1_edge_ref, e1_own_ref, conv2_ref, conv1_ref, head_ref, g_ref, noisy_ref, noise_ref, sems,
    *, n, size, rows1, lat,
):
    rows2 = rows1 // 2
    inner = rows2 - 4
    step = pl.program_id(0)
    last = pl.num_programs(0) - 2

    def prepare():
        fetch = Fetch(
            sems,
            w3=(w3_in, w3_ref),
            e2a=(e2_in.at[pl.ds(0, 4)], e2_ref.at[pl.ds(0, 4)]),
            e2b=(e2_in.at[pl.ds(rows2, 4)], e2_ref.at[pl.ds(4, 4)]),
            wu2=(wu2_in, wu2_ref),
            h2=(h2_own_ref, h2_ref.at[pl.ds(4, inner)]),
            taps2=(taps2_own_ref, taps2_ref.at[pl.ds(4, inner)]),
            e1_edge=(e1_edge_in, e1_edge_ref),
            e1_own=(e1_own_in, e1_own_ref),
            noisy=(noisy_in, noisy_ref),
            noise=(noise_in, noise_ref),
        )
        flags = ends(lat)
        fill_conv1(conv1_ref, w1_ref)
        fill_conv2(conv2_ref, w2_ref)
        fill_head(head_ref, wh_ref)
        mean1, mean2, mean3 = mean_matrix(64), mean_matrix(128), mean_matrix(256)
        bias3, bias2, bias1 = bias_ref[4:5, :], bias_ref[5:6, :], bias_ref[6:7, :]

        for side, ref in ((0, top_ref), (1, bot_ref)):
            at = 0 if side == 0 else 6

            def put3(j, h, u, at=at, side=side):
                if j == 1 - side:
                    h3_ref[3 * side] = h
                put_taps(taps3_ref, at + j, u, 256)

            up3(ref[0:1], ref[1:3], put3, wu3_ref, bias3, mean3, size, flags[side])
            own = 2 if side == 0 else 4
            taps3_ref[own : own + 2] = edge_taps_ref[2 * side : 2 * side + 2]
            h3_ref[1 + side] = edge_h_ref[side]

        rows = [jnp.concatenate([taps3_ref[a : a + 2], taps3_ref[4 + a : 6 + a]], axis=0) for a in range(3)]

        def place2(j):
            return j if j < 4 else rows2 + j - 4

        def put2(j, h, u):
            if j < 2:
                u = u * flags[0]
            if j >= 6:
                u = u * flags[1]
            h2_ref[place2(j)] = h
            put_taps(taps2_ref, place2(j), u, 128)

        fetch.wait("w3", "wu2", "e2a", "e2b")
        up2(h3_ref[...], conv_rows(rows, 768, w3_ref), lambda j: e2_ref[j], put2, wu2_ref, bias2, mean2, size)
        fetch.wait("h2", "taps2", "e1_edge")

        rows = [jnp.concatenate([taps2_ref[a : a + 2], taps2_ref[rows2 + a : rows2 + a + 2]], axis=0) for a in range(3)]
        prior = jnp.concatenate([h2_ref[1:3], h2_ref[rows2 + 1 : rows2 + 3]], axis=0)

        def lay(ro, k, factor=None):
            u = activate(h1_ref[ro, k].astype(F32), bias1, mean1)
            put_taps1(taps1_ref, ro, k, u if factor is None else u * factor)

        def put1(j, ro, h):
            h1_ref[ro, j if j < 2 else rows2 + j - 2] = h

        acc = conv_rows(rows, 512, conv2_ref)
        up1(prior, acc, lambda j, ro: e1_edge_ref[ro, j], put1, wu1_ref, size)

        def first(i, count):
            def put(j, ro, h):
                h1_ref[ro, i + 2 + j] = h

            acc = conv(taps2_ref, i + 2, count, 512, conv2_ref)
            up1(h2_ref[pl.ds(i + 3, count)], acc, lambda j, ro: e1_own_ref[ro, i + j], put, wu1_ref, size)

        def behind(i, count):
            for j in range(count):
                for ro in range(2):
                    lay(ro, i + 2 + j)

        chunk = divisor(rows2 - 2, 6)
        steps = (rows2 - 2) // chunk
        inner_chunk = steps // 2

        def order(c):
            return jnp.where(c == 0, inner_chunk, jnp.where(c <= inner_chunk, c - 1, c))

        fetch.wait("e1_own")
        first(inner_chunk * chunk, chunk)
        for ro in range(2):
            lay(ro, 0, flags[0])
            lay(ro, 1)
            lay(ro, rows2)
            lay(ro, rows2 + 1, flags[1])

        def both(c):
            behind(order(c - 1) * chunk, chunk)
            first(order(c) * chunk, chunk)

        loop(steps - 1, lambda c: both(c + 1))
        behind(order(steps - 1) * chunk, chunk)
        fetch.wait("noisy", "noise")

    pl.when(step == 0)(prepare)

    spread = dotf(g_ref[...], head_ref[...])
    for p in range(4):
        for s in range(4):
            turn_ref[pl.ds(4 * p + s, n, stride=16), :] = spread[p * size : p * size + n, s * 128 : (s + 1) * 128]
    eps = turn_ref[...].T
    nvars, _, cols = noisy_ref.shape
    for o in range(2):
        part = eps[o * 64 : (o + 1) * 64].reshape(nvars, 8, cols)
        rows = pl.ds(pl.multiple_of(jnp.maximum(step - 1, 0) * 16 + o * 8, 8), 8)
        new = factors[0] * noisy_ref[:, rows, :] - factors[1] * part + factors[2] * noise_ref[:, rows, :]
        out_ref[:, o * 8 : (o + 1) * 8, :] = new

    i = jnp.minimum(step, last) * 4
    acc = conv1(taps1_ref, i, 4, conv1_ref)
    flat = 4 * size
    for p in range(4):
        halves = []
        for ro in range(2):
            prior = h1_ref[ro, pl.ds(i + 1, 4), :, p * 128 : (p + 1) * 128].reshape(flat, 128).astype(F32)
            halves.append((prior + acc[p * flat : (p + 1) * flat, ro * 128 : (ro + 1) * 128]).astype(BF))
        both = jnp.concatenate(halves, axis=1)
        for j in range(4):
            g_ref[p * size : (p + 1) * size, j * 256 : (j + 1) * 256] = both[j * size : (j + 1) * size]


def decoder(lat_count, factors, biases, top, bot, edge_h, edge_taps, e2, e1_own, e1_edge, weights, h2, taps2, noisy, step_noise, n, size):
    nvars, lat, cols = noisy.shape
    rows1 = lat // 2
    rows2 = rows1 // 2
    field = pl.BlockSpec((nvars, 16, cols), lambda k: (0, jnp.maximum(k - 1, 0), 0))
    smem = pl.BlockSpec(memory_space=pltpu.SMEM)
    inside = pl.BlockSpec(memory_space=pltpu.VMEM)
    vmem = pltpu.VMEM
    wu3, w3, wu2, w2, wu1, w1, wh = weights
    late = [w3, wu2, e1_edge, e1_own]
    return pl.pallas_call(
        functools.partial(decoder_kernel, n=n, size=size, rows1=rows1, lat=lat_count),
        name="decoder",
        grid=(rows1 // 8 + 1,),
        in_specs=[smem] + [inside] * 10 + [ANYWHERE] * 9,
        out_specs=field,
        out_shape=jax.ShapeDtypeStruct(noisy.shape, F32),
        scratch_shapes=[
            vmem((4, size, 512), BF),
            vmem((8, 8, size, 128), BF),
            vmem((rows2 + 4, size, 512), BF),
            vmem((rows2 + 4, 6, size, 128), BF),
            vmem((2, rows2 + 2, size, 512), BF),
            vmem((2, rows2 + 2, 8, size, 128), BF),
            vmem((cols, 128), F32),
            vmem((8, size, 512), BF),
        ]
        + [vmem(x.shape, BF) for x in late]
        + [vmem((1536, 256), BF), vmem((1024, 256), BF), vmem((1024, 512), BF), vmem((4 * size, 1024), BF)]
        + [vmem(noisy.shape, F32), vmem(noisy.shape, F32), pltpu.SemaphoreType.DMA((10,))],
    )(
        factors, biases, near(top), near(bot), edge_h, edge_taps, wu1, wu3, w2, w1.T, wh.T,
        h2, taps2, e2, *late, noisy, step_noise,
    )


def shift(array, axis, by, closed):
    count = lax.axis_size(axis)
    if closed:
        pairs = [(i, (i + by) % count) for i in range(count)]
    else:
        pairs = [(i, i + by) for i in range(count) if 0 <= i + by < count]
    return lax.ppermute(array, axis, pairs)


def body(
    noisy, coarse, step_noise, timestep, w_time, w_embed, w_enc1, w_down1, w_enc2, w_down2, w_enc3, w_down3,
    w_qkv, w_attn_out, w_up3, w_dec3, w_up2, w_dec2, w_up1, w_dec1, w_head,
):
    nvars, lat, cols = noisy.shape
    n = cols // 16
    size = -(-(n + 2) // 16) * 16
    rows1 = lat // 2
    rows4 = lat // 16
    groups = lax.axis_size("lon")
    lat_count = lax.axis_size("lat")

    wide, left, right = embed_strips(noisy, coarse, w_embed)
    rhalo = shift(left, "lon", -1, True)
    lhalo = shift(right, "lon", 1, True)
    top, mid, bot = embed(noisy, coarse, wide)

    temb = time_embed(timestep, w_time)
    factors = update_factors(timestep)
    widths = [w_enc1.shape[1], w_enc2.shape[1], w_enc3.shape[1], w_qkv.shape[0], w_dec3.shape[1], w_dec2.shape[1], w_dec1.shape[1]]
    starts = [sum(widths[:i]) for i in range(7)]
    biases = jnp.stack(
        [jnp.tile(temb[s : s + w], 512 // w) * (1.0 if i == 3 else 0.5) for i, (s, w) in enumerate(zip(starts, widths))]
    )

    top, bot = add_rims(lhalo, rhalo, top, bot)
    from_top = shift(bot, "lat", 1, False)
    from_bot = shift(top, "lat", -1, False)
    e1_own, d1, taps2, edge_h, edge_taps, conv1_w, conv2_w = encoder_own(
        biases, mid, top, bot, lhalo, rhalo, w_enc1, w_down1, w_enc2, n, size
    )

    copies = max(1, groups // rows4)
    each = max(1, rows4 // groups)
    e1_edge, e2, e3, sent = encoder(
        lat_count, biases, from_top, from_bot, edge_h, edge_taps,
        (conv1_w, w_down1, conv2_w, w_down2, w_enc3, w_down3), d1, taps2, n, size, rows1, (groups, each, copies),
    )
    got = lax.all_to_all(sent, "lon", split_axis=0, concat_axis=0, tiled=True)
    out, e3 = attention(got, biases, e3, w_qkv, w_attn_out, n, size, each)
    a4 = lax.all_to_all(out.reshape(groups, each * size, 512), "lon", split_axis=0, concat_axis=0, tiled=True)
    a4 = a4.reshape(groups * each, size, 512)
    if copies > 1:
        a4 = a4.reshape(rows4, copies, size, 512)[:, 0]

    top = shift(jnp.concatenate([a4[-1:], e3[-2:]]), "lat", 1, False)
    bot = shift(jnp.concatenate([a4[:1], e3[:2]]), "lat", -1, False)
    h2, taps2, edge_h, edge_taps = decoder_own(biases, a4, e3, e2, w_up3, w_dec3, w_up2, size)
    return decoder(
        lat_count, factors, biases, top, bot, edge_h, edge_taps, e2, e1_own, e1_edge,
        (w_up3, w_dec3, w_up2, w_dec2, w_up1, w_dec1, w_head), h2, taps2, noisy, step_noise, n, size,
    )


def solution(mesh):
    field = P(None, "lat", "lon")
    return jax.shard_map(
        body, mesh=mesh, in_specs=(field, field, field) + (P(),) * 18, out_specs=field, check_vma=False
    )
```

```python
import functools
import math

import jax
import jax.numpy as jnp
from jax import lax
from jax.experimental import pallas as pl
from jax.experimental.pallas import tpu as pltpu
from jax.sharding import PartitionSpec as P

HEAD_DIM = 64
T_STEPS = 1000
BF = jnp.bfloat16
F32 = jnp.float32
EPS = 1e-06


def plan(step):
    frac = (step.astype(jnp.float32) / T_STEPS + 0.008) / 1.008
    return jnp.cos(frac * (math.pi / 2)) ** 2


def time_embed(timestep, w_time):
    half = w_time.shape[0] // 2
    freqs = jnp.exp(-math.log(10000.0) * jnp.arange(half, dtype=jnp.float32) / half)
    angle = timestep.astype(jnp.float32)[0] * freqs
    feats = jnp.concatenate([jnp.sin(angle), jnp.cos(angle)])[None]
    return jax.nn.silu(jnp.dot(feats, w_time, precision=lax.Precision.HIGHEST))[0]


def update_factors(timestep):
    current_alpha_product = plan(timestep[0])
    abar_prev = plan(timestep[0] - 1)
    beta = jnp.minimum(1.0 - current_alpha_product / abar_prev, 0.999)
    keep = 1.0 / jnp.sqrt(1.0 - beta)
    noise = beta / jnp.sqrt(1.0 - current_alpha_product) * keep
    sigma = jnp.sqrt(beta * (1.0 - abar_prev) / (1.0 - current_alpha_product))
    return jnp.stack([keep, noise, sigma])


def iota(shape, dim):
    return lax.broadcasted_iota(jnp.int32, shape, dim)


def dotf(a, b):
    return jnp.dot(a, b, preferred_element_type=F32)


def dot_tn(a, b):
    return lax.dot_general(a, b, (((0,), (0,)), ((), ())), preferred_element_type=F32)


def ends(count_of_lat):
    at = lax.axis_index("lat")
    return [jnp.where(at > 0, 1.0, 0.0), jnp.where(at < count_of_lat - 1, 1.0, 0.0)]


def mean_matrix(chans):
    size = 256
    same = (iota((size, size), 0) & -chans) == (iota((size, size), 1) & -chans)
    return jnp.where(same, 4.0 / chans, 0.0).astype(BF)


def activate(x, bias, mean):
    squares = (x * x).astype(BF)
    size = mean.shape[0]
    parts = [dotf(squares[:, i : i + size], mean) for i in range(0, x.shape[1], size)]
    half = x * lax.rsqrt(jnp.concatenate(parts, axis=1) + 4 * EPS) + bias
    return half + half * jnp.tanh(half)


def row_factor(index, low, high, flags):
    return jnp.where(index < low, flags[0], jnp.where(index >= high, flags[1], 1.0))


def put_taps1(ref, parity, k, u):
    size = u.shape[0]
    pairs = [u[:, p * 128 : (p + 1) * 128] for p in range(4)]
    first = iota((size, 128), 1) < 64
    after = pairs[1:] + [pltpu.roll(pairs[0], size - 1, 0)]
    before = [pltpu.roll(pairs[3], 1, 0)] + pairs[:3]
    for p in range(4):
        ref[parity, k, 2 * p] = pairs[p].astype(BF)
        ref[parity, k, 2 * p + 1] = jnp.where(first, after[p], before[p]).astype(BF)


def put_taps(ref, k, u, chans):
    size, lanes = u.shape
    parts = [u[:, i : i + 128] for i in range(0, lanes, 128)]
    edge = chans // 128
    around = (
        [pltpu.roll(x, 1, 0) for x in parts[-edge:]] + parts + [pltpu.roll(x, size - 1, 0) for x in parts[:edge]]
    )
    for i, part in enumerate(around):
        ref[k, i] = part.astype(BF)


def lanes_of(rows, first, last):
    count, _, size, _ = rows.shape
    return [rows[:, b].reshape(count * size, 128) for b in range(first, last)]


def fill_conv1(out_ref, w_ref):
    chans = w_ref.shape[0]
    twice = jnp.where((iota((chans, 128), 1) & 63) == iota((chans, 128), 0), 1.0, 0.0).astype(BF)
    wide = dot_tn(w_ref[...], twice)
    left = iota((chans, 128), 1) < 64
    zero = jnp.zeros((chans, 128), F32)
    for t in range(4):
        for ro in range(2):
            a = t - ro
            for j, dx in enumerate((0, 1, 2, -1)):
                halves = []
                for co in range(2):
                    b = dx - co + 1
                    good = 0 <= a < 3 and 0 <= b < 3
                    halves.append(wide[(a * 3 + b) * chans : (a * 3 + b + 1) * chans] if good else zero)
                value = jnp.where(left, halves[0], halves[1]).astype(BF)
                row = t * 256 + j * 64
                out_ref[row : row + 64, ro * 128 : (ro + 1) * 128] = value


def fill_conv2(out_ref, w_ref):
    zero = jnp.zeros((128, 128), BF)
    for a in range(3):
        part = w_ref[a * 384 : (a + 1) * 384, :]
        out_ref[a * 512 : a * 512 + 384, 0:128] = part
        out_ref[a * 512 + 384 : (a + 1) * 512, 0:128] = zero
        out_ref[a * 512 : a * 512 + 128, 128:256] = zero
        out_ref[a * 512 + 128 : (a + 1) * 512, 128:256] = part


def conv1(taps_ref, i, count, w_ref):
    rows = [
        taps_ref[1, pl.ds(i, count)],
        taps_ref[0, pl.ds(i + 1, count)],
        taps_ref[1, pl.ds(i + 1, count)],
        taps_ref[0, pl.ds(i + 2, count)],
    ]
    lhs = [jnp.concatenate([x for r in rows for x in lanes_of(r, 2 * p, 2 * p + 2)], axis=1) for p in range(4)]
    return dotf(jnp.concatenate(lhs, axis=0), w_ref[...])


def conv_rows(rows, reach, w_ref):
    lhs = [
        jnp.concatenate([x for r in rows for x in lanes_of(r, 2 * q, 2 * q + reach // 128)], axis=1) for q in range(2)
    ]
    return dotf(jnp.concatenate(lhs, axis=0), w_ref[...])


def conv(taps_ref, o, count, reach, w_ref):
    return conv_rows([taps_ref[pl.ds(o + a, count)] for a in range(3)], reach, w_ref)


def loop(count, body):
    def step(i, carry):
        body(i)
        return carry

    lax.fori_loop(0, count, step, 0)


def divisor(total, most):
    return max(d for d in range(1, most + 1) if total % d == 0)


def loop_chunks(total, chunk, body):
    chunk = min(chunk, total)
    steps = -(-total // chunk)
    loop(steps, lambda c: body(jnp.minimum(c * chunk, total - chunk), chunk))


def fill_embed(out_ref, w_ref):
    feats, chans = w_ref.shape
    twice = jnp.where((iota((chans, 128), 1) & 63) == iota((chans, 128), 0), 1.0, 0.0).astype(BF)
    wide = dotf(w_ref[...], twice).astype(BF)
    k = iota((512, feats), 0)
    source = ((k >> 3) & 15) * 4 + (k & 1) * 2 + ((k >> 7) & 1)
    pick = jnp.where(source == iota((512, feats), 1), 1.0, 0.0).astype(BF)
    wide = dotf(pick, wide)
    k = iota((512, 128), 0)
    right = iota((512, 128), 1) >= 64
    same_cell = right == ((k >> 8) == 1)
    for i in range(4):
        keep = same_cell & (((k & 7) >> 1) == i)
        out_ref[:, i * 128 : (i + 1) * 128] = jnp.where(keep, wide, 0.0).astype(BF)


def embed_rows(fields, w_ref, turn_ref, slot):
    n = fields[0].shape[1] // 16
    turn_ref[slot] = jnp.concatenate(fields, axis=0).T
    lhs = [
        jnp.concatenate([turn_ref[slot, pl.ds(4 * p + s, n, stride=16), :] for s in range(4)], axis=1)
        for p in range(4)
    ]
    res = dotf(jnp.concatenate(lhs, axis=0).astype(BF), w_ref[...])
    return [
        jnp.concatenate([res[p * n : (p + 1) * n, i * 128 : (i + 1) * 128] for p in range(4)], axis=1)
        for i in range(4)
    ]


def strips_kernel(w_ref, nl_ref, cl_ref, nr_ref, cr_ref, wide_ref, left_ref, right_ref, turn_ref, strip_ref):
    fill_embed(wide_ref, w_ref)
    octets = nl_ref.shape[1] // 8
    first = iota((64, 128), 1) < 64
    for o in range(octets):
        rows = slice(o * 8, (o + 1) * 8)
        block = jnp.concatenate(
            [
                jnp.where(first, a[:, rows, :].reshape(64, 128), b[:, rows, :].reshape(64, 128))
                for a, b in ((nl_ref, nr_ref), (cl_ref, cr_ref))
            ],
            axis=0,
        ).T
        turn_ref[0, o * 16 : (o + 1) * 16, :] = block[:16]
        turn_ref[1, o * 16 : (o + 1) * 16, :] = block[112:]
    lhs = [
        jnp.concatenate([turn_ref[side, pl.ds(4 * p + s, octets, stride=16), :] for s in range(4)], axis=1)
        for side in range(2)
        for p in range(4)
    ]
    res = dotf(jnp.concatenate(lhs, axis=0).astype(BF), wide_ref[...])
    for side, out_ref in ((0, left_ref), (1, right_ref)):
        for p in range(4):
            at = (side * 4 + p) * octets
            for i in range(4):
                strip_ref[p, pl.ds(i, octets, stride=4), :] = res[at : at + octets, i * 128 : (i + 1) * 128]
        for p in range(4):
            out_ref[:, p * 128 : (p + 1) * 128] = strip_ref[p].astype(BF)


def embed_kernel(wide_ref, noisy_in, coarse_in, top_out, mid_out, bot_out, x_ref, turn_ref, e0_ref, sems, out_sems):
    _, nvars, rows, cols = x_ref.shape
    n = cols // 16
    chunks = rows // 16

    def reads(c):
        part = pl.ds(pl.multiple_of(16 * c, 16), 16)
        return [
            pltpu.make_async_copy(source.at[:, part, :], x_ref.at[t, :, part, :], sems.at[c, t])
            for t, source in enumerate((noisy_in, coarse_in))
        ]

    def write(c, out, place):
        part = pl.ds(pl.multiple_of(c * 8 * n, 8 * n), 8 * n)
        to = pl.ds(pl.multiple_of(place * 8 * n, 8 * n), 8 * n)
        return pltpu.make_async_copy(e0_ref.at[part], out.at[to], out_sems.at[c])

    def writes(c):
        return write(c, top_out, 0) if c == 0 else write(c, bot_out, 0) if c == chunks - 1 else write(c, mid_out, c - 1)

    for c in range(chunks):
        for copy in reads(c):
            copy.start()

    def chunk(c):
        for copy in reads(c):
            copy.wait()
        out = []
        for o in range(2):
            at = pl.ds(pl.multiple_of(16 * c + 8 * o, 8), 8)
            fields = [x_ref[t, :, at, :].reshape(8 * nvars, cols) for t in range(2)]
            out += embed_rows(fields, wide_ref, turn_ref, o)
        e0_ref[pl.ds(pl.multiple_of(c * 8 * n, 8 * n), 8 * n), :] = jnp.concatenate(out, axis=0).astype(BF)

        @pl.when((c > 0) & (c < chunks - 1))
        def _():
            write(c, mid_out, c - 1).start()

    loop(chunks, chunk)
    for c in (0, chunks - 1):
        writes(c).start()
    for c in range(chunks):
        writes(c).wait()


def rims_kernel(left_ref, right_ref, top_in, bot_in, top_out, bot_out, rim_ref, sems):
    count = left_ref.shape[0]
    at = top_out.shape[0] - 16
    copies = []
    for k, out in ((0, top_out), (1, bot_out)):
        rows = slice(0, 16) if k == 0 else slice(count - 16, count)
        pick = slice(0, 8) if k == 0 else slice(8, 16)
        rim_ref[k] = jnp.concatenate([r[rows, :].astype(F32)[pick] for r in (left_ref, right_ref)], axis=0).astype(BF)
        copies.append(pltpu.make_async_copy(rim_ref.at[k], out.at[pl.ds(at, 16)], sems.at[k]))
        copies[-1].start()
    for copy in copies:
        copy.wait()


def near(array):
    return pltpu.with_memory_space_constraint(array, pltpu.VMEM)


ANYWHERE = pl.BlockSpec(memory_space=pl.ANY)


class Fetch:
    def __init__(self, sems, **pairs):
        self.copies = {name: pltpu.make_async_copy(src, dst, sems.at[i]) for i, (name, (src, dst)) in enumerate(pairs.items())}
        for copy in self.copies.values():
            copy.start()

    def wait(self, *names):
        for name in names:
            self.copies[name].wait()


def whole(shape):
    return pl.BlockSpec(shape, lambda *_: (0,) * len(shape))


def embed_strips(noisy, coarse, w_embed):
    nvars, rows, cols = noisy.shape
    sides = [pl.BlockSpec((nvars, rows, 128), lambda k: (0, 0, 0)), pl.BlockSpec((nvars, rows, 128), lambda k: (0, 0, cols // 128 - 1))]
    strip = jax.ShapeDtypeStruct((rows // 2, 512), BF)
    return pl.pallas_call(
        strips_kernel,
        name="embed_strips",
        grid=(1,),
        in_specs=[whole(w_embed.shape), sides[0], sides[0], sides[1], sides[1]],
        out_specs=[whole((512, 512)), whole(strip.shape), whole(strip.shape)],
        out_shape=[jax.ShapeDtypeStruct((512, 512), BF), strip, strip],
        scratch_shapes=[pltpu.VMEM((2, rows * 2, 128), F32), pltpu.VMEM((4, rows // 2, 128), F32)],
    )(w_embed, noisy, coarse, noisy, coarse)


def embed(noisy, coarse, wide):
    nvars, rows, cols = noisy.shape
    n = cols // 16
    pay = jax.ShapeDtypeStruct((8 * n + 16, 512), BF)
    return pl.pallas_call(
        embed_kernel,
        name="embed",
        in_specs=[pl.BlockSpec(memory_space=pltpu.VMEM), ANYWHERE, ANYWHERE],
        out_specs=[ANYWHERE] * 3,
        out_shape=[pay, jax.ShapeDtypeStruct(((rows // 2 - 16) * n, 512), BF), pay],
        scratch_shapes=[
            pltpu.VMEM((2, nvars, rows, cols), F32),
            pltpu.VMEM((2, cols, 128), F32),
            pltpu.VMEM((rows // 2 * n, 512), BF),
            pltpu.SemaphoreType.DMA((rows // 16, 2)),
            pltpu.SemaphoreType.DMA((rows // 16,)),
        ],
    )(wide, noisy, coarse)


def add_rims(left, right, top, bot):
    inside = pl.BlockSpec(memory_space=pltpu.VMEM)
    return pl.pallas_call(
        rims_kernel,
        name="rims",
        in_specs=[inside, inside, ANYWHERE, ANYWHERE],
        out_specs=[ANYWHERE] * 2,
        out_shape=[jax.ShapeDtypeStruct(top.shape, BF)] * 2,
        scratch_shapes=[pltpu.VMEM((2, 16, 512), BF), pltpu.SemaphoreType.DMA((2,))],
        input_output_aliases={2: 0, 3: 1},
    )(near(left), near(right), top, bot)


def full_rows(x, left, right, n, size):
    tail = size - n
    place = iota((tail, 512), 0)
    full = []
    for j in range(x.shape[0] // n):
        rim = jnp.where(place == 0, right[j], jnp.where(place == tail - 1, left[j], 0.0))
        full += [x[j * n : (j + 1) * n], rim]
    return jnp.concatenate(full, axis=0)


def level1(h_ref, taps_ref, k, h, bias, mean, factor=None):
    size = h_ref.shape[2]
    u = activate(h, bias, mean)
    for j in range(h.shape[0] // size):
        part = u[j * size : (j + 1) * size]
        h_ref[j % 2, k + j // 2] = h[j * size : (j + 1) * size].astype(BF)
        put_taps1(taps_ref, j % 2, k + j // 2, part if factor is None else part * factor)


def enc_conv1(taps_ref, h_ref, i, count, conv_ref, wd_ref, store):
    size = taps_ref.shape[3]
    acc = conv1(taps_ref, i, count, conv_ref)
    flat = count * size
    merged = []
    for p in range(4):
        halves = []
        for ro in range(2):
            lanes = slice(p * 128, (p + 1) * 128)
            prior = h_ref[ro, pl.ds(i + 1, count), :, lanes].reshape(flat, 128).astype(F32)
            e = (prior + acc[p * flat : (p + 1) * flat, ro * 128 : (ro + 1) * 128]).astype(BF)
            store(ro, lanes, e.reshape(count, size, 128))
            halves.append(e)
        merged.append(jnp.concatenate(halves, axis=1))
    d = dotf(jnp.concatenate(merged, axis=0), wd_ref[...]).astype(BF)
    return jnp.concatenate([d[p * flat : (p + 1) * flat] for p in range(4)], axis=1)


def encoder_own_kernel(
    bias_ref, mid_ref, top_ref, bot_ref, lhalo_ref, rhalo_ref, w1_ref, wd1_ref, w2_ref,
    e1_out, d1_out, taps2_out, edge_h_out, edge_taps_out, conv1_out, conv2_out,
    lf_ref, rf_ref, h1_ref, taps1_ref, e1_ref, d1_ref, taps2_ref, conv1_ref, conv2_ref, sem, sems,
    *, n, size,
):
    fill_conv1(conv1_ref, w1_ref)
    fill_conv2(conv2_ref, w2_ref)
    weights_out = Fetch(sems, conv1=(conv1_ref, conv1_out), conv2=(conv2_ref, conv2_out))
    lf_ref[...] = lhalo_ref[...].astype(F32)
    rf_ref[...] = rhalo_ref[...].astype(F32)
    mean1, mean2 = mean_matrix(64), mean_matrix(128)
    rows1 = lhalo_ref.shape[0]

    def first(x, row):
        left = [lf_ref[pl.ds(row + j, 1), :] for j in range(4)]
        right = [rf_ref[pl.ds(row + j, 1), :] for j in range(4)]
        k = row // 2
        level1(h1_ref, taps1_ref, k, full_rows(x.astype(F32), left, right, n, size), bias_ref[0:1, :], mean1)

    def first_at(row):
        if row < 8:
            first(top_ref[row * n : (row + 4) * n, :], row)
        elif row < rows1 - 8:
            first(mid_ref[(row - 8) * n : (row - 4) * n, :], row)
        else:
            at = row - rows1 + 8
            first(bot_ref[at * n : (at + 4) * n, :], row)

    def second(i, count):
        def store(ro, lanes, e):
            e1_ref[ro, pl.ds(i, count), :, lanes] = e

        d = enc_conv1(taps1_ref, h1_ref, i, count, conv1_ref, wd1_ref, store)
        d1_ref[pl.ds(i, count)] = d.reshape(count, size, 512)
        u = activate(d.astype(F32), bias_ref[1:2, :], mean2)
        for j in range(count):
            put_taps(taps2_ref, i + j, u[j * size : (j + 1) * size], 128)
        for copy in leave(i):
            copy.start()

    chunk = divisor(rows1 // 2 - 2, 10)
    steps = (rows1 // 2 - 2) // chunk

    def leave(i):
        part = pl.ds(i, chunk)
        slot = i // chunk
        return [
            pltpu.make_async_copy(e1_ref.at[0, part], e1_out.at[0, part], sem.at[slot, 0]),
            pltpu.make_async_copy(e1_ref.at[1, part], e1_out.at[1, part], sem.at[slot, 1]),
            pltpu.make_async_copy(d1_ref.at[part], d1_out.at[part], sem.at[slot, 2]),
            pltpu.make_async_copy(taps2_ref.at[part], taps2_out.at[part], sem.at[slot, 3]),
        ]

    done = 0
    for c in range(steps + 1):
        need = rows1 if c == steps else min(rows1, -(-(2 * chunk * (c + 1) + 3) // 4) * 4)
        while done < need:
            first_at(done)
            done += 4
        if c:
            second((c - 1) * chunk, chunk)
    edges = []
    for side, k in ((0, 0), (1, rows1 // 2 - 2)):
        for t, (source, out) in enumerate(((h1_ref, edge_h_out), (taps1_ref, edge_taps_out))):
            for ro in range(2):
                copy = pltpu.make_async_copy(
                    source.at[ro, pl.ds(k, 2)], out.at[ro, pl.ds(2 * side, 2)], sems.at[2 + 4 * side + 2 * t + ro]
                )
                copy.start()
                edges.append(copy)
    weights_out.wait("conv1", "conv2")
    for copy in edges:
        copy.wait()
    for c in range(steps):
        for copy in leave(c * chunk):
            copy.wait()


def encoder_own(biases, mid, top, bot, lhalo, rhalo, w1, wd1, w2, n, size):
    rows1 = lhalo.shape[0]
    inner = rows1 // 2 - 2
    vmem = pltpu.VMEM
    inside = pl.BlockSpec(memory_space=pltpu.VMEM)
    return pl.pallas_call(
        functools.partial(encoder_own_kernel, n=n, size=size),
        name="encoder_own",
        in_specs=[inside] * 9,
        out_specs=[ANYWHERE] * 7,
        out_shape=[
            jax.ShapeDtypeStruct((2, inner, size, 512), BF),
            jax.ShapeDtypeStruct((inner, size, 512), BF),
            jax.ShapeDtypeStruct((inner, 6, size, 128), BF),
            jax.ShapeDtypeStruct((2, 4, size, 512), BF),
            jax.ShapeDtypeStruct((2, 4, 8, size, 128), BF),
            jax.ShapeDtypeStruct((1024, 256), BF),
            jax.ShapeDtypeStruct((1536, 256), BF),
        ],
        scratch_shapes=[
            vmem((rows1, 512), F32),
            vmem((rows1, 512), F32),
            vmem((2, rows1 // 2, size, 512), BF),
            vmem((2, rows1 // 2, 8, size, 128), BF),
            vmem((2, inner, size, 512), BF),
            vmem((inner, size, 512), BF),
            vmem((inner, 6, size, 128), BF),
            vmem((1024, 256), BF),
            vmem((1536, 256), BF),
            pltpu.SemaphoreType.DMA((inner // divisor(inner, 10), 4)),
            pltpu.SemaphoreType.DMA((10,)),
        ],
    )(biases, mid, top, bot, near(lhalo), near(rhalo), w1.T, wd1, w2)


def encoder_kernel(
    bias_ref, top_ref, bot_ref, wd1_ref,
    edge_h_ref, edge_taps_ref, conv1_in, conv2_in, d1_own_ref, taps2_own_ref, wd2_in, w3_in, wd3_in,
    e1_ref, e2_out, e3_out, send_ref,
    h1_ref, taps1_ref, d1_ref, taps2_ref, d2_ref, taps3_ref, d3_ref, edge_ref,
    conv1_ref, conv2_ref, wd2_ref, w3_ref, wd3_ref, e2_ref, e3_ref, sems, sems2, sems3,
    *, n, size, rows1, sent, lat,
):
    flags = ends(lat)
    rows2, rows3 = rows1 // 2, rows1 // 4
    inner = rows2 - 2
    fetch = Fetch(
        sems,
        **{
            f"{name}{side}{ro}": (
                source.at[ro, pl.ds(2 * side, 2)],
                target.at[ro, pl.ds(4 if side == 0 else 6, 2)],
            )
            for name, source, target in (("h", edge_h_ref, h1_ref), ("t", edge_taps_ref, taps1_ref))
            for side in range(2)
            for ro in range(2)
        },
        conv1=(conv1_in, conv1_ref),
        conv2=(conv2_in, conv2_ref),
        d1=(d1_own_ref, d1_ref.at[pl.ds(4, inner)]),
        taps2=(taps2_own_ref, taps2_ref.at[pl.ds(4, inner)]),
        wd2=(wd2_in, wd2_ref),
        w3=(w3_in, w3_ref),
        wd3=(wd3_in, wd3_ref),
    )
    mean1, mean2, mean3 = mean_matrix(64), mean_matrix(128), mean_matrix(256)

    for side, ref in ((0, top_ref), (1, bot_ref)):
        base = 6 * side
        rims = ref[8 * n :, :].astype(F32)
        x = ref[0 : 8 * n, :].astype(F32)
        left = [rims[j : j + 1] for j in range(8)]
        right = [rims[8 + j : 9 + j] for j in range(8)]
        at = base if side == 0 else base + 2
        level1(h1_ref, taps1_ref, at, full_rows(x, left, right, n, size), bias_ref[0:1, :], mean1, flags[side])

    fetch.wait("conv1", *(f"{name}{side}{ro}" for name in "ht" for side in range(2) for ro in range(2)))
    for side in range(2):

        def store(ro, lanes, e, side=side):
            keep = slice(2, 4) if side == 0 else slice(0, 2)
            e1_ref[ro, 2 * side : 2 * side + 2, :, lanes] = e[keep]

        d = enc_conv1(taps1_ref, h1_ref, 6 * side, 4, conv1_ref, wd1_ref, store)
        at = 0 if side == 0 else rows2 + 2
        d1_ref[at : at + 4] = d.reshape(4, size, 512)
        u = activate(d.astype(F32), bias_ref[1:2, :], mean2)
        for j in range(4):
            inside = j == 3 if side == 0 else j == 0
            part = u[j * size : (j + 1) * size]
            put_taps(taps2_ref, at + j, part if inside else part * flags[side], 128)

    fetch.wait("conv2", "d1", "taps2", "wd2")
    chunk2, chunk3 = divisor(rows3 + 2, 9), divisor(rows3 // 2, 4)

    def leave2(i):
        part = pl.ds(2 * i, 2 * chunk2)
        return pltpu.make_async_copy(e2_ref.at[part], e2_out.at[part], sems2.at[i // chunk2])

    def leave3(i):
        part = pl.ds(2 * i, 2 * chunk3)
        return pltpu.make_async_copy(e3_ref.at[part], e3_out.at[part], sems3.at[i // chunk3])

    def third(i, count2):
        o = 2 * i
        acc = conv(taps2_ref, o, 2 * count2, 512, conv2_ref)
        flat = 2 * count2 * size
        merged = []
        for q in range(2):
            lanes = slice(q * 256, (q + 1) * 256)
            prior = d1_ref[pl.ds(o + 1, 2 * count2), :, lanes].reshape(flat, 256).astype(F32)
            e = (prior + acc[q * flat : (q + 1) * flat]).astype(BF).reshape(2 * count2, size, 256)
            e2_ref[pl.ds(o, 2 * count2), :, lanes] = e
            for j in range(count2):
                merged.append(jnp.concatenate([e[2 * j], e[2 * j + 1]], axis=1))
        d = dotf(jnp.concatenate(merged, axis=0), wd2_ref[...]).astype(BF)
        d = jnp.concatenate([d[: flat // 2], d[flat // 2 :]], axis=1)
        d2_ref[pl.ds(i, count2)] = d.reshape(count2, size, 512)
        u = activate(d.astype(F32), bias_ref[2:3, :], mean3)
        for j in range(count2):
            put_taps(taps3_ref, i + j, u[j * size : (j + 1) * size] * row_factor(i + j, 1, rows3 + 1, flags), 256)
        leave2(i).start()

    loop((rows3 + 2) // chunk2, lambda c: third(c * chunk2, chunk2))
    fetch.wait("w3", "wd3")

    def fourth(i, count3):
        o = 2 * i
        acc = conv(taps3_ref, o, 2 * count3, 768, w3_ref)
        flat = 2 * count3 * size
        acc = jnp.concatenate([acc[:flat], acc[flat:]], axis=1)
        e = (d2_ref[pl.ds(o + 1, 2 * count3)].reshape(flat, 512).astype(F32) + acc).astype(BF)
        wide = e.astype(F32)
        for j in range(2 * count3):
            edge_ref[0, pl.ds(o + j, 1), :] = wide[j * size : j * size + 1]
            edge_ref[1, pl.ds(o + j, 1), :] = wide[j * size + n - 1 : j * size + n]
        e = e.reshape(2 * count3, size, 512)
        e3_ref[pl.ds(o, 2 * count3)] = e
        merged = [jnp.concatenate([e[2 * j], e[2 * j + 1]], axis=1) for j in range(count3)]
        d = dotf(jnp.concatenate(merged, axis=0), wd3_ref[...])
        for j in range(count3):
            d3_ref[i + j] = d[j * size : j * size + n].astype(BF)
        leave3(i).start()

    loop(rows3 // 2 // chunk3, lambda c: fourth(c * chunk3, chunk3))

    left = edge_ref[0].astype(BF)
    right = edge_ref[1].astype(BF)
    groups, each, copies = sent
    before = lax.rem(lax.axis_index("lon") + groups - 1, groups)
    for d in range(groups):
        send_ref[d, 0:rows3, :] = jnp.where(before == d, left, right)
        for e in range(each):
            row = d * each + e if copies == 1 else d // copies
            send_ref[d, rows3 + e * n : rows3 + (e + 1) * n, :] = d3_ref[row]
    for c in range((rows3 + 2) // chunk2):
        leave2(c * chunk2).wait()
    for c in range(rows3 // 2 // chunk3):
        leave3(c * chunk3).wait()


def encoder(lat_count, biases, top, bot, edge_h, edge_taps, weights, d1, taps2, n, size, rows1, sent):
    rows2, rows3 = rows1 // 2, rows1 // 4
    vmem = pltpu.VMEM
    inside = pl.BlockSpec(memory_space=pltpu.VMEM)
    conv1_w, wd1, conv2_w, wd2, w3, wd3 = weights
    return pl.pallas_call(
        functools.partial(encoder_kernel, n=n, size=size, rows1=rows1, sent=sent, lat=lat_count),
        name="encoder",
        in_specs=[inside] * 4 + [ANYWHERE] * 9,
        out_specs=[inside, ANYWHERE, ANYWHERE, inside],
        out_shape=[
            jax.ShapeDtypeStruct((2, 4, size, 512), BF),
            jax.ShapeDtypeStruct((rows2 + 4, size, 512), BF),
            jax.ShapeDtypeStruct((rows3, size, 512), BF),
            jax.ShapeDtypeStruct((sent[0], rows3 + sent[1] * n, 512), BF),
        ],
        scratch_shapes=[
            vmem((2, 12, size, 512), BF),
            vmem((2, 12, 8, size, 128), BF),
            vmem((rows2 + 6, size, 512), BF),
            vmem((rows2 + 6, 6, size, 128), BF),
            vmem((rows3 + 2, size, 512), BF),
            vmem((rows3 + 2, 8, size, 128), BF),
            vmem((rows3 // 2, n, 512), BF),
            vmem((2, rows3, 512), F32),
            vmem(conv1_w.shape, BF),
            vmem(conv2_w.shape, BF),
            vmem(wd2.shape, BF),
            vmem(w3.shape, BF),
            vmem(wd3.shape, BF),
            vmem((rows2 + 4, size, 512), BF),
            vmem((rows3, size, 512), BF),
            pltpu.SemaphoreType.DMA((15,)),
            pltpu.SemaphoreType.DMA(((rows3 + 2) // divisor(rows3 + 2, 9),)),
            pltpu.SemaphoreType.DMA((rows3 // 2 // divisor(rows3 // 2, 4),)),
        ],
    )(
        biases, near(top), near(bot), wd1,
        edge_h, edge_taps, conv1_w, conv2_w, d1, taps2, wd2, w3, wd3,
    )


def attention_kernel(
    x_ref, bias_ref, wqkv_ref, e3_in, wout_in, out_ref, full_ref, mixed_ref, a4_ref, e3_ref, wout_ref, sems,
    *, n, size, each,
):
    fetch = Fetch(sems, e3=(e3_in, e3_ref), wout=(wout_in, wout_ref))
    tail = size - n
    place = iota((tail, 512), 0)
    groups, _, width = x_ref.shape
    length = groups * n
    edge = e3_ref.shape[0]
    scale = HEAD_DIM**-0.5
    for row in range(each):
        at = edge + row * n
        x = jnp.concatenate([x_ref[g, at : at + n, :].astype(F32) for g in range(groups)], axis=0)
        mean = jnp.mean(x * x, axis=1, keepdims=True)
        u = (x * lax.rsqrt(mean + EPS) + bias_ref[3:4, :]).astype(BF)
        qkv = dotf(u, wqkv_ref[...]).astype(BF)
        left = iota((length, 128), 1) < 64
        for h in range(width // 128):
            q = qkv[:, h * 128 : (h + 1) * 128].astype(F32) * scale
            k = qkv[:, width + h * 128 : width + (h + 1) * 128]
            v = qkv[:, 2 * width + h * 128 : 2 * width + (h + 1) * 128]
            outs = []
            for side in range(2):
                mine = left if side == 0 else jnp.logical_not(left)
                qs = jnp.where(mine, q, 0.0).astype(BF)
                s = lax.dot_general(qs, k, (((1,), (1,)), ((), ())), preferred_element_type=F32)
                e = jnp.exp(s - jnp.max(s, axis=1, keepdims=True))
                total = jnp.sum(e, axis=1, keepdims=True)
                outs.append(dotf(e.astype(BF), v) / total)
            mixed_ref[:, h * 128 : (h + 1) * 128] = jnp.where(left, outs[0], outs[1]).astype(BF)
        if row == 0:
            fetch.wait("e3", "wout")
        a4_ref[...] = x + dotf(mixed_ref[...], wout_ref[...])
        for t in range(length // n):
            after = (t * n + n) % length
            before = (t * n - 1) % length
            rim = jnp.where(
                place == 0,
                a4_ref[after : after + 1, :],
                jnp.where(place == tail - 1, a4_ref[before : before + 1, :], 0.0),
            )
            out_ref[t, row] = jnp.concatenate([a4_ref[t * n : (t + 1) * n, :], rim], axis=0).astype(BF)

    here = lax.axis_index("lon")
    lf = x_ref[lax.rem(here + groups - 1, groups), 0:edge, :].astype(F32)
    rf = x_ref[lax.rem(here + 1, groups), 0:edge, :].astype(F32)
    for r in range(edge):
        rim = jnp.where(place == 0, rf[r : r + 1], jnp.where(place == tail - 1, lf[r : r + 1], 0.0))
        full_ref[r] = jnp.concatenate([e3_ref[r, 0:n, :].astype(F32), rim], axis=0).astype(BF)


def attention(x, biases, e3, w_qkv, w_out, n, size, each):
    groups, _, width = x.shape
    length = groups * n
    return pl.pallas_call(
        functools.partial(attention_kernel, n=n, size=size, each=each),
        name="attention",
        in_specs=[pl.BlockSpec(memory_space=pltpu.VMEM)] * 3 + [ANYWHERE] * 2,
        out_shape=[
            jax.ShapeDtypeStruct((groups, each, size, width), BF),
            jax.ShapeDtypeStruct((e3.shape[0], size, width), BF),
        ],
        scratch_shapes=[
            pltpu.VMEM((length, width), BF),
            pltpu.VMEM((length, width), F32),
            pltpu.VMEM(e3.shape, BF),
            pltpu.VMEM(w_out.shape, BF),
            pltpu.SemaphoreType.DMA((2,)),
        ],
    )(near(x), biases, w_qkv, e3, w_out)


def fill_head(out_ref, w_ref):
    outs, chans = w_ref.shape
    col = iota((outs, 512), 1)
    source = ((col >> 3) & 7) * 4 + (col & 1) * 2 + ((col >> 7) & 1)
    pick = jnp.where(source == iota((outs, 512), 0), 1.0, 0.0).astype(BF)
    wide = dot_tn(w_ref[...], pick)
    col = iota((chans, 512), 1)
    for o in range(2):
        for i in range(4):
            for c in range(2):
                keep = (((col >> 6) & 1) == o) & (((col & 7) >> 1) == i) & ((col >> 8) == c)
                row = o * 512 + i * 128 + c * 64
                out_ref[row : row + 64, :] = jnp.where(keep, wide, 0.0).astype(BF)


def up3(a, e, put, wu_ref, bias, mean, size, factor=None):
    spread = dotf(a.reshape(-1, 512), wu_ref[...])
    for j in range(a.shape[0]):
        for ro in range(2):
            part = spread[j * size : (j + 1) * size, ro * 512 : (ro + 1) * 512]
            h = (part + e[2 * j + ro].astype(F32)).astype(BF)
            u = activate(h.astype(F32), bias, mean)
            put(2 * j + ro, h, u if factor is None else u * factor)


def up2(prior, acc, e, put, wu_ref, bias, mean, size):
    count = prior.shape[0]
    flat = count * size
    g = []
    for q in range(2):
        mine = prior[:, :, q * 256 : (q + 1) * 256].reshape(flat, 256).astype(F32)
        g.append((mine + acc[q * flat : (q + 1) * flat]).astype(BF))
    spread = dotf(jnp.concatenate(g, axis=0), wu_ref[...])
    for j in range(count):
        for ro in range(2):
            part = [
                spread[q * flat + j * size : q * flat + (j + 1) * size, ro * 256 : (ro + 1) * 256] for q in range(2)
            ]
            h = (jnp.concatenate(part, axis=1) + e(2 * j + ro).astype(F32)).astype(BF)
            put(2 * j + ro, h, activate(h.astype(F32), bias, mean))


def up1(prior, acc, e, put, wu_ref, size):
    count = prior.shape[0]
    flat = count * size
    g = []
    for q in range(2):
        mine = prior[:, :, q * 256 : (q + 1) * 256].reshape(flat, 256).astype(F32)
        both = (mine + acc[q * flat : (q + 1) * flat]).astype(BF)
        g += [both[:, :128], both[:, 128:]]
    spread = dotf(jnp.concatenate(g, axis=0), wu_ref[...])
    for j in range(count):
        for ro in range(2):
            part = [
                spread[p * flat + j * size : p * flat + (j + 1) * size, ro * 128 : (ro + 1) * 128] for p in range(4)
            ]
            h = (jnp.concatenate(part, axis=1) + e(j, ro).astype(F32)).astype(BF)
            put(j, ro, h)


def decoder_own_kernel(
    bias_ref, a4_ref, e3_ref, wu3_ref, w3_in, wu2_in, e2_in,
    h2_out, taps2_out, edge_h_out, edge_taps_out,
    h3_ref, taps3_ref, w3_ref, wu2_ref, e2_ref, h2_ref, taps2_ref, sems, sems2,
    *, size,
):
    rows4, rows3 = a4_ref.shape[0], e3_ref.shape[0]
    fetch = Fetch(
        sems, w3=(w3_in, w3_ref), wu2=(wu2_in, wu2_ref), e2=(e2_in.at[pl.ds(4, 2 * rows3 - 4)], e2_ref)
    )
    mean2, mean3 = mean_matrix(128), mean_matrix(256)

    def third(i, count):
        def put(j, h, u):
            h3_ref[2 * i + j] = h
            put_taps(taps3_ref, 2 * i + j, u, 256)

        up3(a4_ref[pl.ds(i, count)], e3_ref[pl.ds(2 * i, 2 * count)], put, wu3_ref, bias_ref[4:5, :], mean3, size)

    loop_chunks(rows4, 4, third)

    edges = []
    for side, at in ((0, 0), (1, rows3 - 2)):
        edges.append(
            pltpu.make_async_copy(taps3_ref.at[pl.ds(at, 2)], edge_taps_out.at[pl.ds(2 * side, 2)], sems.at[3 + side])
        )
        edges.append(
            pltpu.make_async_copy(h3_ref.at[pl.ds(at + side, 1)], edge_h_out.at[pl.ds(side, 1)], sems.at[5 + side])
        )
    for copy in edges:
        copy.start()
    chunk = divisor(rows3 - 2, 7)

    def leave(o):
        part = pl.ds(2 * o, 2 * chunk)
        return [
            pltpu.make_async_copy(h2_ref.at[part], h2_out.at[part], sems2.at[o // chunk, 0]),
            pltpu.make_async_copy(taps2_ref.at[part], taps2_out.at[part], sems2.at[o // chunk, 1]),
        ]

    def second(o, count):
        def put(j, h, u):
            h2_ref[2 * o + j] = h
            put_taps(taps2_ref, 2 * o + j, u, 128)

        acc = conv(taps3_ref, o, count, 768, w3_ref)
        up2(h3_ref[pl.ds(o + 1, count)], acc, lambda j: e2_ref[2 * o + j], put, wu2_ref, bias_ref[5:6, :], mean2, size)

        for copy in leave(o):
            copy.start()

    fetch.wait("w3", "wu2", "e2")
    loop((rows3 - 2) // chunk, lambda c: second(c * chunk, chunk))
    for copy in edges:
        copy.wait()
    for c in range((rows3 - 2) // chunk):
        for copy in leave(c * chunk):
            copy.wait()


def decoder_own(biases, a4, e3, e2, wu3, w3, wu2, size):
    rows3 = e3.shape[0]
    inner = 2 * (rows3 - 2)
    out = pltpu.VMEM
    inside = pl.BlockSpec(memory_space=pltpu.VMEM)
    return pl.pallas_call(
        functools.partial(decoder_own_kernel, size=size),
        name="decoder_own",
        in_specs=[inside] * 4 + [ANYWHERE] * 3,
        out_specs=[ANYWHERE] * 4,
        out_shape=[
            jax.ShapeDtypeStruct((inner, size, 512), BF),
            jax.ShapeDtypeStruct((inner, 6, size, 128), BF),
            jax.ShapeDtypeStruct((2, size, 512), BF),
            jax.ShapeDtypeStruct((4, 8, size, 128), BF),
        ],
        scratch_shapes=[
            out((rows3, size, 512), BF),
            out((rows3, 8, size, 128), BF),
            out(w3.shape, BF),
            out(wu2.shape, BF),
            out((2 * rows3 - 4, size, 512), BF),
            out((inner, size, 512), BF),
            out((inner, 6, size, 128), BF),
            pltpu.SemaphoreType.DMA((7,)),
            pltpu.SemaphoreType.DMA(((rows3 - 2) // divisor(rows3 - 2, 7), 2)),
        ],
    )(biases, near(a4), e3, wu3, w3, wu2, e2)


def decoder_kernel(
    factors, bias_ref, top_ref, bot_ref, edge_h_ref, edge_taps_ref, wu1_ref, w2_ref, w1_ref, wh_ref,
    wu3_in, h2_own_ref, taps2_own_ref, e2_in, w3_in, wu2_in, e1_edge_in, e1_own_in, noisy_in, noise_in,
    out_ref,
    h3_ref, taps3_ref, h2_ref, taps2_ref, h1_ref, taps1_ref, turn_ref,
    wu3_ref, e2_ref, w3_ref, wu2_ref, e1_edge_ref, e1_own_ref, conv2_ref, conv1_ref, head_ref, g_ref, noisy_ref, noise_ref, sems,
    *, n, size, rows1, lat,
):
    rows2 = rows1 // 2
    inner = rows2 - 4
    step = pl.program_id(0)
    last = pl.num_programs(0) - 2

    def prepare():
        fetch = Fetch(
            sems,
            wu3=(wu3_in, wu3_ref),
            w3=(w3_in, w3_ref),
            e2a=(e2_in.at[pl.ds(0, 4)], e2_ref.at[pl.ds(0, 4)]),
            e2b=(e2_in.at[pl.ds(rows2, 4)], e2_ref.at[pl.ds(4, 4)]),
            wu2=(wu2_in, wu2_ref),
            h2=(h2_own_ref, h2_ref.at[pl.ds(4, inner)]),
            taps2=(taps2_own_ref, taps2_ref.at[pl.ds(4, inner)]),
            e1_edge=(e1_edge_in, e1_edge_ref),
            e1_own=(e1_own_in, e1_own_ref),
            noisy=(noisy_in, noisy_ref),
            noise=(noise_in, noise_ref),
        )
        flags = ends(lat)
        fill_conv1(conv1_ref, w1_ref)
        fill_conv2(conv2_ref, w2_ref)
        fill_head(head_ref, wh_ref)
        fetch.wait("wu3")
        mean1, mean2, mean3 = mean_matrix(64), mean_matrix(128), mean_matrix(256)
        bias3, bias2, bias1 = bias_ref[4:5, :], bias_ref[5:6, :], bias_ref[6:7, :]

        for side, ref in ((0, top_ref), (1, bot_ref)):
            at = 0 if side == 0 else 6

            def put3(j, h, u, at=at, side=side):
                if j == 1 - side:
                    h3_ref[3 * side] = h
                put_taps(taps3_ref, at + j, u, 256)

            up3(ref[0:1], ref[1:3], put3, wu3_ref, bias3, mean3, size, flags[side])
            own = 2 if side == 0 else 4
            taps3_ref[own : own + 2] = edge_taps_ref[2 * side : 2 * side + 2]
            h3_ref[1 + side] = edge_h_ref[side]

        rows = [jnp.concatenate([taps3_ref[a : a + 2], taps3_ref[4 + a : 6 + a]], axis=0) for a in range(3)]

        def place2(j):
            return j if j < 4 else rows2 + j - 4

        def put2(j, h, u):
            if j < 2:
                u = u * flags[0]
            if j >= 6:
                u = u * flags[1]
            h2_ref[place2(j)] = h
            put_taps(taps2_ref, place2(j), u, 128)

        fetch.wait("w3", "wu2", "e2a", "e2b")
        up2(h3_ref[...], conv_rows(rows, 768, w3_ref), lambda j: e2_ref[j], put2, wu2_ref, bias2, mean2, size)
        fetch.wait("h2", "taps2", "e1_edge")

        rows = [jnp.concatenate([taps2_ref[a : a + 2], taps2_ref[rows2 + a : rows2 + a + 2]], axis=0) for a in range(3)]
        prior = jnp.concatenate([h2_ref[1:3], h2_ref[rows2 + 1 : rows2 + 3]], axis=0)

        def lay(ro, k, factor=None):
            u = activate(h1_ref[ro, k].astype(F32), bias1, mean1)
            put_taps1(taps1_ref, ro, k, u if factor is None else u * factor)

        def put1(j, ro, h):
            h1_ref[ro, j if j < 2 else rows2 + j - 2] = h

        acc = conv_rows(rows, 512, conv2_ref)
        up1(prior, acc, lambda j, ro: e1_edge_ref[ro, j], put1, wu1_ref, size)

        def first(i, count):
            def put(j, ro, h):
                h1_ref[ro, i + 2 + j] = h

            acc = conv(taps2_ref, i + 2, count, 512, conv2_ref)
            up1(h2_ref[pl.ds(i + 3, count)], acc, lambda j, ro: e1_own_ref[ro, i + j], put, wu1_ref, size)

        def behind(i, count):
            for j in range(count):
                for ro in range(2):
                    lay(ro, i + 2 + j)

        chunk = divisor(rows2 - 2, 10)
        steps = (rows2 - 2) // chunk
        inner_chunk = steps // 2

        def order(c):
            return jnp.where(c == 0, inner_chunk, jnp.where(c <= inner_chunk, c - 1, c))

        fetch.wait("e1_own")
        first(inner_chunk * chunk, chunk)
        for ro in range(2):
            lay(ro, 0, flags[0])
            lay(ro, 1)
            lay(ro, rows2)
            lay(ro, rows2 + 1, flags[1])

        def both(c):
            behind(order(c - 1) * chunk, chunk)
            first(order(c) * chunk, chunk)

        loop(steps - 1, lambda c: both(c + 1))
        behind(order(steps - 1) * chunk, chunk)
        fetch.wait("noisy", "noise")

    pl.when(step == 0)(prepare)

    spread = dotf(g_ref[...], head_ref[...])
    for p in range(4):
        for s in range(4):
            turn_ref[pl.ds(4 * p + s, n, stride=16), :] = spread[p * size : p * size + n, s * 128 : (s + 1) * 128]
    eps = turn_ref[...].T
    nvars, _, cols = noisy_ref.shape
    for o in range(2):
        part = eps[o * 64 : (o + 1) * 64].reshape(nvars, 8, cols)
        rows = pl.ds(pl.multiple_of(jnp.maximum(step - 1, 0) * 16 + o * 8, 8), 8)
        new = factors[0] * noisy_ref[:, rows, :] - factors[1] * part + factors[2] * noise_ref[:, rows, :]
        out_ref[:, o * 8 : (o + 1) * 8, :] = new

    i = jnp.minimum(step, last) * 4
    acc = conv1(taps1_ref, i, 4, conv1_ref)
    flat = 4 * size
    for p in range(4):
        halves = []
        for ro in range(2):
            prior = h1_ref[ro, pl.ds(i + 1, 4), :, p * 128 : (p + 1) * 128].reshape(flat, 128).astype(F32)
            halves.append((prior + acc[p * flat : (p + 1) * flat, ro * 128 : (ro + 1) * 128]).astype(BF))
        both = jnp.concatenate(halves, axis=1)
        for j in range(4):
            g_ref[p * size : (p + 1) * size, j * 256 : (j + 1) * 256] = both[j * size : (j + 1) * size]


def decoder(lat_count, factors, biases, top, bot, edge_h, edge_taps, e2, e1_own, e1_edge, weights, h2, taps2, noisy, step_noise, n, size):
    nvars, lat, cols = noisy.shape
    rows1 = lat // 2
    rows2 = rows1 // 2
    field = pl.BlockSpec((nvars, 16, cols), lambda k: (0, jnp.maximum(k - 1, 0), 0))
    smem = pl.BlockSpec(memory_space=pltpu.SMEM)
    inside = pl.BlockSpec(memory_space=pltpu.VMEM)
    vmem = pltpu.VMEM
    wu3, w3, wu2, w2, wu1, w1, wh = weights
    late = [w3, wu2, e1_edge, e1_own]
    return pl.pallas_call(
        functools.partial(decoder_kernel, n=n, size=size, rows1=rows1, lat=lat_count),
        name="decoder",
        grid=(rows1 // 8 + 1,),
        in_specs=[smem] + [inside] * 9 + [ANYWHERE] * 10,
        out_specs=field,
        out_shape=jax.ShapeDtypeStruct(noisy.shape, F32),
        scratch_shapes=[
            vmem((4, size, 512), BF),
            vmem((8, 8, size, 128), BF),
            vmem((rows2 + 4, size, 512), BF),
            vmem((rows2 + 4, 6, size, 128), BF),
            vmem((2, rows2 + 2, size, 512), BF),
            vmem((2, rows2 + 2, 8, size, 128), BF),
            vmem((cols, 128), F32),
            vmem(wu3.shape, BF),
            vmem((8, size, 512), BF),
        ]
        + [vmem(x.shape, BF) for x in late]
        + [vmem((1536, 256), BF), vmem((1024, 256), BF), vmem((1024, 512), BF), vmem((4 * size, 1024), BF)]
        + [vmem(noisy.shape, F32), vmem(noisy.shape, F32), pltpu.SemaphoreType.DMA((11,))],
    )(
        factors, biases, near(top), near(bot), edge_h, edge_taps, wu1, w2, w1.T, wh.T, wu3,
        h2, taps2, e2, *late, noisy, step_noise,
    )


def shift(array, axis, by, closed):
    count = lax.axis_size(axis)
    if closed:
        pairs = [(i, (i + by) % count) for i in range(count)]
    else:
        pairs = [(i, i + by) for i in range(count) if 0 <= i + by < count]
    return lax.ppermute(array, axis, pairs)


def body(
    noisy, coarse, step_noise, timestep, w_time, w_embed, w_enc1, w_down1, w_enc2, w_down2, w_enc3, w_down3,
    w_qkv, w_attn_out, w_up3, w_dec3, w_up2, w_dec2, w_up1, w_dec1, w_head,
):
    nvars, lat, cols = noisy.shape
    n = cols // 16
    size = -(-(n + 2) // 16) * 16
    rows1 = lat // 2
    rows4 = lat // 16
    groups = lax.axis_size("lon")
    lat_count = lax.axis_size("lat")

    wide, left, right = embed_strips(noisy, coarse, w_embed)
    rhalo = shift(left, "lon", -1, True)
    lhalo = shift(right, "lon", 1, True)
    top, mid, bot = embed(noisy, coarse, wide)

    temb = time_embed(timestep, w_time)
    factors = update_factors(timestep)
    widths = [w_enc1.shape[1], w_enc2.shape[1], w_enc3.shape[1], w_qkv.shape[0], w_dec3.shape[1], w_dec2.shape[1], w_dec1.shape[1]]
    starts = [sum(widths[:i]) for i in range(7)]
    biases = jnp.stack(
        [jnp.tile(temb[s : s + w], 512 // w) * (1.0 if i == 3 else 0.5) for i, (s, w) in enumerate(zip(starts, widths))]
    )

    top, bot = add_rims(lhalo, rhalo, top, bot)
    from_top = shift(bot, "lat", 1, False)
    from_bot = shift(top, "lat", -1, False)
    e1_own, d1, taps2, edge_h, edge_taps, conv1_w, conv2_w = encoder_own(
        biases, mid, top, bot, lhalo, rhalo, w_enc1, w_down1, w_enc2, n, size
    )

    copies = max(1, groups // rows4)
    each = max(1, rows4 // groups)
    e1_edge, e2, e3, sent = encoder(
        lat_count, biases, from_top, from_bot, edge_h, edge_taps,
        (conv1_w, w_down1, conv2_w, w_down2, w_enc3, w_down3), d1, taps2, n, size, rows1, (groups, each, copies),
    )
    got = lax.all_to_all(sent, "lon", split_axis=0, concat_axis=0, tiled=True)
    out, e3 = attention(got, biases, e3, w_qkv, w_attn_out, n, size, each)
    a4 = lax.all_to_all(out.reshape(groups, each * size, 512), "lon", split_axis=0, concat_axis=0, tiled=True)
    a4 = a4.reshape(groups * each, size, 512)
    if copies > 1:
        a4 = a4.reshape(rows4, copies, size, 512)[:, 0]

    top = shift(jnp.concatenate([a4[-1:], e3[-2:]]), "lat", 1, False)
    bot = shift(jnp.concatenate([a4[:1], e3[:2]]), "lat", -1, False)
    h2, taps2, edge_h, edge_taps = decoder_own(biases, a4, e3, e2, w_up3, w_dec3, w_up2, size)
    return decoder(
        lat_count, factors, biases, top, bot, edge_h, edge_taps, e2, e1_own, e1_edge,
        (w_up3, w_dec3, w_up2, w_dec2, w_up1, w_dec1, w_head), h2, taps2, noisy, step_noise, n, size,
    )


def solution(mesh):
    field = P(None, "lat", "lon")
    return jax.shard_map(
        body, mesh=mesh, in_specs=(field, field, field) + (P(),) * 18, out_specs=field, check_vma=False
    )
```

```python
import functools
import math

import jax
import jax.numpy as jnp
from jax import lax
from jax.experimental import pallas as pl
from jax.experimental.pallas import tpu as pltpu
from jax.sharding import PartitionSpec as P

HEAD_DIM = 64
T_STEPS = 1000
BF = jnp.bfloat16
F32 = jnp.float32
EPS = 1e-06


def plan(step):
    frac = (step.astype(jnp.float32) / T_STEPS + 0.008) / 1.008
    return jnp.cos(frac * (math.pi / 2)) ** 2


def time_embed(timestep, w_time):
    half = w_time.shape[0] // 2
    freqs = jnp.exp(-math.log(10000.0) * jnp.arange(half, dtype=jnp.float32) / half)
    angle = timestep.astype(jnp.float32)[0] * freqs
    feats = jnp.concatenate([jnp.sin(angle), jnp.cos(angle)])[None]
    return jax.nn.silu(jnp.dot(feats, w_time, precision=lax.Precision.HIGHEST))[0]


def update_factors(timestep):
    current_alpha_product = plan(timestep[0])
    abar_prev = plan(timestep[0] - 1)
    beta = jnp.minimum(1.0 - current_alpha_product / abar_prev, 0.999)
    keep = 1.0 / jnp.sqrt(1.0 - beta)
    noise = beta / jnp.sqrt(1.0 - current_alpha_product) * keep
    sigma = jnp.sqrt(beta * (1.0 - abar_prev) / (1.0 - current_alpha_product))
    return jnp.stack([keep, noise, sigma])


def iota(shape, dim):
    return lax.broadcasted_iota(jnp.int32, shape, dim)


def dotf(a, b):
    return jnp.dot(a, b, preferred_element_type=F32)


def dot_tn(a, b):
    return lax.dot_general(a, b, (((0,), (0,)), ((), ())), preferred_element_type=F32)


def ends(count_of_lat):
    at = lax.axis_index("lat")
    return [jnp.where(at > 0, 1.0, 0.0), jnp.where(at < count_of_lat - 1, 1.0, 0.0)]


def mean_matrix(chans):
    size = 256
    same = (iota((size, size), 0) & -chans) == (iota((size, size), 1) & -chans)
    return jnp.where(same, 4.0 / chans, 0.0).astype(BF)


def activate(x, bias, mean):
    squares = (x * x).astype(BF)
    size = mean.shape[0]
    parts = [dotf(squares[:, i : i + size], mean) for i in range(0, x.shape[1], size)]
    half = x * lax.rsqrt(jnp.concatenate(parts, axis=1) + 4 * EPS) + bias
    return half + half * jnp.tanh(half)


def row_factor(index, low, high, flags):
    return jnp.where(index < low, flags[0], jnp.where(index >= high, flags[1], 1.0))


def put_taps1(ref, parity, k, u):
    size = u.shape[0]
    pairs = [u[:, p * 128 : (p + 1) * 128] for p in range(4)]
    first = iota((size, 128), 1) < 64
    after = pairs[1:] + [pltpu.roll(pairs[0], size - 1, 0)]
    before = [pltpu.roll(pairs[3], 1, 0)] + pairs[:3]
    for p in range(4):
        ref[parity, k, 2 * p] = pairs[p].astype(BF)
        ref[parity, k, 2 * p + 1] = jnp.where(first, after[p], before[p]).astype(BF)


def put_taps(ref, k, u, chans):
    size, lanes = u.shape
    parts = [u[:, i : i + 128] for i in range(0, lanes, 128)]
    edge = chans // 128
    around = (
        [pltpu.roll(x, 1, 0) for x in parts[-edge:]] + parts + [pltpu.roll(x, size - 1, 0) for x in parts[:edge]]
    )
    for i, part in enumerate(around):
        ref[k, i] = part.astype(BF)


def lanes_of(rows, first, last):
    count, _, size, _ = rows.shape
    return [rows[:, b].reshape(count * size, 128) for b in range(first, last)]


def fill_conv1(out_ref, w_ref):
    chans = w_ref.shape[0]
    twice = jnp.where((iota((chans, 128), 1) & 63) == iota((chans, 128), 0), 1.0, 0.0).astype(BF)
    wide = dot_tn(w_ref[...], twice)
    left = iota((chans, 128), 1) < 64
    zero = jnp.zeros((chans, 128), F32)
    for t in range(4):
        for ro in range(2):
            a = t - ro
            for j, dx in enumerate((0, 1, 2, -1)):
                halves = []
                for co in range(2):
                    b = dx - co + 1
                    good = 0 <= a < 3 and 0 <= b < 3
                    halves.append(wide[(a * 3 + b) * chans : (a * 3 + b + 1) * chans] if good else zero)
                value = jnp.where(left, halves[0], halves[1]).astype(BF)
                row = t * 256 + j * 64
                out_ref[row : row + 64, ro * 128 : (ro + 1) * 128] = value


def fill_conv2(out_ref, w_ref):
    zero = jnp.zeros((128, 128), BF)
    for a in range(3):
        part = w_ref[a * 384 : (a + 1) * 384, :]
        out_ref[a * 512 : a * 512 + 384, 0:128] = part
        out_ref[a * 512 + 384 : (a + 1) * 512, 0:128] = zero
        out_ref[a * 512 : a * 512 + 128, 128:256] = zero
        out_ref[a * 512 + 128 : (a + 1) * 512, 128:256] = part


def conv1(taps_ref, i, count, w_ref):
    rows = [
        taps_ref[1, pl.ds(i, count)],
        taps_ref[0, pl.ds(i + 1, count)],
        taps_ref[1, pl.ds(i + 1, count)],
        taps_ref[0, pl.ds(i + 2, count)],
    ]
    lhs = [jnp.concatenate([x for r in rows for x in lanes_of(r, 2 * p, 2 * p + 2)], axis=1) for p in range(4)]
    return dotf(jnp.concatenate(lhs, axis=0), w_ref[...])


def conv_rows(rows, reach, w_ref):
    lhs = [
        jnp.concatenate([x for r in rows for x in lanes_of(r, 2 * q, 2 * q + reach // 128)], axis=1) for q in range(2)
    ]
    return dotf(jnp.concatenate(lhs, axis=0), w_ref[...])


def conv(taps_ref, o, count, reach, w_ref):
    return conv_rows([taps_ref[pl.ds(o + a, count)] for a in range(3)], reach, w_ref)


def loop(count, body):
    def step(i, carry):
        body(i)
        return carry

    lax.fori_loop(0, count, step, 0)


def divisor(total, most):
    return max(d for d in range(1, most + 1) if total % d == 0)


def loop_chunks(total, chunk, body):
    chunk = min(chunk, total)
    steps = -(-total // chunk)
    loop(steps, lambda c: body(jnp.minimum(c * chunk, total - chunk), chunk))


def fill_embed(out_ref, w_ref):
    feats, chans = w_ref.shape
    twice = jnp.where((iota((chans, 128), 1) & 63) == iota((chans, 128), 0), 1.0, 0.0).astype(BF)
    wide = dotf(w_ref[...], twice).astype(BF)
    k = iota((512, feats), 0)
    source = ((k >> 3) & 15) * 4 + (k & 1) * 2 + ((k >> 7) & 1)
    pick = jnp.where(source == iota((512, feats), 1), 1.0, 0.0).astype(BF)
    wide = dotf(pick, wide)
    k = iota((512, 128), 0)
    right = iota((512, 128), 1) >= 64
    same_cell = right == ((k >> 8) == 1)
    for i in range(4):
        keep = same_cell & (((k & 7) >> 1) == i)
        out_ref[:, i * 128 : (i + 1) * 128] = jnp.where(keep, wide, 0.0).astype(BF)


def embed_rows(fields, w_ref, turn_ref, slot):
    n = fields[0].shape[1] // 16
    turn_ref[slot] = jnp.concatenate(fields, axis=0).T
    lhs = [
        jnp.concatenate([turn_ref[slot, pl.ds(4 * p + s, n, stride=16), :] for s in range(4)], axis=1)
        for p in range(4)
    ]
    res = dotf(jnp.concatenate(lhs, axis=0).astype(BF), w_ref[...])
    return [
        jnp.concatenate([res[p * n : (p + 1) * n, i * 128 : (i + 1) * 128] for p in range(4)], axis=1)
        for i in range(4)
    ]


def strips_kernel(w_ref, nl_ref, cl_ref, nr_ref, cr_ref, wide_ref, left_ref, right_ref, turn_ref, strip_ref):
    fill_embed(wide_ref, w_ref)
    octets = nl_ref.shape[1] // 8
    first = iota((64, 128), 1) < 64
    for o in range(octets):
        rows = slice(o * 8, (o + 1) * 8)
        block = jnp.concatenate(
            [
                jnp.where(first, a[:, rows, :].reshape(64, 128), b[:, rows, :].reshape(64, 128))
                for a, b in ((nl_ref, nr_ref), (cl_ref, cr_ref))
            ],
            axis=0,
        ).T
        turn_ref[0, o * 16 : (o + 1) * 16, :] = block[:16]
        turn_ref[1, o * 16 : (o + 1) * 16, :] = block[112:]
    lhs = [
        jnp.concatenate([turn_ref[side, pl.ds(4 * p + s, octets, stride=16), :] for s in range(4)], axis=1)
        for side in range(2)
        for p in range(4)
    ]
    res = dotf(jnp.concatenate(lhs, axis=0).astype(BF), wide_ref[...])
    for side, out_ref in ((0, left_ref), (1, right_ref)):
        for p in range(4):
            at = (side * 4 + p) * octets
            for i in range(4):
                strip_ref[p, pl.ds(i, octets, stride=4), :] = res[at : at + octets, i * 128 : (i + 1) * 128]
        for p in range(4):
            out_ref[:, p * 128 : (p + 1) * 128] = strip_ref[p].astype(BF)


def embed_kernel(wide_ref, noisy_in, coarse_in, top_out, mid_out, bot_out, x_ref, turn_ref, e0_ref, sems, out_sems):
    _, nvars, rows, cols = x_ref.shape
    n = cols // 16
    chunks = rows // 16

    def reads(c):
        part = pl.ds(pl.multiple_of(16 * c, 16), 16)
        return [
            pltpu.make_async_copy(source.at[:, part, :], x_ref.at[t, :, part, :], sems.at[c, t])
            for t, source in enumerate((noisy_in, coarse_in))
        ]

    def write(c, out, place):
        part = pl.ds(pl.multiple_of(c * 8 * n, 8 * n), 8 * n)
        to = pl.ds(pl.multiple_of(place * 8 * n, 8 * n), 8 * n)
        return pltpu.make_async_copy(e0_ref.at[part], out.at[to], out_sems.at[c])

    def writes(c):
        return write(c, top_out, 0) if c == 0 else write(c, bot_out, 0) if c == chunks - 1 else write(c, mid_out, c - 1)

    for c in range(chunks):
        for copy in reads(c):
            copy.start()

    def chunk(c):
        for copy in reads(c):
            copy.wait()
        out = []
        for o in range(2):
            at = pl.ds(pl.multiple_of(16 * c + 8 * o, 8), 8)
            fields = [x_ref[t, :, at, :].reshape(8 * nvars, cols) for t in range(2)]
            out += embed_rows(fields, wide_ref, turn_ref, o)
        e0_ref[pl.ds(pl.multiple_of(c * 8 * n, 8 * n), 8 * n), :] = jnp.concatenate(out, axis=0).astype(BF)

        @pl.when((c > 0) & (c < chunks - 1))
        def _():
            write(c, mid_out, c - 1).start()

    loop(chunks, chunk)
    for c in (0, chunks - 1):
        writes(c).start()
    for c in range(chunks):
        writes(c).wait()


def rims_kernel(left_ref, right_ref, top_in, bot_in, top_out, bot_out, rim_ref, sems):
    count = left_ref.shape[0]
    at = top_out.shape[0] - 16
    copies = []
    for k, out in ((0, top_out), (1, bot_out)):
        rows = slice(0, 16) if k == 0 else slice(count - 16, count)
        pick = slice(0, 8) if k == 0 else slice(8, 16)
        rim_ref[k] = jnp.concatenate([r[rows, :].astype(F32)[pick] for r in (left_ref, right_ref)], axis=0).astype(BF)
        copies.append(pltpu.make_async_copy(rim_ref.at[k], out.at[pl.ds(at, 16)], sems.at[k]))
        copies[-1].start()
    for copy in copies:
        copy.wait()


def near(array):
    return pltpu.with_memory_space_constraint(array, pltpu.VMEM)


ANYWHERE = pl.BlockSpec(memory_space=pl.ANY)


class Fetch:
    def __init__(self, sems, **pairs):
        self.copies = {name: pltpu.make_async_copy(src, dst, sems.at[i]) for i, (name, (src, dst)) in enumerate(pairs.items())}
        for copy in self.copies.values():
            copy.start()

    def wait(self, *names):
        for name in names:
            self.copies[name].wait()


def whole(shape):
    return pl.BlockSpec(shape, lambda *_: (0,) * len(shape))


def embed_strips(noisy, coarse, w_embed):
    nvars, rows, cols = noisy.shape
    sides = [pl.BlockSpec((nvars, rows, 128), lambda k: (0, 0, 0)), pl.BlockSpec((nvars, rows, 128), lambda k: (0, 0, cols // 128 - 1))]
    strip = jax.ShapeDtypeStruct((rows // 2, 512), BF)
    return pl.pallas_call(
        strips_kernel,
        name="embed_strips",
        grid=(1,),
        in_specs=[whole(w_embed.shape), sides[0], sides[0], sides[1], sides[1]],
        out_specs=[whole((512, 512)), whole(strip.shape), whole(strip.shape)],
        out_shape=[jax.ShapeDtypeStruct((512, 512), BF), strip, strip],
        scratch_shapes=[pltpu.VMEM((2, rows * 2, 128), F32), pltpu.VMEM((4, rows // 2, 128), F32)],
    )(w_embed, noisy, coarse, noisy, coarse)


def embed(noisy, coarse, wide):
    nvars, rows, cols = noisy.shape
    n = cols // 16
    pay = jax.ShapeDtypeStruct((8 * n + 16, 512), BF)
    return pl.pallas_call(
        embed_kernel,
        name="embed",
        in_specs=[pl.BlockSpec(memory_space=pltpu.VMEM), ANYWHERE, ANYWHERE],
        out_specs=[ANYWHERE] * 3,
        out_shape=[pay, jax.ShapeDtypeStruct(((rows // 2 - 16) * n, 512), BF), pay],
        scratch_shapes=[
            pltpu.VMEM((2, nvars, rows, cols), F32),
            pltpu.VMEM((2, cols, 128), F32),
            pltpu.VMEM((rows // 2 * n, 512), BF),
            pltpu.SemaphoreType.DMA((rows // 16, 2)),
            pltpu.SemaphoreType.DMA((rows // 16,)),
        ],
    )(wide, noisy, coarse)


def add_rims(left, right, top, bot):
    inside = pl.BlockSpec(memory_space=pltpu.VMEM)
    return pl.pallas_call(
        rims_kernel,
        name="rims",
        in_specs=[inside, inside, ANYWHERE, ANYWHERE],
        out_specs=[ANYWHERE] * 2,
        out_shape=[jax.ShapeDtypeStruct(top.shape, BF)] * 2,
        scratch_shapes=[pltpu.VMEM((2, 16, 512), BF), pltpu.SemaphoreType.DMA((2,))],
        input_output_aliases={2: 0, 3: 1},
    )(near(left), near(right), top, bot)


def full_rows(x, left, right, n, size):
    tail = size - n
    place = iota((tail, 512), 0)
    full = []
    for j in range(x.shape[0] // n):
        rim = jnp.where(place == 0, right[j], jnp.where(place == tail - 1, left[j], 0.0))
        full += [x[j * n : (j + 1) * n], rim]
    return jnp.concatenate(full, axis=0)


def level1(h_ref, taps_ref, k, h, bias, mean, factor=None):
    size = h_ref.shape[2]
    u = activate(h, bias, mean)
    for j in range(h.shape[0] // size):
        part = u[j * size : (j + 1) * size]
        h_ref[j % 2, k + j // 2] = h[j * size : (j + 1) * size].astype(BF)
        put_taps1(taps_ref, j % 2, k + j // 2, part if factor is None else part * factor)


def enc_conv1(taps_ref, h_ref, i, count, conv_ref, wd_ref, store):
    size = taps_ref.shape[3]
    acc = conv1(taps_ref, i, count, conv_ref)
    flat = count * size
    merged = []
    for p in range(4):
        halves = []
        for ro in range(2):
            lanes = slice(p * 128, (p + 1) * 128)
            prior = h_ref[ro, pl.ds(i + 1, count), :, lanes].reshape(flat, 128).astype(F32)
            e = (prior + acc[p * flat : (p + 1) * flat, ro * 128 : (ro + 1) * 128]).astype(BF)
            store(ro, lanes, e.reshape(count, size, 128))
            halves.append(e)
        merged.append(jnp.concatenate(halves, axis=1))
    d = dotf(jnp.concatenate(merged, axis=0), wd_ref[...]).astype(BF)
    return jnp.concatenate([d[p * flat : (p + 1) * flat] for p in range(4)], axis=1)


def encoder_own_kernel(
    bias_ref, mid_ref, top_ref, bot_ref, lhalo_ref, rhalo_ref, w1_ref, wd1_ref, w2_ref,
    e1_out, d1_out, taps2_out, edge_h_out, edge_taps_out, conv1_out, conv2_out,
    lf_ref, rf_ref, h1_ref, taps1_ref, e1_ref, d1_ref, taps2_ref, conv1_ref, conv2_ref, sem, sems,
    *, n, size,
):
    fill_conv1(conv1_ref, w1_ref)
    fill_conv2(conv2_ref, w2_ref)
    weights_out = Fetch(sems, conv1=(conv1_ref, conv1_out), conv2=(conv2_ref, conv2_out))
    lf_ref[...] = lhalo_ref[...].astype(F32)
    rf_ref[...] = rhalo_ref[...].astype(F32)
    mean1, mean2 = mean_matrix(64), mean_matrix(128)
    rows1 = lhalo_ref.shape[0]

    def first(x, row):
        left = [lf_ref[pl.ds(row + j, 1), :] for j in range(4)]
        right = [rf_ref[pl.ds(row + j, 1), :] for j in range(4)]
        k = row // 2
        level1(h1_ref, taps1_ref, k, full_rows(x.astype(F32), left, right, n, size), bias_ref[0:1, :], mean1)

    def first_at(row):
        if row < 8:
            first(top_ref[row * n : (row + 4) * n, :], row)
        elif row < rows1 - 8:
            first(mid_ref[(row - 8) * n : (row - 4) * n, :], row)
        else:
            at = row - rows1 + 8
            first(bot_ref[at * n : (at + 4) * n, :], row)

    def second(i, count):
        def store(ro, lanes, e):
            e1_ref[ro, pl.ds(i, count), :, lanes] = e

        d = enc_conv1(taps1_ref, h1_ref, i, count, conv1_ref, wd1_ref, store)
        d1_ref[pl.ds(i, count)] = d.reshape(count, size, 512)
        u = activate(d.astype(F32), bias_ref[1:2, :], mean2)
        for j in range(count):
            put_taps(taps2_ref, i + j, u[j * size : (j + 1) * size], 128)
        for copy in leave(i):
            copy.start()

    chunk = divisor(rows1 // 2 - 2, 10)
    steps = (rows1 // 2 - 2) // chunk

    def leave(i):
        part = pl.ds(i, chunk)
        slot = i // chunk
        return [
            pltpu.make_async_copy(e1_ref.at[0, part], e1_out.at[0, part], sem.at[slot, 0]),
            pltpu.make_async_copy(e1_ref.at[1, part], e1_out.at[1, part], sem.at[slot, 1]),
            pltpu.make_async_copy(d1_ref.at[part], d1_out.at[part], sem.at[slot, 2]),
            pltpu.make_async_copy(taps2_ref.at[part], taps2_out.at[part], sem.at[slot, 3]),
        ]

    done = 0
    for c in range(steps + 1):
        need = rows1 if c == steps else min(rows1, -(-(2 * chunk * (c + 1) + 3) // 4) * 4)
        while done < need:
            first_at(done)
            done += 4
        if c:
            second((c - 1) * chunk, chunk)
    edges = []
    for side, k in ((0, 0), (1, rows1 // 2 - 2)):
        for t, (source, out) in enumerate(((h1_ref, edge_h_out), (taps1_ref, edge_taps_out))):
            for ro in range(2):
                copy = pltpu.make_async_copy(
                    source.at[ro, pl.ds(k, 2)], out.at[ro, pl.ds(2 * side, 2)], sems.at[2 + 4 * side + 2 * t + ro]
                )
                copy.start()
                edges.append(copy)
    weights_out.wait("conv1", "conv2")
    for copy in edges:
        copy.wait()
    for c in range(steps):
        for copy in leave(c * chunk):
            copy.wait()


def encoder_own(biases, mid, top, bot, lhalo, rhalo, w1, wd1, w2, n, size):
    rows1 = lhalo.shape[0]
    inner = rows1 // 2 - 2
    vmem = pltpu.VMEM
    inside = pl.BlockSpec(memory_space=pltpu.VMEM)
    return pl.pallas_call(
        functools.partial(encoder_own_kernel, n=n, size=size),
        name="encoder_own",
        in_specs=[inside] * 9,
        out_specs=[ANYWHERE] * 7,
        out_shape=[
            jax.ShapeDtypeStruct((2, inner, size, 512), BF),
            jax.ShapeDtypeStruct((inner, size, 512), BF),
            jax.ShapeDtypeStruct((inner, 6, size, 128), BF),
            jax.ShapeDtypeStruct((2, 4, size, 512), BF),
            jax.ShapeDtypeStruct((2, 4, 8, size, 128), BF),
            jax.ShapeDtypeStruct((1024, 256), BF),
            jax.ShapeDtypeStruct((1536, 256), BF),
        ],
        scratch_shapes=[
            vmem((rows1, 512), F32),
            vmem((rows1, 512), F32),
            vmem((2, rows1 // 2, size, 512), BF),
            vmem((2, rows1 // 2, 8, size, 128), BF),
            vmem((2, inner, size, 512), BF),
            vmem((inner, size, 512), BF),
            vmem((inner, 6, size, 128), BF),
            vmem((1024, 256), BF),
            vmem((1536, 256), BF),
            pltpu.SemaphoreType.DMA((inner // divisor(inner, 10), 4)),
            pltpu.SemaphoreType.DMA((10,)),
        ],
    )(biases, mid, top, bot, near(lhalo), near(rhalo), w1.T, wd1, w2)


def encoder_kernel(
    bias_ref, top_ref, bot_ref, wd1_ref,
    edge_h_ref, edge_taps_ref, conv1_in, conv2_in, d1_own_ref, taps2_own_ref, wd2_in, w3_in, wd3_in,
    e1_ref, e2_out, e3_out, send_ref,
    h1_ref, taps1_ref, d1_ref, taps2_ref, d2_ref, taps3_ref, d3_ref, edge_ref,
    conv1_ref, conv2_ref, wd2_ref, w3_ref, wd3_ref, e2_ref, e3_ref, sems, sems2, sems3,
    *, n, size, rows1, sent, lat,
):
    flags = ends(lat)
    rows2, rows3 = rows1 // 2, rows1 // 4
    inner = rows2 - 2
    fetch = Fetch(
        sems,
        **{
            f"{name}{side}{ro}": (
                source.at[ro, pl.ds(2 * side, 2)],
                target.at[ro, pl.ds(4 if side == 0 else 6, 2)],
            )
            for name, source, target in (("h", edge_h_ref, h1_ref), ("t", edge_taps_ref, taps1_ref))
            for side in range(2)
            for ro in range(2)
        },
        conv1=(conv1_in, conv1_ref),
        conv2=(conv2_in, conv2_ref),
        d1=(d1_own_ref, d1_ref.at[pl.ds(4, inner)]),
        taps2=(taps2_own_ref, taps2_ref.at[pl.ds(4, inner)]),
        wd2=(wd2_in, wd2_ref),
        w3=(w3_in, w3_ref),
        wd3=(wd3_in, wd3_ref),
    )
    mean1, mean2, mean3 = mean_matrix(64), mean_matrix(128), mean_matrix(256)

    for side, ref in ((0, top_ref), (1, bot_ref)):
        base = 6 * side
        rims = ref[8 * n :, :].astype(F32)
        x = ref[0 : 8 * n, :].astype(F32)
        left = [rims[j : j + 1] for j in range(8)]
        right = [rims[8 + j : 9 + j] for j in range(8)]
        at = base if side == 0 else base + 2
        level1(h1_ref, taps1_ref, at, full_rows(x, left, right, n, size), bias_ref[0:1, :], mean1, flags[side])

    fetch.wait("conv1", *(f"{name}{side}{ro}" for name in "ht" for side in range(2) for ro in range(2)))
    for side in range(2):

        def store(ro, lanes, e, side=side):
            keep = slice(2, 4) if side == 0 else slice(0, 2)
            e1_ref[ro, 2 * side : 2 * side + 2, :, lanes] = e[keep]

        d = enc_conv1(taps1_ref, h1_ref, 6 * side, 4, conv1_ref, wd1_ref, store)
        at = 0 if side == 0 else rows2 + 2
        d1_ref[at : at + 4] = d.reshape(4, size, 512)
        u = activate(d.astype(F32), bias_ref[1:2, :], mean2)
        for j in range(4):
            inside = j == 3 if side == 0 else j == 0
            part = u[j * size : (j + 1) * size]
            put_taps(taps2_ref, at + j, part if inside else part * flags[side], 128)

    fetch.wait("conv2", "d1", "taps2", "wd2")
    chunk2, chunk3 = divisor(rows3 + 2, 9), divisor(rows3 // 2, 8)

    def leave2(i):
        part = pl.ds(2 * i, 2 * chunk2)
        return pltpu.make_async_copy(e2_ref.at[part], e2_out.at[part], sems2.at[i // chunk2])

    def leave3(i):
        part = pl.ds(2 * i, 2 * chunk3)
        return pltpu.make_async_copy(e3_ref.at[part], e3_out.at[part], sems3.at[i // chunk3])

    def third(i, count2):
        o = 2 * i
        acc = conv(taps2_ref, o, 2 * count2, 512, conv2_ref)
        flat = 2 * count2 * size
        merged = []
        for q in range(2):
            lanes = slice(q * 256, (q + 1) * 256)
            prior = d1_ref[pl.ds(o + 1, 2 * count2), :, lanes].reshape(flat, 256).astype(F32)
            e = (prior + acc[q * flat : (q + 1) * flat]).astype(BF).reshape(2 * count2, size, 256)
            e2_ref[pl.ds(o, 2 * count2), :, lanes] = e
            for j in range(count2):
                merged.append(jnp.concatenate([e[2 * j], e[2 * j + 1]], axis=1))
        d = dotf(jnp.concatenate(merged, axis=0), wd2_ref[...]).astype(BF)
        d = jnp.concatenate([d[: flat // 2], d[flat // 2 :]], axis=1)
        d2_ref[pl.ds(i, count2)] = d.reshape(count2, size, 512)
        u = activate(d.astype(F32), bias_ref[2:3, :], mean3)
        for j in range(count2):
            put_taps(taps3_ref, i + j, u[j * size : (j + 1) * size] * row_factor(i + j, 1, rows3 + 1, flags), 256)
        leave2(i).start()

    loop((rows3 + 2) // chunk2, lambda c: third(c * chunk2, chunk2))
    fetch.wait("w3", "wd3")

    def fourth(i, count3):
        o = 2 * i
        acc = conv(taps3_ref, o, 2 * count3, 768, w3_ref)
        flat = 2 * count3 * size
        acc = jnp.concatenate([acc[:flat], acc[flat:]], axis=1)
        e = (d2_ref[pl.ds(o + 1, 2 * count3)].reshape(flat, 512).astype(F32) + acc).astype(BF)
        wide = e.astype(F32)
        for j in range(2 * count3):
            edge_ref[0, pl.ds(o + j, 1), :] = wide[j * size : j * size + 1]
            edge_ref[1, pl.ds(o + j, 1), :] = wide[j * size + n - 1 : j * size + n]
        e = e.reshape(2 * count3, size, 512)
        e3_ref[pl.ds(o, 2 * count3)] = e
        merged = [jnp.concatenate([e[2 * j], e[2 * j + 1]], axis=1) for j in range(count3)]
        d = dotf(jnp.concatenate(merged, axis=0), wd3_ref[...])
        for j in range(count3):
            d3_ref[i + j] = d[j * size : j * size + n].astype(BF)
        leave3(i).start()

    loop(rows3 // 2 // chunk3, lambda c: fourth(c * chunk3, chunk3))

    left = edge_ref[0].astype(BF)
    right = edge_ref[1].astype(BF)
    groups, each, copies = sent
    before = lax.rem(lax.axis_index("lon") + groups - 1, groups)
    for d in range(groups):
        send_ref[d, 0:rows3, :] = jnp.where(before == d, left, right)
        for e in range(each):
            row = d * each + e if copies == 1 else d // copies
            send_ref[d, rows3 + e * n : rows3 + (e + 1) * n, :] = d3_ref[row]
    for c in range((rows3 + 2) // chunk2):
        leave2(c * chunk2).wait()
    for c in range(rows3 // 2 // chunk3):
        leave3(c * chunk3).wait()


def encoder(lat_count, biases, top, bot, edge_h, edge_taps, weights, d1, taps2, n, size, rows1, sent):
    rows2, rows3 = rows1 // 2, rows1 // 4
    vmem = pltpu.VMEM
    inside = pl.BlockSpec(memory_space=pltpu.VMEM)
    conv1_w, wd1, conv2_w, wd2, w3, wd3 = weights
    return pl.pallas_call(
        functools.partial(encoder_kernel, n=n, size=size, rows1=rows1, sent=sent, lat=lat_count),
        name="encoder",
        in_specs=[inside] * 4 + [ANYWHERE] * 9,
        out_specs=[inside, ANYWHERE, ANYWHERE, inside],
        out_shape=[
            jax.ShapeDtypeStruct((2, 4, size, 512), BF),
            jax.ShapeDtypeStruct((rows2 + 4, size, 512), BF),
            jax.ShapeDtypeStruct((rows3, size, 512), BF),
            jax.ShapeDtypeStruct((sent[0], rows3 + sent[1] * n, 512), BF),
        ],
        scratch_shapes=[
            vmem((2, 12, size, 512), BF),
            vmem((2, 12, 8, size, 128), BF),
            vmem((rows2 + 6, size, 512), BF),
            vmem((rows2 + 6, 6, size, 128), BF),
            vmem((rows3 + 2, size, 512), BF),
            vmem((rows3 + 2, 8, size, 128), BF),
            vmem((rows3 // 2, n, 512), BF),
            vmem((2, rows3, 512), F32),
            vmem(conv1_w.shape, BF),
            vmem(conv2_w.shape, BF),
            vmem(wd2.shape, BF),
            vmem(w3.shape, BF),
            vmem(wd3.shape, BF),
            vmem((rows2 + 4, size, 512), BF),
            vmem((rows3, size, 512), BF),
            pltpu.SemaphoreType.DMA((15,)),
            pltpu.SemaphoreType.DMA(((rows3 + 2) // divisor(rows3 + 2, 9),)),
            pltpu.SemaphoreType.DMA((rows3 // 2 // divisor(rows3 // 2, 8),)),
        ],
    )(
        biases, near(top), near(bot), wd1,
        edge_h, edge_taps, conv1_w, conv2_w, d1, taps2, wd2, w3, wd3,
    )


def attention_kernel(
    x_ref, bias_ref, wqkv_ref, e3_in, wout_in, out_ref, full_ref, mixed_ref, a4_ref, e3_ref, wout_ref, sems,
    *, n, size, each,
):
    fetch = Fetch(sems, e3=(e3_in, e3_ref), wout=(wout_in, wout_ref))
    tail = size - n
    place = iota((tail, 512), 0)
    groups, _, width = x_ref.shape
    length = groups * n
    edge = e3_ref.shape[0]
    scale = HEAD_DIM**-0.5
    for row in range(each):
        at = edge + row * n
        x = jnp.concatenate([x_ref[g, at : at + n, :].astype(F32) for g in range(groups)], axis=0)
        mean = jnp.mean(x * x, axis=1, keepdims=True)
        u = (x * lax.rsqrt(mean + EPS) + bias_ref[3:4, :]).astype(BF)
        qkv = dotf(u, wqkv_ref[...]).astype(BF)
        left = iota((length, 128), 1) < 64
        for h in range(width // 128):
            q = qkv[:, h * 128 : (h + 1) * 128].astype(F32) * scale
            k = qkv[:, width + h * 128 : width + (h + 1) * 128]
            v = qkv[:, 2 * width + h * 128 : 2 * width + (h + 1) * 128]
            outs = []
            for side in range(2):
                mine = left if side == 0 else jnp.logical_not(left)
                qs = jnp.where(mine, q, 0.0).astype(BF)
                s = lax.dot_general(qs, k, (((1,), (1,)), ((), ())), preferred_element_type=F32)
                e = jnp.exp(s - jnp.max(s, axis=1, keepdims=True))
                total = jnp.sum(e, axis=1, keepdims=True)
                outs.append(dotf(e.astype(BF), v) / total)
            mixed_ref[:, h * 128 : (h + 1) * 128] = jnp.where(left, outs[0], outs[1]).astype(BF)
        if row == 0:
            fetch.wait("e3", "wout")
        a4_ref[...] = x + dotf(mixed_ref[...], wout_ref[...])
        for t in range(length // n):
            after = (t * n + n) % length
            before = (t * n - 1) % length
            rim = jnp.where(
                place == 0,
                a4_ref[after : after + 1, :],
                jnp.where(place == tail - 1, a4_ref[before : before + 1, :], 0.0),
            )
            out_ref[t, row] = jnp.concatenate([a4_ref[t * n : (t + 1) * n, :], rim], axis=0).astype(BF)

    here = lax.axis_index("lon")
    lf = x_ref[lax.rem(here + groups - 1, groups), 0:edge, :].astype(F32)
    rf = x_ref[lax.rem(here + 1, groups), 0:edge, :].astype(F32)
    for r in range(edge):
        rim = jnp.where(place == 0, rf[r : r + 1], jnp.where(place == tail - 1, lf[r : r + 1], 0.0))
        full_ref[r] = jnp.concatenate([e3_ref[r, 0:n, :].astype(F32), rim], axis=0).astype(BF)


def attention(x, biases, e3, w_qkv, w_out, n, size, each):
    groups, _, width = x.shape
    length = groups * n
    return pl.pallas_call(
        functools.partial(attention_kernel, n=n, size=size, each=each),
        name="attention",
        in_specs=[pl.BlockSpec(memory_space=pltpu.VMEM)] * 3 + [ANYWHERE] * 2,
        out_shape=[
            jax.ShapeDtypeStruct((groups, each, size, width), BF),
            jax.ShapeDtypeStruct((e3.shape[0], size, width), BF),
        ],
        scratch_shapes=[
            pltpu.VMEM((length, width), BF),
            pltpu.VMEM((length, width), F32),
            pltpu.VMEM(e3.shape, BF),
            pltpu.VMEM(w_out.shape, BF),
            pltpu.SemaphoreType.DMA((2,)),
        ],
    )(near(x), biases, w_qkv, e3, w_out)


def fill_head(out_ref, w_ref):
    outs, chans = w_ref.shape
    col = iota((outs, 512), 1)
    source = ((col >> 3) & 7) * 4 + (col & 1) * 2 + ((col >> 7) & 1)
    pick = jnp.where(source == iota((outs, 512), 0), 1.0, 0.0).astype(BF)
    wide = dot_tn(w_ref[...], pick)
    col = iota((chans, 512), 1)
    for o in range(2):
        for i in range(4):
            for c in range(2):
                keep = (((col >> 6) & 1) == o) & (((col & 7) >> 1) == i) & ((col >> 8) == c)
                row = o * 512 + i * 128 + c * 64
                out_ref[row : row + 64, :] = jnp.where(keep, wide, 0.0).astype(BF)


def up3(a, e, put, wu_ref, bias, mean, size, factor=None):
    spread = dotf(a.reshape(-1, 512), wu_ref[...])
    for j in range(a.shape[0]):
        for ro in range(2):
            part = spread[j * size : (j + 1) * size, ro * 512 : (ro + 1) * 512]
            h = (part + e[2 * j + ro].astype(F32)).astype(BF)
            u = activate(h.astype(F32), bias, mean)
            put(2 * j + ro, h, u if factor is None else u * factor)


def up2(prior, acc, e, put, wu_ref, bias, mean, size):
    count = prior.shape[0]
    flat = count * size
    g = []
    for q in range(2):
        mine = prior[:, :, q * 256 : (q + 1) * 256].reshape(flat, 256).astype(F32)
        g.append((mine + acc[q * flat : (q + 1) * flat]).astype(BF))
    spread = dotf(jnp.concatenate(g, axis=0), wu_ref[...])
    for j in range(count):
        for ro in range(2):
            part = [
                spread[q * flat + j * size : q * flat + (j + 1) * size, ro * 256 : (ro + 1) * 256] for q in range(2)
            ]
            h = (jnp.concatenate(part, axis=1) + e(2 * j + ro).astype(F32)).astype(BF)
            put(2 * j + ro, h, activate(h.astype(F32), bias, mean))


def up1(prior, acc, e, put, wu_ref, size):
    count = prior.shape[0]
    flat = count * size
    g = []
    for q in range(2):
        mine = prior[:, :, q * 256 : (q + 1) * 256].reshape(flat, 256).astype(F32)
        both = (mine + acc[q * flat : (q + 1) * flat]).astype(BF)
        g += [both[:, :128], both[:, 128:]]
    spread = dotf(jnp.concatenate(g, axis=0), wu_ref[...])
    for j in range(count):
        for ro in range(2):
            part = [
                spread[p * flat + j * size : p * flat + (j + 1) * size, ro * 128 : (ro + 1) * 128] for p in range(4)
            ]
            h = (jnp.concatenate(part, axis=1) + e(j, ro).astype(F32)).astype(BF)
            put(j, ro, h)


def decoder_own_kernel(
    bias_ref, a4_ref, e3_ref, wu3_ref, w3_in, wu2_in, e2_in,
    h2_out, taps2_out, edge_h_out, edge_taps_out,
    h3_ref, taps3_ref, w3_ref, wu2_ref, e2_ref, h2_ref, taps2_ref, sems, sems2,
    *, size,
):
    rows4, rows3 = a4_ref.shape[0], e3_ref.shape[0]
    fetch = Fetch(
        sems, w3=(w3_in, w3_ref), wu2=(wu2_in, wu2_ref), e2=(e2_in.at[pl.ds(4, 2 * rows3 - 4)], e2_ref)
    )
    mean2, mean3 = mean_matrix(128), mean_matrix(256)

    def third(i, count):
        def put(j, h, u):
            h3_ref[2 * i + j] = h
            put_taps(taps3_ref, 2 * i + j, u, 256)

        up3(a4_ref[pl.ds(i, count)], e3_ref[pl.ds(2 * i, 2 * count)], put, wu3_ref, bias_ref[4:5, :], mean3, size)

    loop_chunks(rows4, 4, third)

    edges = []
    for side, at in ((0, 0), (1, rows3 - 2)):
        edges.append(
            pltpu.make_async_copy(taps3_ref.at[pl.ds(at, 2)], edge_taps_out.at[pl.ds(2 * side, 2)], sems.at[3 + side])
        )
        edges.append(
            pltpu.make_async_copy(h3_ref.at[pl.ds(at + side, 1)], edge_h_out.at[pl.ds(side, 1)], sems.at[5 + side])
        )
    for copy in edges:
        copy.start()
    chunk = divisor(rows3 - 2, 7)

    def leave(o):
        part = pl.ds(2 * o, 2 * chunk)
        return [
            pltpu.make_async_copy(h2_ref.at[part], h2_out.at[part], sems2.at[o // chunk, 0]),
            pltpu.make_async_copy(taps2_ref.at[part], taps2_out.at[part], sems2.at[o // chunk, 1]),
        ]

    def second(o, count):
        def put(j, h, u):
            h2_ref[2 * o + j] = h
            put_taps(taps2_ref, 2 * o + j, u, 128)

        acc = conv(taps3_ref, o, count, 768, w3_ref)
        up2(h3_ref[pl.ds(o + 1, count)], acc, lambda j: e2_ref[2 * o + j], put, wu2_ref, bias_ref[5:6, :], mean2, size)

        for copy in leave(o):
            copy.start()

    fetch.wait("w3", "wu2", "e2")
    loop((rows3 - 2) // chunk, lambda c: second(c * chunk, chunk))
    for copy in edges:
        copy.wait()
    for c in range((rows3 - 2) // chunk):
        for copy in leave(c * chunk):
            copy.wait()


def decoder_own(biases, a4, e3, e2, wu3, w3, wu2, size):
    rows3 = e3.shape[0]
    inner = 2 * (rows3 - 2)
    out = pltpu.VMEM
    inside = pl.BlockSpec(memory_space=pltpu.VMEM)
    return pl.pallas_call(
        functools.partial(decoder_own_kernel, size=size),
        name="decoder_own",
        in_specs=[inside] * 4 + [ANYWHERE] * 3,
        out_specs=[ANYWHERE] * 4,
        out_shape=[
            jax.ShapeDtypeStruct((inner, size, 512), BF),
            jax.ShapeDtypeStruct((inner, 6, size, 128), BF),
            jax.ShapeDtypeStruct((2, size, 512), BF),
            jax.ShapeDtypeStruct((4, 8, size, 128), BF),
        ],
        scratch_shapes=[
            out((rows3, size, 512), BF),
            out((rows3, 8, size, 128), BF),
            out(w3.shape, BF),
            out(wu2.shape, BF),
            out((2 * rows3 - 4, size, 512), BF),
            out((inner, size, 512), BF),
            out((inner, 6, size, 128), BF),
            pltpu.SemaphoreType.DMA((7,)),
            pltpu.SemaphoreType.DMA(((rows3 - 2) // divisor(rows3 - 2, 7), 2)),
        ],
    )(biases, near(a4), e3, wu3, w3, wu2, e2)


def decoder_kernel(
    factors, bias_ref, top_ref, bot_ref, edge_h_ref, edge_taps_ref, wu1_ref, w2_ref, w1_ref, wh_ref,
    wu3_in, h2_own_ref, taps2_own_ref, e2_in, w3_in, wu2_in, e1_edge_in, e1_own_in, noisy_in, noise_in,
    out_ref,
    h3_ref, taps3_ref, h2_ref, taps2_ref, h1_ref, taps1_ref, turn_ref,
    wu3_ref, e2_ref, w3_ref, wu2_ref, e1_edge_ref, e1_own_ref, conv2_ref, conv1_ref, head_ref, g_ref, noisy_ref, noise_ref, sems,
    *, n, size, rows1, lat,
):
    rows2 = rows1 // 2
    inner = rows2 - 4
    step = pl.program_id(0)
    last = pl.num_programs(0) - 2

    def prepare():
        fetch = Fetch(
            sems,
            wu3=(wu3_in, wu3_ref),
            w3=(w3_in, w3_ref),
            e2a=(e2_in.at[pl.ds(0, 4)], e2_ref.at[pl.ds(0, 4)]),
            e2b=(e2_in.at[pl.ds(rows2, 4)], e2_ref.at[pl.ds(4, 4)]),
            wu2=(wu2_in, wu2_ref),
            h2=(h2_own_ref, h2_ref.at[pl.ds(4, inner)]),
            taps2=(taps2_own_ref, taps2_ref.at[pl.ds(4, inner)]),
            e1_edge=(e1_edge_in, e1_edge_ref),
            e1_own=(e1_own_in, e1_own_ref),
            noisy=(noisy_in, noisy_ref),
            noise=(noise_in, noise_ref),
        )
        flags = ends(lat)
        fill_conv1(conv1_ref, w1_ref)
        fill_conv2(conv2_ref, w2_ref)
        fill_head(head_ref, wh_ref)
        fetch.wait("wu3")
        mean1, mean2, mean3 = mean_matrix(64), mean_matrix(128), mean_matrix(256)
        bias3, bias2, bias1 = bias_ref[4:5, :], bias_ref[5:6, :], bias_ref[6:7, :]

        for side, ref in ((0, top_ref), (1, bot_ref)):
            at = 0 if side == 0 else 6

            def put3(j, h, u, at=at, side=side):
                if j == 1 - side:
                    h3_ref[3 * side] = h
                put_taps(taps3_ref, at + j, u, 256)

            up3(ref[0:1], ref[1:3], put3, wu3_ref, bias3, mean3, size, flags[side])
            own = 2 if side == 0 else 4
            taps3_ref[own : own + 2] = edge_taps_ref[2 * side : 2 * side + 2]
            h3_ref[1 + side] = edge_h_ref[side]

        rows = [jnp.concatenate([taps3_ref[a : a + 2], taps3_ref[4 + a : 6 + a]], axis=0) for a in range(3)]

        def place2(j):
            return j if j < 4 else rows2 + j - 4

        def put2(j, h, u):
            if j < 2:
                u = u * flags[0]
            if j >= 6:
                u = u * flags[1]
            h2_ref[place2(j)] = h
            put_taps(taps2_ref, place2(j), u, 128)

        fetch.wait("w3", "wu2", "e2a", "e2b")
        up2(h3_ref[...], conv_rows(rows, 768, w3_ref), lambda j: e2_ref[j], put2, wu2_ref, bias2, mean2, size)
        fetch.wait("h2", "taps2", "e1_edge")

        rows = [jnp.concatenate([taps2_ref[a : a + 2], taps2_ref[rows2 + a : rows2 + a + 2]], axis=0) for a in range(3)]
        prior = jnp.concatenate([h2_ref[1:3], h2_ref[rows2 + 1 : rows2 + 3]], axis=0)

        def lay(ro, k, factor=None):
            u = activate(h1_ref[ro, k].astype(F32), bias1, mean1)
            put_taps1(taps1_ref, ro, k, u if factor is None else u * factor)

        def put1(j, ro, h):
            h1_ref[ro, j if j < 2 else rows2 + j - 2] = h

        acc = conv_rows(rows, 512, conv2_ref)
        up1(prior, acc, lambda j, ro: e1_edge_ref[ro, j], put1, wu1_ref, size)

        def first(i, count):
            def put(j, ro, h):
                h1_ref[ro, i + 2 + j] = h

            acc = conv(taps2_ref, i + 2, count, 512, conv2_ref)
            up1(h2_ref[pl.ds(i + 3, count)], acc, lambda j, ro: e1_own_ref[ro, i + j], put, wu1_ref, size)

        def behind(i, count):
            for j in range(count):
                for ro in range(2):
                    lay(ro, i + 2 + j)

        chunk = divisor(rows2 - 2, 10)
        steps = (rows2 - 2) // chunk
        inner_chunk = steps // 2

        def order(c):
            return jnp.where(c == 0, inner_chunk, jnp.where(c <= inner_chunk, c - 1, c))

        fetch.wait("e1_own")
        first(inner_chunk * chunk, chunk)
        for ro in range(2):
            lay(ro, 0, flags[0])
            lay(ro, 1)
            lay(ro, rows2)
            lay(ro, rows2 + 1, flags[1])

        def both(c):
            behind(order(c - 1) * chunk, chunk)
            first(order(c) * chunk, chunk)

        loop(steps - 1, lambda c: both(c + 1))
        behind(order(steps - 1) * chunk, chunk)
        fetch.wait("noisy", "noise")

    pl.when(step == 0)(prepare)

    spread = dotf(g_ref[...], head_ref[...])
    for p in range(4):
        for s in range(4):
            turn_ref[pl.ds(4 * p + s, n, stride=16), :] = spread[p * size : p * size + n, s * 128 : (s + 1) * 128]
    eps = turn_ref[...].T
    nvars, _, cols = noisy_ref.shape
    for o in range(2):
        part = eps[o * 64 : (o + 1) * 64].reshape(nvars, 8, cols)
        rows = pl.ds(pl.multiple_of(jnp.maximum(step - 1, 0) * 16 + o * 8, 8), 8)
        new = factors[0] * noisy_ref[:, rows, :] - factors[1] * part + factors[2] * noise_ref[:, rows, :]
        out_ref[:, o * 8 : (o + 1) * 8, :] = new

    i = jnp.minimum(step, last) * 4
    acc = conv1(taps1_ref, i, 4, conv1_ref)
    flat = 4 * size
    for p in range(4):
        halves = []
        for ro in range(2):
            prior = h1_ref[ro, pl.ds(i + 1, 4), :, p * 128 : (p + 1) * 128].reshape(flat, 128).astype(F32)
            halves.append((prior + acc[p * flat : (p + 1) * flat, ro * 128 : (ro + 1) * 128]).astype(BF))
        both = jnp.concatenate(halves, axis=1)
        for j in range(4):
            g_ref[p * size : (p + 1) * size, j * 256 : (j + 1) * 256] = both[j * size : (j + 1) * size]


def decoder(lat_count, factors, biases, top, bot, edge_h, edge_taps, e2, e1_own, e1_edge, weights, h2, taps2, noisy, step_noise, n, size):
    nvars, lat, cols = noisy.shape
    rows1 = lat // 2
    rows2 = rows1 // 2
    field = pl.BlockSpec((nvars, 16, cols), lambda k: (0, jnp.maximum(k - 1, 0), 0))
    smem = pl.BlockSpec(memory_space=pltpu.SMEM)
    inside = pl.BlockSpec(memory_space=pltpu.VMEM)
    vmem = pltpu.VMEM
    wu3, w3, wu2, w2, wu1, w1, wh = weights
    late = [w3, wu2, e1_edge, e1_own]
    return pl.pallas_call(
        functools.partial(decoder_kernel, n=n, size=size, rows1=rows1, lat=lat_count),
        name="decoder",
        grid=(rows1 // 8 + 1,),
        in_specs=[smem] + [inside] * 9 + [ANYWHERE] * 10,
        out_specs=field,
        out_shape=jax.ShapeDtypeStruct(noisy.shape, F32),
        scratch_shapes=[
            vmem((4, size, 512), BF),
            vmem((8, 8, size, 128), BF),
            vmem((rows2 + 4, size, 512), BF),
            vmem((rows2 + 4, 6, size, 128), BF),
            vmem((2, rows2 + 2, size, 512), BF),
            vmem((2, rows2 + 2, 8, size, 128), BF),
            vmem((cols, 128), F32),
            vmem(wu3.shape, BF),
            vmem((8, size, 512), BF),
        ]
        + [vmem(x.shape, BF) for x in late]
        + [vmem((1536, 256), BF), vmem((1024, 256), BF), vmem((1024, 512), BF), vmem((4 * size, 1024), BF)]
        + [vmem(noisy.shape, F32), vmem(noisy.shape, F32), pltpu.SemaphoreType.DMA((11,))],
    )(
        factors, biases, near(top), near(bot), edge_h, edge_taps, wu1, w2, w1.T, wh.T, wu3,
        h2, taps2, e2, *late, noisy, step_noise,
    )


def shift(array, axis, by, closed):
    count = lax.axis_size(axis)
    if closed:
        pairs = [(i, (i + by) % count) for i in range(count)]
    else:
        pairs = [(i, i + by) for i in range(count) if 0 <= i + by < count]
    return lax.ppermute(array, axis, pairs)


def body(
    noisy, coarse, step_noise, timestep, w_time, w_embed, w_enc1, w_down1, w_enc2, w_down2, w_enc3, w_down3,
    w_qkv, w_attn_out, w_up3, w_dec3, w_up2, w_dec2, w_up1, w_dec1, w_head,
):
    nvars, lat, cols = noisy.shape
    n = cols // 16
    size = -(-(n + 2) // 16) * 16
    rows1 = lat // 2
    rows4 = lat // 16
    groups = lax.axis_size("lon")
    lat_count = lax.axis_size("lat")

    wide, left, right = embed_strips(noisy, coarse, w_embed)
    rhalo = shift(left, "lon", -1, True)
    lhalo = shift(right, "lon", 1, True)
    top, mid, bot = embed(noisy, coarse, wide)

    temb = time_embed(timestep, w_time)
    factors = update_factors(timestep)
    widths = [w_enc1.shape[1], w_enc2.shape[1], w_enc3.shape[1], w_qkv.shape[0], w_dec3.shape[1], w_dec2.shape[1], w_dec1.shape[1]]
    starts = [sum(widths[:i]) for i in range(7)]
    biases = jnp.stack(
        [jnp.tile(temb[s : s + w], 512 // w) * (1.0 if i == 3 else 0.5) for i, (s, w) in enumerate(zip(starts, widths))]
    )

    top, bot = add_rims(lhalo, rhalo, top, bot)
    from_top = shift(bot, "lat", 1, False)
    from_bot = shift(top, "lat", -1, False)
    e1_own, d1, taps2, edge_h, edge_taps, conv1_w, conv2_w = encoder_own(
        biases, mid, top, bot, lhalo, rhalo, w_enc1, w_down1, w_enc2, n, size
    )

    copies = max(1, groups // rows4)
    each = max(1, rows4 // groups)
    e1_edge, e2, e3, sent = encoder(
        lat_count, biases, from_top, from_bot, edge_h, edge_taps,
        (conv1_w, w_down1, conv2_w, w_down2, w_enc3, w_down3), d1, taps2, n, size, rows1, (groups, each, copies),
    )
    got = lax.all_to_all(sent, "lon", split_axis=0, concat_axis=0, tiled=True)
    out, e3 = attention(got, biases, e3, w_qkv, w_attn_out, n, size, each)
    a4 = lax.all_to_all(out.reshape(groups, each * size, 512), "lon", split_axis=0, concat_axis=0, tiled=True)
    a4 = a4.reshape(groups * each, size, 512)
    if copies > 1:
        a4 = a4.reshape(rows4, copies, size, 512)[:, 0]

    top = shift(jnp.concatenate([a4[-1:], e3[-2:]]), "lat", 1, False)
    bot = shift(jnp.concatenate([a4[:1], e3[:2]]), "lat", -1, False)
    h2, taps2, edge_h, edge_taps = decoder_own(biases, a4, e3, e2, w_up3, w_dec3, w_up2, size)
    return decoder(
        lat_count, factors, biases, top, bot, edge_h, edge_taps, e2, e1_own, e1_edge,
        (w_up3, w_dec3, w_up2, w_dec2, w_up1, w_dec1, w_head), h2, taps2, noisy, step_noise, n, size,
    )


def solution(mesh):
    field = P(None, "lat", "lon")
    return jax.shard_map(
        body, mesh=mesh, in_specs=(field, field, field) + (P(),) * 18, out_specs=field, check_vma=False
    )
```
